256 devices in a mesh: uly: 16 (over z, y_hi), blk: 16 (over x, y_lo, core).
Axes of the slice: x: 4, y: 4 (y_hi: 2, y_lo: 2; y = y_hi * 2 + y_lo), z: 8, core: 2. Of those that a mesh axis runs over, the one named last changes fastest.
Arguments:
- queries: bfloat16 [32768, 1024], P(('blk', 'uly')), may hold values from -6 to 6
- keys: bfloat16 [32768, 1024], P(('blk', 'uly')), may hold values from -6 to 6
- values: bfloat16 [32768, 1024], P(('blk', 'uly')), may hold values from -6 to 6
- lengths: int32 [64], replicated, may hold values from 1 to 1024, 32768 in all
- conv_weight: float32 [31, 1024], P(None, 'uly'), may hold values from -8 to 8
- norm_gain: float32 [1024], P('uly'), may hold values from 0.1 to 1.9
- cotangent: bfloat16 [1024, 32768], P('uly', 'blk'), may hold values from -6 to 6
Outputs:
- conv_out: bfloat16 [1024, 32768], P('uly', 'blk')
- grad_queries: bfloat16 [1024, 32768], P('uly', 'blk')
- grad_keys: bfloat16 [1024, 32768], P('uly', 'blk')
- grad_values: bfloat16 [1024, 32768], P('uly', 'blk')
The draws below stay inside these ranges and needn't reach their ends.
Inputs may be any that keep to these rules, and one draw needn't show every extreme that they name: `lengths`: utterances follow one another and cover the 32768 frames; one utterance has exactly 1024 frames.
All inputs are finite; a program needn't handle non-finite values.
Results may differ from the reference program's by a relative error of at most 0.03.
Values may be sent and summed in bfloat16 or wider, within the bound.
A program may use at most 64 MiB of HBM per device.

```python
import math
import jax
import jax.numpy as jnp
import numpy as np
from jax import lax

D = 1024
HEADS = 16
KERNEL = 31
HEAD_DIM = 64
MAXLEN = 1024
FRAMES = 32768
UTTS = 64
QB = 512
HALF = 15


def drawn_pair(key):
    shape_full = (FRAMES, D)
    query_noise = jax.random.normal(jax.random.fold_in(key, 11), shape_full, jnp.float32)
    key_noise = jax.random.normal(jax.random.fold_in(key, 12), shape_full, jnp.float32)
    return (jnp.clip(query_noise, -6.0, 6.0), jnp.clip(key_noise, -6.0, 6.0))


def draw_queries(key, part):
    return drawn_pair(key)[0].astype(jnp.bfloat16)


def draw_keys(key, part):
    return drawn_pair(key)[1].astype(jnp.bfloat16)


def draw_conv_weight(key, part):
    base_taps = jax.random.normal(jax.random.fold_in(key, 21), (KERNEL, D), jnp.float32)
    channel_level = jnp.exp(jax.random.uniform(jax.random.fold_in(key, 22), (1, D), jnp.float32, 0.0, 2.3026))
    return jnp.clip(base_taps, -4.0, 4.0) * channel_level * KERNEL ** (-0.5)


def level_of(own_key, dims, shards, smallest, largest):
    def one(axis_at, shards_of):
        heights = jax.random.uniform(jax.random.fold_in(jax.random.fold_in(own_key, 6), axis_at), (shards_of,), jnp.float32, smallest / len(shards), largest / len(shards))
        return jnp.repeat(jnp.exp(heights), dims[axis_at] // shards_of).reshape((-1,) + (1,) * (len(dims) - axis_at - 1))

    gain = one(*shards[0])
    for cut in shards[1:]:
        gain = gain * one(*cut)
    return gain


def length_profile(amount, total, limit, slope):
    loads = [(1 << 20) // math.isqrt(standing ** slope) + 1 for standing in range(2, amount + 1)]
    spare, given = total - limit - (amount - 1), [1] * (amount - 1)
    while spare > 0:
        free = [i for i in range(amount - 1) if given[i] < limit]
        whole, left = sum([loads[i] for i in free]), spare
        for i in free:
            extra = min(limit - given[i], max(1, left * loads[i] // whole), spare)
            given[i] = given[i] + extra
            spare = spare - extra
    return np.array([limit] + given)


def uneven(rng, number_of, total, bound, lean):
    if number_of == 2:
        one = jax.random.randint(rng, (), max(1, total - bound), min(bound, total - 1) + 1)
        return jnp.stack([one, total - one])
    sizes = jnp.asarray(length_profile(number_of, total, bound, lean), jnp.int32)
    twos = (number_of - 1) // 2
    giver, taker = sizes[1:1 + 2 * twos:2], sizes[2:2 + 2 * twos:2]
    room = jnp.minimum(giver - 1, bound - taker)
    shifted = jax.random.randint(jax.random.fold_in(rng, 1), (twos,), 0, 1 << 20) % (room + 1)
    sizes = sizes.at[1:1 + 2 * twos:2].set(giver - shifted).at[2:2 + 2 * twos:2].set(taker + shifted)
    return sizes[jax.random.permutation(jax.random.fold_in(rng, 2), number_of)]


def noise(stream_key, shape, scale, limit, pieces=(), kind=jnp.bfloat16):
    loudness = level_of(stream_key, shape, pieces, -0.22, 0.18) if pieces else 1.0
    drawn = jax.random.normal(stream_key, shape, jnp.float32) * scale * loudness
    return jnp.minimum(jnp.maximum(drawn, -limit), limit).astype(kind)


def setup_inputs(seed: int = 0) -> dict:
    key_of = jax.random.split(jax.random.key(seed), 8)
    return {
        "queries": draw_queries(jax.random.fold_in(key_of[7], 71), 0),
        "keys": draw_keys(jax.random.fold_in(key_of[7], 71), 0),
        "values": noise(key_of[2], (FRAMES, D), 1.0, 6.0, ((0, 256),)),
        "lengths": uneven(key_of[3], UTTS, FRAMES, MAXLEN, 2).astype(jnp.int32),
        "conv_weight": draw_conv_weight(jax.random.fold_in(key_of[7], 71), 0),
        "norm_gain": jnp.clip(1.0 + 0.18 * jax.random.normal(key_of[5], (D,), jnp.float32), 0.1, 1.9),
        "cotangent": noise(key_of[6], (D, FRAMES), 1.0, 6.0, ((0, 16), (1, 16))),
    }


def segment_ids(lengths, frames, frame_total):
    starts = (jnp.cumsum(lengths) - lengths).astype(jnp.int32)
    seg_ids = lax.optimization_barrier(jnp.sum((starts[None, :] <= frames[:, None]).astype(jnp.int32), axis=1)) - 1
    inside = (frames >= 0) & (frames < frame_total)
    return jnp.where(inside, seg_ids, -1).astype(jnp.int32)

def rounded(values_in):
    return lax.optimization_barrier(values_in.astype(jnp.bfloat16)).astype(jnp.float32)

def tile_probs(query_rows, key_rows, query_seg, key_seg):
    scores = HEAD_DIM ** (-0.5) * jnp.einsum('rhe,she->hrs', query_rows.astype(jnp.float32), key_rows.astype(jnp.float32))
    same_seg = (query_seg[:, None] == key_seg[None, :])[None]
    row_top = lax.optimization_barrier(jnp.max(jnp.where(same_seg, scores, -1e+30), axis=2, keepdims=True))
    shifted_exp = jnp.where(same_seg, jnp.exp(scores - row_top), 0.0)
    row_total = lax.optimization_barrier(jnp.sum(shifted_exp, axis=2, keepdims=True))
    return shifted_exp / row_total

def reference(queries, keys, values, lengths, conv_weight, norm_gain, cotangent):
    score_scale = HEAD_DIM ** (-0.5)
    window = QB + 2 * MAXLEN
    shape_heads = (FRAMES, HEADS, HEAD_DIM)
    q_heads = queries.reshape(shape_heads)
    pad_rows = ((MAXLEN, MAXLEN), (0, 0), (0, 0))
    k_pad = jnp.pad(keys.reshape(shape_heads), pad_rows)
    v_pad = jnp.pad(values.reshape(shape_heads), pad_rows)
    seg_own = segment_ids(lengths, jnp.arange(FRAMES, dtype=jnp.int32), FRAMES)
    seg_pad = segment_ids(lengths, jnp.arange(FRAMES + 2 * MAXLEN, dtype=jnp.int32) - MAXLEN, FRAMES)
    seg_conv = segment_ids(lengths, jnp.arange(FRAMES + 2 * HALF, dtype=jnp.int32) - HALF, FRAMES)
    starts = jnp.arange(FRAMES // QB, dtype=jnp.int32) * QB

    def window_rows(row_start):
        return (lax.dynamic_slice_in_dim(q_heads, row_start, QB, 0), lax.dynamic_slice_in_dim(k_pad, row_start, window, 0), lax.dynamic_slice_in_dim(v_pad, row_start, window, 0), lax.dynamic_slice_in_dim(seg_own, row_start, QB, 0), lax.dynamic_slice_in_dim(seg_pad, row_start, window, 0))

    def forward_block(row_start):
        query_rows, key_rows, value_rows, query_seg, key_seg = window_rows(row_start)
        probs = tile_probs(query_rows, key_rows, query_seg, key_seg)
        attended = jnp.einsum('hrs,she->rhe', rounded(probs), value_rows.astype(jnp.float32))
        return attended.astype(jnp.bfloat16)
    attended = lax.map(forward_block, starts).reshape(FRAMES, D)
    attended_pad = jnp.pad(attended.astype(jnp.float32), ((HALF, HALF), (0, 0)))
    conv_sum = jnp.zeros((FRAMES, D), jnp.float32)
    for tap_index in range(KERNEL):
        same_seg = (seg_conv[tap_index:tap_index + FRAMES] == seg_own)[:, None]
        conv_sum = conv_sum + conv_weight[tap_index][None, :] * jnp.where(same_seg, attended_pad[tap_index:tap_index + FRAMES], 0.0)
    grouped = conv_sum.reshape(shape_heads)
    spread = jnp.sqrt(lax.optimization_barrier(jnp.mean(grouped * grouped, axis=2, keepdims=True)) + 1e-05)
    normed = grouped / spread
    pre_act = normed.reshape(FRAMES, D) * norm_gain[None, :]
    sigmoid_gate = jax.nn.sigmoid(pre_act)
    conv_out = (pre_act * sigmoid_gate).astype(jnp.bfloat16)
    grad_pre = cotangent.astype(jnp.float32).T * sigmoid_gate * (1.0 + pre_act * (1.0 - sigmoid_gate))
    weighted = (grad_pre * norm_gain[None, :]).reshape(shape_heads)
    grad_conv = ((weighted - normed * lax.optimization_barrier(jnp.mean(weighted * normed, axis=2, keepdims=True))) / spread).reshape(FRAMES, D)
    grad_pad = jnp.pad(grad_conv, ((HALF, HALF), (0, 0)))
    grad_sum = jnp.zeros((FRAMES, D), jnp.float32)
    for tap_index in range(KERNEL):
        offset = 2 * HALF - tap_index
        same_seg = (seg_conv[offset:offset + FRAMES] == seg_own)[:, None]
        grad_sum = grad_sum + conv_weight[tap_index][None, :] * jnp.where(same_seg, grad_pad[offset:offset + FRAMES], 0.0)
    grad_attended = grad_sum.astype(jnp.bfloat16)
    row_delta = lax.optimization_barrier(jnp.sum((grad_attended.astype(jnp.float32) * attended.astype(jnp.float32)).reshape(shape_heads), axis=2))
    grad_heads = grad_attended.reshape(shape_heads)

    def backward_block(running, row_start):
        grad_k, grad_v = running
        query_rows, key_rows, value_rows, query_seg, key_seg = window_rows(row_start)
        grad_rows = lax.dynamic_slice_in_dim(grad_heads, row_start, QB, 0).astype(jnp.float32)
        delta_rows = lax.dynamic_slice_in_dim(row_delta, row_start, QB, 0)
        probs = tile_probs(query_rows, key_rows, query_seg, key_seg)
        grad_p = jnp.einsum('rhe,she->hrs', grad_rows, value_rows.astype(jnp.float32))
        grad_s = rounded(probs * (grad_p - delta_rows.T[:, :, None]))
        grad_q = score_scale * jnp.einsum('hrs,she->rhe', grad_s, key_rows.astype(jnp.float32))
        key_term = score_scale * jnp.einsum('hrs,rhe->she', grad_s, query_rows.astype(jnp.float32))
        value_term = jnp.einsum('hrs,rhe->she', rounded(probs), grad_rows)
        grad_k = lax.dynamic_update_slice_in_dim(grad_k, lax.dynamic_slice_in_dim(grad_k, row_start, window, 0) + key_term, row_start, 0)
        grad_v = lax.dynamic_update_slice_in_dim(grad_v, lax.dynamic_slice_in_dim(grad_v, row_start, window, 0) + value_term, row_start, 0)
        return ((grad_k, grad_v), grad_q.astype(jnp.bfloat16))
    zero_pad = jnp.zeros((FRAMES + 2 * MAXLEN, HEADS, HEAD_DIM), jnp.float32)
    (grad_k, grad_v), grad_q = lax.scan(backward_block, (zero_pad, zero_pad), starts)
    grad_queries = grad_q.reshape(FRAMES, D)
    grad_keys = grad_k[MAXLEN:MAXLEN + FRAMES].reshape(FRAMES, D).astype(jnp.bfloat16)
    grad_values = grad_v[MAXLEN:MAXLEN + FRAMES].reshape(FRAMES, D).astype(jnp.bfloat16)
    return (conv_out.T, grad_queries.T, grad_keys.T, grad_values.T)
```

```python
import jax
import jax.numpy as jnp
from jax import lax
from jax.sharding import PartitionSpec as P

KERNEL = 31
HEAD_DIM = 64


def extended(block, sides, width):
    for axis, dim in sides:
        count = lax.axis_size(axis)
        forward = [(i, i + 1) for i in range(count - 1)]
        backward = [(target, source) for source, target in forward]
        low = lax.ppermute(
            lax.slice_in_dim(block, block.shape[dim] - width, None, axis=dim), axis, forward
        )
        high = lax.ppermute(lax.slice_in_dim(block, 0, width, axis=dim), axis, backward)
        block = jnp.concatenate([low, block, high], axis=dim)
    return block


def passed_along(block, axis, distance):
    devices = range(lax.axis_size(axis))
    route = [(i - distance, i) for i in devices if i - distance in devices]
    return lax.ppermute(block, axis, route)


def segment_ids(lengths, frames, frame_total):
    starts = jnp.cumsum(lengths) - lengths
    seg_ids = jnp.sum((starts[None, :] <= frames[:, None]).astype(jnp.int32), axis=1) - 1
    inside = (frames >= 0) & (frames < frame_total)
    return jnp.where(inside, seg_ids, -1)


def rows_at(values_in, row_start, row_count):
    return lax.dynamic_slice_in_dim(values_in, row_start, row_count, 0)


def masked_scores(query_rows, key_rows, query_seg, key_seg):
    scores = HEAD_DIM ** (-0.5) * jnp.einsum(
        "rhe,she->hrs", query_rows, key_rows, preferred_element_type=jnp.float32
    )
    same_seg = (query_seg[:, None] == key_seg[None, :])[None]
    return (scores, same_seg)


def weights_of(scores, same_seg, row_top, row_total):
    return jnp.where(same_seg, jnp.exp(scores - row_top), 0.0) / row_total


def on_device(queries, keys, values, lengths, conv_weight, norm_gain, cotangent):
    rows_in, width = queries.shape
    heads_total = width // HEAD_DIM
    stacked = jnp.stack(
        [a.reshape(rows_in, heads_total, HEAD_DIM) for a in (queries, keys, values)], axis=2
    ).reshape(rows_in, heads_total * 3 * HEAD_DIM)
    local_qkv = lax.all_to_all(stacked, "uly", split_axis=1, concat_axis=0, tiled=True)
    local_qkv = local_qkv.reshape(local_qkv.shape[0], -1, 3, HEAD_DIM)
    local_q, local_k, local_v = (
        local_qkv[:, :, i].reshape(local_qkv.shape[0], -1) for i in range(3)
    )
    block_rows, channels = local_q.shape
    heads_here = channels // HEAD_DIM
    maxlen = block_rows // 2
    rows_q = min(512, block_rows)
    window = rows_q + 2 * maxlen
    conv_half = KERNEL // 2
    block_count = block_rows // rows_q
    score_scale = HEAD_DIM ** (-0.5)
    frame_total = lax.axis_size("blk") * block_rows
    first_frame = lax.axis_index("blk") * block_rows
    seg_ext = segment_ids(
        lengths,
        first_frame - maxlen + jnp.arange(block_rows + 2 * maxlen, dtype=jnp.int32),
        frame_total,
    )
    seg_own = seg_ext[maxlen : maxlen + block_rows]
    seg_conv = seg_ext[maxlen - conv_half : maxlen + block_rows + conv_half]
    near_pairs = extended(jnp.concatenate([local_k, local_v], axis=1), (("blk", 0),), maxlen)
    k_ext = near_pairs[:, :channels].reshape(-1, heads_here, HEAD_DIM)
    v_ext = near_pairs[:, channels:].reshape(-1, heads_here, HEAD_DIM)
    q_heads = local_q.reshape(block_rows, heads_here, HEAD_DIM)
    starts = jnp.arange(block_count, dtype=jnp.int32) * rows_q

    def forward_block(row_start):
        scores, same_seg = masked_scores(
            rows_at(q_heads, row_start, rows_q),
            rows_at(k_ext, row_start, window),
            rows_at(seg_own, row_start, rows_q),
            rows_at(seg_ext, row_start, window),
        )
        row_top = jnp.max(jnp.where(same_seg, scores, -1e30), axis=2, keepdims=True)
        shifted_exp = jnp.where(same_seg, jnp.exp(scores - row_top), 0.0)
        row_total = jnp.sum(shifted_exp, axis=2, keepdims=True)
        weights_bf = (shifted_exp / row_total).astype(jnp.bfloat16)
        attended = jnp.einsum(
            "hrs,she->rhe",
            weights_bf,
            rows_at(v_ext, row_start, window),
            preferred_element_type=jnp.float32,
        )
        return (attended.astype(jnp.bfloat16), row_top[:, :, 0].T, row_total[:, :, 0].T)

    attended, row_tops, row_totals = lax.map(forward_block, starts)
    attended = attended.reshape(block_rows, channels)
    row_tops = row_tops.reshape(block_rows, heads_here)
    row_totals = row_totals.reshape(block_rows, heads_here)
    attended_ext = extended(attended, (("blk", 0),), conv_half)
    conv_sum = jnp.zeros((block_rows, channels), jnp.float32)
    for tap_index in range(KERNEL):
        same_seg = (seg_conv[tap_index : tap_index + block_rows] == seg_own)[:, None]
        conv_sum = conv_sum + conv_weight[tap_index][None, :] * jnp.where(
            same_seg, attended_ext[tap_index : tap_index + block_rows].astype(jnp.float32), 0.0
        )
    grouped = conv_sum.reshape(block_rows, heads_here, HEAD_DIM)
    spread = jnp.sqrt(jnp.mean(grouped * grouped, axis=2, keepdims=True) + 1e-05)
    normed = grouped / spread
    pre_act = normed.reshape(block_rows, channels) * norm_gain[None, :]
    sigmoid_gate = jax.nn.sigmoid(pre_act)
    conv_out = (pre_act * sigmoid_gate).astype(jnp.bfloat16)
    grad_pre = (
        cotangent.astype(jnp.float32).T * sigmoid_gate * (1.0 + pre_act * (1.0 - sigmoid_gate))
    )
    weighted = (grad_pre * norm_gain[None, :]).reshape(block_rows, heads_here, HEAD_DIM)
    grad_conv = (
        (weighted - normed * jnp.mean(weighted * normed, axis=2, keepdims=True)) / spread
    ).reshape(block_rows, channels)
    grad_ext = extended(grad_conv, (("blk", 0),), conv_half)
    grad_sum = jnp.zeros((block_rows, channels), jnp.float32)
    for tap_index in range(KERNEL):
        offset = 2 * conv_half - tap_index
        same_seg = (seg_conv[offset : offset + block_rows] == seg_own)[:, None]
        grad_sum = grad_sum + conv_weight[tap_index][None, :] * jnp.where(
            same_seg, grad_ext[offset : offset + block_rows], 0.0
        )
    grad_attended = grad_sum.astype(jnp.bfloat16)
    row_delta = jnp.sum(
        (grad_attended.astype(jnp.float32) * attended.astype(jnp.float32)).reshape(
            block_rows, heads_here, HEAD_DIM
        ),
        axis=2,
    )
    grad_heads = grad_attended.reshape(block_rows, heads_here, HEAD_DIM)

    def tile_grads(row_start):
        query_rows = rows_at(q_heads, row_start, rows_q)
        key_rows = rows_at(k_ext, row_start, window)
        value_rows = rows_at(v_ext, row_start, window)
        grad_rows = rows_at(grad_heads, row_start, rows_q)
        scores, same_seg = masked_scores(
            query_rows,
            key_rows,
            rows_at(seg_own, row_start, rows_q),
            rows_at(seg_ext, row_start, window),
        )
        probs = weights_of(
            scores,
            same_seg,
            rows_at(row_tops, row_start, rows_q).T[:, :, None],
            rows_at(row_totals, row_start, rows_q).T[:, :, None],
        )
        grad_p = jnp.einsum(
            "rhe,she->hrs", grad_rows, value_rows, preferred_element_type=jnp.float32
        )
        grad_s = (probs * (grad_p - rows_at(row_delta, row_start, rows_q).T[:, :, None])).astype(
            jnp.bfloat16
        )
        grad_q = (
            score_scale
            * jnp.einsum("hrs,she->rhe", grad_s, key_rows, preferred_element_type=jnp.float32)
        ).astype(jnp.bfloat16)
        return (probs, grad_s, grad_q, query_rows, grad_rows)

    def backward_block(running, row_start):
        probs, grad_s, grad_q, query_rows, grad_rows = tile_grads(row_start)
        key_term = score_scale * jnp.einsum(
            "hrs,rhe->she", grad_s, query_rows, preferred_element_type=jnp.float32
        )
        value_term = jnp.einsum(
            "hrs,rhe->she",
            probs.astype(jnp.bfloat16),
            grad_rows,
            preferred_element_type=jnp.float32,
        )
        key_value = jnp.concatenate(
            [key_term.reshape(window, channels), value_term.reshape(window, channels)], axis=1
        )
        running = lax.dynamic_update_slice_in_dim(
            running, rows_at(running, row_start, window) + key_value, row_start, 0
        )
        return (running, grad_q)

    ext_terms, grad_q = lax.scan(
        backward_block, jnp.zeros((block_rows + 2 * maxlen, 2 * channels), jnp.float32), starts
    )
    received = []
    for rim_part, direction in ((ext_terms[:maxlen], -1), (ext_terms[maxlen + block_rows :], 1)):
        received.append(
            passed_along(rim_part.astype(jnp.bfloat16), "blk", direction).astype(rim_part.dtype)
        )
    key_grads = ext_terms[maxlen : maxlen + block_rows] + jnp.concatenate(
        [received[1], received[0]], axis=0
    )
    grad_queries = grad_q.reshape(block_rows, channels)
    grad_keys = key_grads[:, :channels].astype(jnp.bfloat16)
    grad_values = key_grads[:, channels:].astype(jnp.bfloat16)
    return (conv_out.T, grad_queries.T, grad_keys.T, grad_values.T)


def solution(mesh):
    in_specs = (
        P(("blk", "uly"), None),
        P(("blk", "uly"), None),
        P(("blk", "uly"), None),
        P(),
        P(None, "uly"),
        P("uly"),
        P("uly", "blk"),
    )
    out_specs = (P("uly", "blk"), P("uly", "blk"), P("uly", "blk"), P("uly", "blk"))
    return jax.shard_map(
        on_device, mesh=mesh, in_specs=in_specs, out_specs=out_specs, check_vma=False
    )
```

```python
import jax
import jax.numpy as jnp
import functools
from jax import lax
from jax.experimental import pallas as pl
from jax.experimental.pallas import tpu as pltpu
from jax.sharding import PartitionSpec as P

KERNEL = 31
HEAD_DIM = 64


def extended(block, sides, width):
    for axis, dim in sides:
        count = lax.axis_size(axis)
        forward = [(i, i + 1) for i in range(count - 1)]
        backward = [(target, source) for source, target in forward]
        low = lax.ppermute(
            lax.slice_in_dim(block, block.shape[dim] - width, None, axis=dim), axis, forward
        )
        high = lax.ppermute(lax.slice_in_dim(block, 0, width, axis=dim), axis, backward)
        block = jnp.concatenate([low, block, high], axis=dim)
    return block


def passed_along(block, axis, distance):
    devices = range(lax.axis_size(axis))
    route = [(i - distance, i) for i in devices if i - distance in devices]
    return lax.ppermute(block, axis, route)


def segment_ids(lengths, frames, frame_total):
    starts = jnp.cumsum(lengths) - lengths
    seg_ids = jnp.sum((starts[None, :] <= frames[:, None]).astype(jnp.int32), axis=1) - 1
    inside = (frames >= 0) & (frames < frame_total)
    return jnp.where(inside, seg_ids, -1)


def rows_at(values_in, row_start, row_count):
    return lax.dynamic_slice_in_dim(values_in, row_start, row_count, 0)


def masked_scores(query_rows, key_rows, query_seg, key_seg):
    scores = HEAD_DIM ** (-0.5) * jnp.einsum(
        "rhe,she->hrs", query_rows, key_rows, preferred_element_type=jnp.float32
    )
    same_seg = (query_seg[:, None] == key_seg[None, :])[None]
    return (scores, same_seg)


def weights_of(scores, same_seg, row_top, row_total):
    return jnp.where(same_seg, jnp.exp(scores - row_top), 0.0) / row_total


TILE_Q = 256
TILE_K = 256
NT = (((1,), (1,)), ((), ()))
TN = (((0,), (0,)), ((), ()))


def forward_kernel(lo_ref, hi_ref, q_ref, k_ref, v_ref, qseg_ref, kseg_ref, o_ref, m_ref, l_ref):
    scale = HEAD_DIM ** (-0.5)

    def q_body(i, carry):
        r0 = pl.multiple_of(i * TILE_Q, TILE_Q)
        q = q_ref[pl.ds(r0, TILE_Q), :]
        qs = qseg_ref[pl.ds(r0, TILE_Q), :]

        def k_body(j, c):
            m, l, acc = c
            c0 = pl.multiple_of(j * TILE_K, TILE_K)
            k = k_ref[pl.ds(c0, TILE_K), :]
            v = v_ref[pl.ds(c0, TILE_K), :]
            ks = kseg_ref[:, pl.ds(c0, TILE_K)]
            s = scale * lax.dot_general(q, k, NT, preferred_element_type=jnp.float32)
            mask = qs == ks
            m_new = jnp.maximum(m, jnp.max(jnp.where(mask, s, -1e30), axis=1, keepdims=True))
            alpha = jnp.exp(m - m_new)
            p = jnp.where(mask, jnp.exp(s - m_new), 0.0)
            l = alpha * l + jnp.sum(p, axis=1, keepdims=True)
            acc = alpha * acc + jnp.dot(
                p.astype(jnp.bfloat16), v, preferred_element_type=jnp.float32
            )
            return (m_new, l, acc)

        init = (
            jnp.full((TILE_Q, 1), -1e30, jnp.float32),
            jnp.zeros((TILE_Q, 1), jnp.float32),
            jnp.zeros((TILE_Q, HEAD_DIM), jnp.float32),
        )
        m, l, acc = lax.fori_loop(lo_ref[i], hi_ref[i], k_body, init)
        o_ref[pl.ds(r0, TILE_Q), :] = (acc / l).astype(o_ref.dtype)
        m_ref[pl.ds(r0, TILE_Q), :] = m
        l_ref[pl.ds(r0, TILE_Q), :] = l
        return carry

    lax.fori_loop(0, q_ref.shape[0] // TILE_Q, q_body, 0)


def backward_kernel(
    lo_ref, hi_ref, q_ref, k_ref, v_ref, do_ref, qseg_ref, kseg_ref, m_ref, il_ref, d_ref,
    dq_ref, dk_ref, dv_ref,
):
    scale = HEAD_DIM ** (-0.5)
    dk_ref[...] = jnp.zeros_like(dk_ref)
    dv_ref[...] = jnp.zeros_like(dv_ref)

    def q_body(i, carry):
        r0 = pl.multiple_of(i * TILE_Q, TILE_Q)
        q = q_ref[pl.ds(r0, TILE_Q), :]
        do = do_ref[pl.ds(r0, TILE_Q), :]
        qs = qseg_ref[pl.ds(r0, TILE_Q), :]
        m = m_ref[pl.ds(r0, TILE_Q), :]
        il = il_ref[pl.ds(r0, TILE_Q), :]
        dlt = d_ref[pl.ds(r0, TILE_Q), :]

        def k_body(j, dq):
            c0 = pl.multiple_of(j * TILE_K, TILE_K)
            k = k_ref[pl.ds(c0, TILE_K), :]
            v = v_ref[pl.ds(c0, TILE_K), :]
            ks = kseg_ref[:, pl.ds(c0, TILE_K)]
            s = scale * lax.dot_general(q, k, NT, preferred_element_type=jnp.float32)
            mask = qs == ks
            p = jnp.where(mask, jnp.exp(s - m) * il, 0.0)
            dp = lax.dot_general(do, v, NT, preferred_element_type=jnp.float32)
            ds = (p * (dp - dlt)).astype(jnp.bfloat16)
            dk_ref[pl.ds(c0, TILE_K), :] += lax.dot_general(
                ds, q, TN, preferred_element_type=jnp.float32
            )
            dv_ref[pl.ds(c0, TILE_K), :] += lax.dot_general(
                p.astype(jnp.bfloat16), do, TN, preferred_element_type=jnp.float32
            )
            return dq + jnp.dot(ds, k, preferred_element_type=jnp.float32)

        dq = lax.fori_loop(
            lo_ref[i], hi_ref[i], k_body, jnp.zeros((TILE_Q, HEAD_DIM), jnp.float32)
        )
        dq_ref[pl.ds(r0, TILE_Q), :] = (scale * dq).astype(dq_ref.dtype)
        return carry

    lax.fori_loop(0, q_ref.shape[0] // TILE_Q, q_body, 0)
    dk_ref[...] = scale * dk_ref[...]


def vmem_call(kernel, n_smem, n_vmem, out_shape):
    return pl.pallas_call(
        kernel,
        out_shape=out_shape,
        in_specs=[pl.BlockSpec(memory_space=pltpu.SMEM)] * n_smem
        + [pl.BlockSpec(memory_space=pltpu.VMEM)] * n_vmem,
        out_specs=[pl.BlockSpec(memory_space=pltpu.VMEM)] * len(out_shape),
    )


def tile_ranges(lengths, seg_own, base, ext_rows):
    ends = jnp.cumsum(lengths)
    starts = ends - lengths
    first = seg_own[::TILE_Q]
    last = seg_own[TILE_Q - 1 :: TILE_Q]
    lo = (starts[first] - base) // TILE_K
    hi = (ends[last] - base + TILE_K - 1) // TILE_K
    lo = jnp.clip(lo, 0, ext_rows // TILE_K).astype(jnp.int32)
    hi = jnp.clip(hi, lo, ext_rows // TILE_K).astype(jnp.int32)
    return (lo, hi)


def on_device(queries, keys, values, lengths, conv_weight, norm_gain, cotangent):
    rows_in, width = queries.shape
    heads_total = width // HEAD_DIM
    stacked = jnp.stack(
        [a.reshape(rows_in, heads_total, HEAD_DIM) for a in (queries, keys, values)], axis=2
    ).reshape(rows_in, heads_total * 3 * HEAD_DIM)
    local_qkv = lax.all_to_all(stacked, "uly", split_axis=1, concat_axis=0, tiled=True)
    local_qkv = local_qkv.reshape(local_qkv.shape[0], -1, 3, HEAD_DIM)
    local_q, local_k, local_v = (
        local_qkv[:, :, i].reshape(local_qkv.shape[0], -1) for i in range(3)
    )
    block_rows, channels = local_q.shape
    heads_here = channels // HEAD_DIM
    maxlen = block_rows // 2
    rows_q = min(512, block_rows)
    window = rows_q + 2 * maxlen
    conv_half = KERNEL // 2
    block_count = block_rows // rows_q
    score_scale = HEAD_DIM ** (-0.5)
    frame_total = lax.axis_size("blk") * block_rows
    first_frame = lax.axis_index("blk") * block_rows
    seg_ext = segment_ids(
        lengths,
        first_frame - maxlen + jnp.arange(block_rows + 2 * maxlen, dtype=jnp.int32),
        frame_total,
    )
    seg_own = seg_ext[maxlen : maxlen + block_rows]
    seg_conv = seg_ext[maxlen - conv_half : maxlen + block_rows + conv_half]
    near_pairs = extended(jnp.concatenate([local_k, local_v], axis=1), (("blk", 0),), maxlen)
    k_ext = near_pairs[:, :channels].reshape(-1, heads_here, HEAD_DIM)
    v_ext = near_pairs[:, channels:].reshape(-1, heads_here, HEAD_DIM)
    q_heads = local_q.reshape(block_rows, heads_here, HEAD_DIM)
    starts = jnp.arange(block_count, dtype=jnp.int32) * rows_q

    assert heads_here == 1
    lo_t, hi_t = tile_ranges(lengths, seg_own, first_frame - maxlen, block_rows + 2 * maxlen)
    qseg_col = seg_own[:, None].astype(jnp.int32)
    kseg_row = seg_ext[None, :].astype(jnp.int32)
    k_flat = k_ext.reshape(-1, HEAD_DIM)
    v_flat = v_ext.reshape(-1, HEAD_DIM)
    attended, row_tops, row_totals = vmem_call(
        forward_kernel,
        2,
        5,
        (
            jax.ShapeDtypeStruct((block_rows, HEAD_DIM), jnp.bfloat16),
            jax.ShapeDtypeStruct((block_rows, 1), jnp.float32),
            jax.ShapeDtypeStruct((block_rows, 1), jnp.float32),
        ),
    )(lo_t, hi_t, local_q, k_flat, v_flat, qseg_col, kseg_row)
    attended_ext = extended(attended, (("blk", 0),), conv_half)
    conv_sum = jnp.zeros((block_rows, channels), jnp.float32)
    for tap_index in range(KERNEL):
        same_seg = (seg_conv[tap_index : tap_index + block_rows] == seg_own)[:, None]
        conv_sum = conv_sum + conv_weight[tap_index][None, :] * jnp.where(
            same_seg, attended_ext[tap_index : tap_index + block_rows].astype(jnp.float32), 0.0
        )
    grouped = conv_sum.reshape(block_rows, heads_here, HEAD_DIM)
    spread = jnp.sqrt(jnp.mean(grouped * grouped, axis=2, keepdims=True) + 1e-05)
    normed = grouped / spread
    pre_act = normed.reshape(block_rows, channels) * norm_gain[None, :]
    sigmoid_gate = jax.nn.sigmoid(pre_act)
    conv_out = (pre_act * sigmoid_gate).astype(jnp.bfloat16)
    grad_pre = (
        cotangent.astype(jnp.float32).T * sigmoid_gate * (1.0 + pre_act * (1.0 - sigmoid_gate))
    )
    weighted = (grad_pre * norm_gain[None, :]).reshape(block_rows, heads_here, HEAD_DIM)
    grad_conv = (
        (weighted - normed * jnp.mean(weighted * normed, axis=2, keepdims=True)) / spread
    ).reshape(block_rows, channels)
    grad_ext = extended(grad_conv, (("blk", 0),), conv_half)
    grad_sum = jnp.zeros((block_rows, channels), jnp.float32)
    for tap_index in range(KERNEL):
        offset = 2 * conv_half - tap_index
        same_seg = (seg_conv[offset : offset + block_rows] == seg_own)[:, None]
        grad_sum = grad_sum + conv_weight[tap_index][None, :] * jnp.where(
            same_seg, grad_ext[offset : offset + block_rows], 0.0
        )
    grad_attended = grad_sum.astype(jnp.bfloat16)
    row_delta = jnp.sum(
        (grad_attended.astype(jnp.float32) * attended.astype(jnp.float32)).reshape(
            block_rows, heads_here, HEAD_DIM
        ),
        axis=2,
    )
    grad_heads = grad_attended.reshape(block_rows, heads_here, HEAD_DIM)

    grad_q, dk_ext, dv_ext = vmem_call(
        backward_kernel,
        2,
        9,
        (
            jax.ShapeDtypeStruct((block_rows, HEAD_DIM), jnp.bfloat16),
            jax.ShapeDtypeStruct((block_rows + 2 * maxlen, HEAD_DIM), jnp.float32),
            jax.ShapeDtypeStruct((block_rows + 2 * maxlen, HEAD_DIM), jnp.float32),
        ),
    )(
        lo_t,
        hi_t,
        local_q,
        k_flat,
        v_flat,
        grad_attended,
        qseg_col,
        kseg_row,
        row_tops,
        1.0 / row_totals,
        row_delta,
    )
    ext_terms = jnp.concatenate([dk_ext, dv_ext], axis=1)
    received = []
    for rim_part, direction in ((ext_terms[:maxlen], -1), (ext_terms[maxlen + block_rows :], 1)):
        received.append(
            passed_along(rim_part.astype(jnp.bfloat16), "blk", direction).astype(rim_part.dtype)
        )
    key_grads = ext_terms[maxlen : maxlen + block_rows] + jnp.concatenate(
        [received[1], received[0]], axis=0
    )
    grad_queries = grad_q.reshape(block_rows, channels)
    grad_keys = key_grads[:, :channels].astype(jnp.bfloat16)
    grad_values = key_grads[:, channels:].astype(jnp.bfloat16)
    return (conv_out.T, grad_queries.T, grad_keys.T, grad_values.T)


def solution(mesh):
    in_specs = (
        P(("blk", "uly"), None),
        P(("blk", "uly"), None),
        P(("blk", "uly"), None),
        P(),
        P(None, "uly"),
        P("uly"),
        P("uly", "blk"),
    )
    out_specs = (P("uly", "blk"), P("uly", "blk"), P("uly", "blk"), P("uly", "blk"))
    return jax.shard_map(
        on_device, mesh=mesh, in_specs=in_specs, out_specs=out_specs, check_vma=False
    )
```

```python
import jax
import jax.numpy as jnp
import functools
from jax import lax
from jax.experimental import pallas as pl
from jax.experimental.pallas import tpu as pltpu
from jax.sharding import PartitionSpec as P

KERNEL = 31
HEAD_DIM = 64


def extended(block, sides, width):
    for axis, dim in sides:
        count = lax.axis_size(axis)
        forward = [(i, i + 1) for i in range(count - 1)]
        backward = [(target, source) for source, target in forward]
        low = lax.ppermute(
            lax.slice_in_dim(block, block.shape[dim] - width, None, axis=dim), axis, forward
        )
        high = lax.ppermute(lax.slice_in_dim(block, 0, width, axis=dim), axis, backward)
        block = jnp.concatenate([low, block, high], axis=dim)
    return block


def passed_along(block, axis, distance):
    devices = range(lax.axis_size(axis))
    route = [(i - distance, i) for i in devices if i - distance in devices]
    return lax.ppermute(block, axis, route)


def segment_ids(lengths, frames, frame_total):
    starts = jnp.cumsum(lengths) - lengths
    seg_ids = jnp.sum((starts[None, :] <= frames[:, None]).astype(jnp.int32), axis=1) - 1
    inside = (frames >= 0) & (frames < frame_total)
    return jnp.where(inside, seg_ids, -1)


def rows_at(values_in, row_start, row_count):
    return lax.dynamic_slice_in_dim(values_in, row_start, row_count, 0)


def masked_scores(query_rows, key_rows, query_seg, key_seg):
    scores = HEAD_DIM ** (-0.5) * jnp.einsum(
        "rhe,she->hrs", query_rows, key_rows, preferred_element_type=jnp.float32
    )
    same_seg = (query_seg[:, None] == key_seg[None, :])[None]
    return (scores, same_seg)


def weights_of(scores, same_seg, row_top, row_total):
    return jnp.where(same_seg, jnp.exp(scores - row_top), 0.0) / row_total


TILE_Q = 256
TILE_K = 256
NT = (((1,), (1,)), ((), ()))
TN = (((0,), (0,)), ((), ()))


def forward_kernel(lo_ref, hi_ref, q_ref, k_ref, v_ref, qseg_ref, kseg_ref, o_ref, m_ref, l_ref):
    scale = HEAD_DIM ** (-0.5)

    def q_body(i, carry):
        r0 = pl.multiple_of(i * TILE_Q, TILE_Q)
        q = q_ref[pl.ds(r0, TILE_Q), :]
        qs = qseg_ref[pl.ds(r0, TILE_Q), :]

        def k_body(j, c):
            m, l, acc = c
            c0 = pl.multiple_of(j * TILE_K, TILE_K)
            k = k_ref[pl.ds(c0, TILE_K), :]
            v = v_ref[pl.ds(c0, TILE_K), :]
            ks = kseg_ref[:, pl.ds(c0, TILE_K)]
            s = scale * lax.dot_general(q, k, NT, preferred_element_type=jnp.float32)
            mask = qs == ks
            m_new = jnp.maximum(m, jnp.max(jnp.where(mask, s, -1e30), axis=1, keepdims=True))
            alpha = jnp.exp(m - m_new)
            p = jnp.where(mask, jnp.exp(s - m_new), 0.0)
            l = alpha * l + jnp.sum(p, axis=1, keepdims=True)
            acc = alpha * acc + jnp.dot(
                p.astype(jnp.bfloat16), v, preferred_element_type=jnp.float32
            )
            return (m_new, l, acc)

        init = (
            jnp.full((TILE_Q, 1), -1e30, jnp.float32),
            jnp.zeros((TILE_Q, 1), jnp.float32),
            jnp.zeros((TILE_Q, HEAD_DIM), jnp.float32),
        )
        m, l, acc = lax.fori_loop(lo_ref[i], hi_ref[i], k_body, init)
        o_ref[pl.ds(r0, TILE_Q), :] = (acc / l).astype(o_ref.dtype)
        m_ref[pl.ds(r0, TILE_Q), :] = m
        l_ref[pl.ds(r0, TILE_Q), :] = l
        return carry

    lax.fori_loop(0, q_ref.shape[0] // TILE_Q, q_body, 0)


def backward_kernel(
    lo_ref, hi_ref, q_ref, k_ref, v_ref, do_ref, qseg_ref, kseg_ref, m_ref, il_ref, d_ref,
    dq_ref, dk_ref, dv_ref,
):
    scale = HEAD_DIM ** (-0.5)
    dk_ref[...] = jnp.zeros_like(dk_ref)
    dv_ref[...] = jnp.zeros_like(dv_ref)

    def q_body(i, carry):
        r0 = pl.multiple_of(i * TILE_Q, TILE_Q)
        q = q_ref[pl.ds(r0, TILE_Q), :]
        do = do_ref[pl.ds(r0, TILE_Q), :]
        qs = qseg_ref[pl.ds(r0, TILE_Q), :]
        m = m_ref[pl.ds(r0, TILE_Q), :]
        il = il_ref[pl.ds(r0, TILE_Q), :]
        dlt = d_ref[pl.ds(r0, TILE_Q), :]

        def k_body(j, dq):
            c0 = pl.multiple_of(j * TILE_K, TILE_K)
            k = k_ref[pl.ds(c0, TILE_K), :]
            v = v_ref[pl.ds(c0, TILE_K), :]
            ks = kseg_ref[:, pl.ds(c0, TILE_K)]
            s = scale * lax.dot_general(q, k, NT, preferred_element_type=jnp.float32)
            mask = qs == ks
            p = jnp.where(mask, jnp.exp(s - m) * il, 0.0)
            dp = lax.dot_general(do, v, NT, preferred_element_type=jnp.float32)
            ds = (p * (dp - dlt)).astype(jnp.bfloat16)
            dk_ref[pl.ds(c0, TILE_K), :] += lax.dot_general(
                ds, q, TN, preferred_element_type=jnp.float32
            )
            dv_ref[pl.ds(c0, TILE_K), :] += lax.dot_general(
                p.astype(jnp.bfloat16), do, TN, preferred_element_type=jnp.float32
            )
            return dq + jnp.dot(ds, k, preferred_element_type=jnp.float32)

        dq = lax.fori_loop(
            lo_ref[i], hi_ref[i], k_body, jnp.zeros((TILE_Q, HEAD_DIM), jnp.float32)
        )
        dq_ref[pl.ds(r0, TILE_Q), :] = (scale * dq).astype(dq_ref.dtype)
        return carry

    lax.fori_loop(0, q_ref.shape[0] // TILE_Q, q_body, 0)
    dk_ref[...] = scale * dk_ref[...]


def vmem_call(kernel, n_smem, n_vmem, out_shape):
    return pl.pallas_call(
        kernel,
        out_shape=out_shape,
        in_specs=[pl.BlockSpec(memory_space=pltpu.SMEM)] * n_smem
        + [pl.BlockSpec(memory_space=pltpu.VMEM)] * n_vmem,
        out_specs=[pl.BlockSpec(memory_space=pltpu.VMEM)] * len(out_shape),
    )


def tile_ranges(lengths, seg_own, base, ext_rows):
    ends = jnp.cumsum(lengths)
    starts = ends - lengths
    first = seg_own[::TILE_Q]
    last = seg_own[TILE_Q - 1 :: TILE_Q]
    lo = (starts[first] - base) // TILE_K
    hi = (ends[last] - base + TILE_K - 1) // TILE_K
    lo = jnp.clip(lo, 0, ext_rows // TILE_K).astype(jnp.int32)
    hi = jnp.clip(hi, lo, ext_rows // TILE_K).astype(jnp.int32)
    return (lo, hi)


CONV_PAD = 128
CONV_CHUNK = 256


def conv_chunk(x_ref, wt_ref, lo, hi, c0, sign):
    window = x_ref[:, pl.ds(c0, CONV_CHUNK + 2 * CONV_PAD)]
    width = window.shape[1]
    total = jnp.zeros((window.shape[0], CONV_CHUNK), jnp.float32)
    for tap in range(KERNEL):
        d = sign * (tap - KERNEL // 2)
        shifted = pltpu.roll(window, (width - d) % width, 1) if d else window
        keep = (lo <= d) & (d < hi)
        total = total + wt_ref[:, tap : tap + 1] * jnp.where(
            keep, shifted[:, CONV_PAD : CONV_PAD + CONV_CHUNK], 0.0
        )
    return total


def conv_forward_kernel(x_ref, wt_ref, gain_ref, cot_ref, lo_ref, hi_ref, out_ref, gc_ref):
    gain = gain_ref[...]

    def body(c, carry):
        c0 = pl.multiple_of(c * CONV_CHUNK, CONV_CHUNK)
        cols = pl.ds(c0, CONV_CHUNK)
        conv_sum = conv_chunk(x_ref, wt_ref, lo_ref[:, cols], hi_ref[:, cols], c0, 1)
        spread = jnp.sqrt(jnp.mean(conv_sum * conv_sum, axis=0, keepdims=True) + 1e-05)
        normed = conv_sum / spread
        pre_act = normed * gain
        gate = 1.0 / (1.0 + jnp.exp(-pre_act))
        out_ref[:, cols] = (pre_act * gate).astype(out_ref.dtype)
        grad_pre = cot_ref[:, cols].astype(jnp.float32) * gate * (1.0 + pre_act * (1.0 - gate))
        weighted = grad_pre * gain
        gc_ref[:, cols] = (
            weighted - normed * jnp.mean(weighted * normed, axis=0, keepdims=True)
        ) / spread
        return carry

    lax.fori_loop(0, out_ref.shape[1] // CONV_CHUNK, body, 0)


def conv_backward_kernel(y_ref, wt_ref, att_ref, lo_ref, hi_ref, ga_ref, delta_ref):
    def body(c, carry):
        c0 = pl.multiple_of(c * CONV_CHUNK, CONV_CHUNK)
        cols = pl.ds(c0, CONV_CHUNK)
        grad_sum = conv_chunk(y_ref, wt_ref, lo_ref[:, cols], hi_ref[:, cols], c0, -1)
        grad_att = grad_sum.astype(ga_ref.dtype)
        ga_ref[:, cols] = grad_att
        delta_ref[:, cols] = jnp.sum(
            grad_att.astype(jnp.float32) * att_ref[:, cols].astype(jnp.float32),
            axis=0,
            keepdims=True,
        )
        return carry

    lax.fori_loop(0, ga_ref.shape[1] // CONV_CHUNK, body, 0)


def padded_rims(block, half):
    count = lax.axis_size("blk")
    forward = [(i, i + 1) for i in range(count - 1)]
    backward = [(target, source) for source, target in forward]
    low = lax.ppermute(block[:, block.shape[1] - half :], "blk", forward)
    high = lax.ppermute(block[:, :half], "blk", backward)
    gap = jnp.zeros((block.shape[0], CONV_PAD - half), jnp.float32)
    return jnp.concatenate(
        [gap, low.astype(jnp.float32), block.astype(jnp.float32), high.astype(jnp.float32), gap],
        axis=1,
    )


def on_device(queries, keys, values, lengths, conv_weight, norm_gain, cotangent):
    rows_in, width = queries.shape
    heads_total = width // HEAD_DIM
    stacked = jnp.stack(
        [a.reshape(rows_in, heads_total, HEAD_DIM) for a in (queries, keys, values)], axis=2
    ).reshape(rows_in, heads_total * 3 * HEAD_DIM)
    local_qkv = lax.all_to_all(stacked, "uly", split_axis=1, concat_axis=0, tiled=True)
    local_qkv = local_qkv.reshape(local_qkv.shape[0], -1, 3, HEAD_DIM)
    local_q, local_k, local_v = (
        local_qkv[:, :, i].reshape(local_qkv.shape[0], -1) for i in range(3)
    )
    block_rows, channels = local_q.shape
    heads_here = channels // HEAD_DIM
    maxlen = block_rows // 2
    rows_q = min(512, block_rows)
    window = rows_q + 2 * maxlen
    conv_half = KERNEL // 2
    block_count = block_rows // rows_q
    score_scale = HEAD_DIM ** (-0.5)
    frame_total = lax.axis_size("blk") * block_rows
    first_frame = lax.axis_index("blk") * block_rows
    seg_ext = segment_ids(
        lengths,
        first_frame - maxlen + jnp.arange(block_rows + 2 * maxlen, dtype=jnp.int32),
        frame_total,
    )
    seg_own = seg_ext[maxlen : maxlen + block_rows]
    seg_conv = seg_ext[maxlen - conv_half : maxlen + block_rows + conv_half]
    near_pairs = extended(jnp.concatenate([local_k, local_v], axis=1), (("blk", 0),), maxlen)
    k_ext = near_pairs[:, :channels].reshape(-1, heads_here, HEAD_DIM)
    v_ext = near_pairs[:, channels:].reshape(-1, heads_here, HEAD_DIM)
    q_heads = local_q.reshape(block_rows, heads_here, HEAD_DIM)
    starts = jnp.arange(block_count, dtype=jnp.int32) * rows_q

    assert heads_here == 1
    lo_t, hi_t = tile_ranges(lengths, seg_own, first_frame - maxlen, block_rows + 2 * maxlen)
    qseg_col = seg_own[:, None].astype(jnp.int32)
    kseg_row = seg_ext[None, :].astype(jnp.int32)
    k_flat = k_ext.reshape(-1, HEAD_DIM)
    v_flat = v_ext.reshape(-1, HEAD_DIM)
    attended, row_tops, row_totals = vmem_call(
        forward_kernel,
        2,
        5,
        (
            jax.ShapeDtypeStruct((block_rows, HEAD_DIM), jnp.bfloat16),
            jax.ShapeDtypeStruct((block_rows, 1), jnp.float32),
            jax.ShapeDtypeStruct((block_rows, 1), jnp.float32),
        ),
    )(lo_t, hi_t, local_q, k_flat, v_flat, qseg_col, kseg_row)
    ends = jnp.cumsum(lengths)
    seg_at = jnp.clip(seg_own, 0, lengths.shape[0] - 1)
    frame_at = first_frame + jnp.arange(block_rows, dtype=jnp.int32)
    lo_off = (ends[seg_at] - lengths[seg_at] - frame_at)[None, :].astype(jnp.int32)
    hi_off = (ends[seg_at] - frame_at)[None, :].astype(jnp.int32)
    weight_t = conv_weight.T
    att_t = attended.T
    conv_out_t, grad_conv_t = vmem_call(
        conv_forward_kernel,
        0,
        6,
        (
            jax.ShapeDtypeStruct((HEAD_DIM, block_rows), jnp.bfloat16),
            jax.ShapeDtypeStruct((HEAD_DIM, block_rows), jnp.float32),
        ),
    )(padded_rims(att_t, conv_half), weight_t, norm_gain[:, None], cotangent, lo_off, hi_off)
    grad_att_t, delta_row = vmem_call(
        conv_backward_kernel,
        0,
        5,
        (
            jax.ShapeDtypeStruct((HEAD_DIM, block_rows), jnp.bfloat16),
            jax.ShapeDtypeStruct((1, block_rows), jnp.float32),
        ),
    )(padded_rims(grad_conv_t, conv_half), weight_t, att_t, lo_off, hi_off)
    grad_attended = grad_att_t.T
    row_delta = delta_row.T

    grad_q, dk_ext, dv_ext = vmem_call(
        backward_kernel,
        2,
        9,
        (
            jax.ShapeDtypeStruct((block_rows, HEAD_DIM), jnp.bfloat16),
            jax.ShapeDtypeStruct((block_rows + 2 * maxlen, HEAD_DIM), jnp.float32),
            jax.ShapeDtypeStruct((block_rows + 2 * maxlen, HEAD_DIM), jnp.float32),
        ),
    )(
        lo_t,
        hi_t,
        local_q,
        k_flat,
        v_flat,
        grad_attended,
        qseg_col,
        kseg_row,
        row_tops,
        1.0 / row_totals,
        row_delta,
    )
    ext_terms = jnp.concatenate([dk_ext, dv_ext], axis=1)
    received = []
    for rim_part, direction in ((ext_terms[:maxlen], -1), (ext_terms[maxlen + block_rows :], 1)):
        received.append(
            passed_along(rim_part.astype(jnp.bfloat16), "blk", direction).astype(rim_part.dtype)
        )
    key_grads = ext_terms[maxlen : maxlen + block_rows] + jnp.concatenate(
        [received[1], received[0]], axis=0
    )
    grad_queries = grad_q.reshape(block_rows, channels)
    grad_keys = key_grads[:, :channels].astype(jnp.bfloat16)
    grad_values = key_grads[:, channels:].astype(jnp.bfloat16)
    return (conv_out_t, grad_queries.T, grad_keys.T, grad_values.T)


def solution(mesh):
    in_specs = (
        P(("blk", "uly"), None),
        P(("blk", "uly"), None),
        P(("blk", "uly"), None),
        P(),
        P(None, "uly"),
        P("uly"),
        P("uly", "blk"),
    )
    out_specs = (P("uly", "blk"), P("uly", "blk"), P("uly", "blk"), P("uly", "blk"))
    return jax.shard_map(
        on_device, mesh=mesh, in_specs=in_specs, out_specs=out_specs, check_vma=False
    )
```

```python
import jax
import jax.numpy as jnp
import functools
from jax import lax
from jax.experimental import pallas as pl
from jax.experimental.pallas import tpu as pltpu
from jax.sharding import PartitionSpec as P

KERNEL = 31
HEAD_DIM = 64


def extended(block, sides, width):
    for axis, dim in sides:
        count = lax.axis_size(axis)
        forward = [(i, i + 1) for i in range(count - 1)]
        backward = [(target, source) for source, target in forward]
        low = lax.ppermute(
            lax.slice_in_dim(block, block.shape[dim] - width, None, axis=dim), axis, forward
        )
        high = lax.ppermute(lax.slice_in_dim(block, 0, width, axis=dim), axis, backward)
        block = jnp.concatenate([low, block, high], axis=dim)
    return block


def passed_along(block, axis, distance):
    devices = range(lax.axis_size(axis))
    route = [(i - distance, i) for i in devices if i - distance in devices]
    return lax.ppermute(block, axis, route)


def segment_ids(lengths, frames, frame_total):
    starts = jnp.cumsum(lengths) - lengths
    seg_ids = jnp.sum((starts[None, :] <= frames[:, None]).astype(jnp.int32), axis=1) - 1
    inside = (frames >= 0) & (frames < frame_total)
    return jnp.where(inside, seg_ids, -1)


def rows_at(values_in, row_start, row_count):
    return lax.dynamic_slice_in_dim(values_in, row_start, row_count, 0)


def masked_scores(query_rows, key_rows, query_seg, key_seg):
    scores = HEAD_DIM ** (-0.5) * jnp.einsum(
        "rhe,she->hrs", query_rows, key_rows, preferred_element_type=jnp.float32
    )
    same_seg = (query_seg[:, None] == key_seg[None, :])[None]
    return (scores, same_seg)


def weights_of(scores, same_seg, row_top, row_total):
    return jnp.where(same_seg, jnp.exp(scores - row_top), 0.0) / row_total


TILE_Q = 256
TILE_K = 256
NT = (((1,), (1,)), ((), ()))
TN = (((0,), (0,)), ((), ()))


def forward_kernel(lo_ref, hi_ref, q_ref, k_ref, v_ref, qseg_ref, kseg_ref, o_ref, m_ref, l_ref):
    scale = HEAD_DIM ** (-0.5)

    def q_body(i, carry):
        r0 = pl.multiple_of(i * TILE_Q, TILE_Q)
        q = q_ref[pl.ds(r0, TILE_Q), :]
        qs = qseg_ref[pl.ds(r0, TILE_Q), :]

        def k_body(j, c):
            m, l, acc = c
            c0 = pl.multiple_of(j * TILE_K, TILE_K)
            k = k_ref[pl.ds(c0, TILE_K), :]
            v = v_ref[pl.ds(c0, TILE_K), :]
            ks = kseg_ref[:, pl.ds(c0, TILE_K)]
            s = scale * lax.dot_general(q, k, NT, preferred_element_type=jnp.float32)
            mask = qs == ks
            m_new = jnp.maximum(m, jnp.max(jnp.where(mask, s, -1e30), axis=1, keepdims=True))
            alpha = jnp.exp(m - m_new)
            p = jnp.where(mask, jnp.exp(s - m_new), 0.0)
            l = alpha * l + jnp.sum(p, axis=1, keepdims=True)
            acc = alpha * acc + jnp.dot(
                p.astype(jnp.bfloat16), v, preferred_element_type=jnp.float32
            )
            return (m_new, l, acc)

        init = (
            jnp.full((TILE_Q, 1), -1e30, jnp.float32),
            jnp.zeros((TILE_Q, 1), jnp.float32),
            jnp.zeros((TILE_Q, HEAD_DIM), jnp.float32),
        )
        m, l, acc = lax.fori_loop(lo_ref[i], hi_ref[i], k_body, init)
        o_ref[pl.ds(r0, TILE_Q), :] = (acc / l).astype(o_ref.dtype)
        m_ref[pl.ds(r0, TILE_Q), :] = m
        l_ref[pl.ds(r0, TILE_Q), :] = l
        return carry

    lax.fori_loop(0, q_ref.shape[0] // TILE_Q, q_body, 0)


def backward_kernel(
    lo_ref, hi_ref, q_ref, k_ref, v_ref, do_ref, qseg_ref, kseg_ref, m_ref, il_ref, d_ref,
    dq_ref, dk_ref, dv_ref,
):
    scale = HEAD_DIM ** (-0.5)
    dk_ref[...] = jnp.zeros_like(dk_ref)
    dv_ref[...] = jnp.zeros_like(dv_ref)

    def q_body(i, carry):
        r0 = pl.multiple_of(i * TILE_Q, TILE_Q)
        q = q_ref[pl.ds(r0, TILE_Q), :]
        do = do_ref[pl.ds(r0, TILE_Q), :]
        qs = qseg_ref[pl.ds(r0, TILE_Q), :]
        m = m_ref[pl.ds(r0, TILE_Q), :]
        il = il_ref[pl.ds(r0, TILE_Q), :]
        dlt = d_ref[pl.ds(r0, TILE_Q), :]

        def k_body(j, dq):
            c0 = pl.multiple_of(j * TILE_K, TILE_K)
            k = k_ref[pl.ds(c0, TILE_K), :]
            v = v_ref[pl.ds(c0, TILE_K), :]
            ks = kseg_ref[:, pl.ds(c0, TILE_K)]
            s = scale * lax.dot_general(q, k, NT, preferred_element_type=jnp.float32)
            mask = qs == ks
            p = jnp.where(mask, jnp.exp(s - m) * il, 0.0)
            dp = lax.dot_general(do, v, NT, preferred_element_type=jnp.float32)
            ds = (p * (dp - dlt)).astype(jnp.bfloat16)
            dk_ref[pl.ds(c0, TILE_K), :] += lax.dot_general(
                ds, q, TN, preferred_element_type=jnp.float32
            )
            dv_ref[pl.ds(c0, TILE_K), :] += lax.dot_general(
                p.astype(jnp.bfloat16), do, TN, preferred_element_type=jnp.float32
            )
            return dq + jnp.dot(ds, k, preferred_element_type=jnp.float32)

        dq = lax.fori_loop(
            lo_ref[i], hi_ref[i], k_body, jnp.zeros((TILE_Q, HEAD_DIM), jnp.float32)
        )
        dq_ref[pl.ds(r0, TILE_Q), :] = (scale * dq).astype(dq_ref.dtype)
        return carry

    lax.fori_loop(0, q_ref.shape[0] // TILE_Q, q_body, 0)
    dk_ref[...] = scale * dk_ref[...]


def vmem_call(kernel, n_smem, n_vmem, out_shape):
    return pl.pallas_call(
        kernel,
        out_shape=out_shape,
        in_specs=[pl.BlockSpec(memory_space=pltpu.SMEM)] * n_smem
        + [pl.BlockSpec(memory_space=pltpu.VMEM)] * n_vmem,
        out_specs=[pl.BlockSpec(memory_space=pltpu.VMEM)] * len(out_shape),
    )


def segment_bounds(lengths, frames):
    ends = jnp.cumsum(lengths)
    starts = ends - lengths
    seg_start = jnp.max(jnp.where(starts[None, :] <= frames[:, None], starts[None, :], 0), axis=1)
    big = jnp.iinfo(jnp.int32).max
    seg_end = jnp.min(jnp.where(ends[None, :] > frames[:, None], ends[None, :], big), axis=1)
    return (seg_start, jnp.minimum(seg_end, ends[-1]))


def tile_ranges(lengths, base, ext_rows, block_rows):
    frames = base + (ext_rows - block_rows) // 2 + jnp.arange(block_rows, dtype=jnp.int32)
    seg_start, seg_end = segment_bounds(lengths, frames)
    lo = (seg_start[::TILE_Q] - base) // TILE_K
    hi = (seg_end[TILE_Q - 1 :: TILE_Q] - base + TILE_K - 1) // TILE_K
    lo = jnp.clip(lo, 0, ext_rows // TILE_K).astype(jnp.int32)
    hi = jnp.clip(hi, lo, ext_rows // TILE_K).astype(jnp.int32)
    return (lo, hi)


CONV_PAD = 128
CONV_CHUNK = 256


def conv_chunk(x_ref, wt_ref, lo, hi, c0, sign):
    window = x_ref[:, pl.ds(c0, CONV_CHUNK + 2 * CONV_PAD)]
    width = window.shape[1]
    total = jnp.zeros((window.shape[0], CONV_CHUNK), jnp.float32)
    for tap in range(KERNEL):
        d = sign * (tap - KERNEL // 2)
        shifted = pltpu.roll(window, (width - d) % width, 1) if d else window
        keep = (lo <= d) & (d < hi)
        total = total + wt_ref[:, tap : tap + 1] * jnp.where(
            keep, shifted[:, CONV_PAD : CONV_PAD + CONV_CHUNK], 0.0
        )
    return total


def conv_forward_kernel(x_ref, wt_ref, gain_ref, cot_ref, lo_ref, hi_ref, out_ref, gc_ref):
    gain = gain_ref[...]

    def body(c, carry):
        c0 = pl.multiple_of(c * CONV_CHUNK, CONV_CHUNK)
        cols = pl.ds(c0, CONV_CHUNK)
        conv_sum = conv_chunk(x_ref, wt_ref, lo_ref[:, cols], hi_ref[:, cols], c0, 1)
        spread = jnp.sqrt(jnp.mean(conv_sum * conv_sum, axis=0, keepdims=True) + 1e-05)
        normed = conv_sum / spread
        pre_act = normed * gain
        gate = 1.0 / (1.0 + jnp.exp(-pre_act))
        out_ref[:, cols] = (pre_act * gate).astype(out_ref.dtype)
        grad_pre = cot_ref[:, cols].astype(jnp.float32) * gate * (1.0 + pre_act * (1.0 - gate))
        weighted = grad_pre * gain
        gc_ref[:, cols] = (
            weighted - normed * jnp.mean(weighted * normed, axis=0, keepdims=True)
        ) / spread
        return carry

    lax.fori_loop(0, out_ref.shape[1] // CONV_CHUNK, body, 0)


def conv_backward_kernel(y_ref, wt_ref, att_ref, lo_ref, hi_ref, ga_ref, delta_ref):
    def body(c, carry):
        c0 = pl.multiple_of(c * CONV_CHUNK, CONV_CHUNK)
        cols = pl.ds(c0, CONV_CHUNK)
        grad_sum = conv_chunk(y_ref, wt_ref, lo_ref[:, cols], hi_ref[:, cols], c0, -1)
        grad_att = grad_sum.astype(ga_ref.dtype)
        ga_ref[:, cols] = grad_att
        delta_ref[:, cols] = jnp.sum(
            grad_att.astype(jnp.float32) * att_ref[:, cols].astype(jnp.float32),
            axis=0,
            keepdims=True,
        )
        return carry

    lax.fori_loop(0, ga_ref.shape[1] // CONV_CHUNK, body, 0)


def padded_rims(block, half):
    count = lax.axis_size("blk")
    forward = [(i, i + 1) for i in range(count - 1)]
    backward = [(target, source) for source, target in forward]
    low = lax.ppermute(block[:, block.shape[1] - half :], "blk", forward)
    high = lax.ppermute(block[:, :half], "blk", backward)
    gap = jnp.zeros((block.shape[0], CONV_PAD - half), jnp.float32)
    return jnp.concatenate(
        [gap, low.astype(jnp.float32), block.astype(jnp.float32), high.astype(jnp.float32), gap],
        axis=1,
    )


def on_device(queries, keys, values, lengths, conv_weight, norm_gain, cotangent):
    rows_in, width = queries.shape
    heads_total = width // HEAD_DIM
    stacked = jnp.stack(
        [a.reshape(rows_in, heads_total, HEAD_DIM) for a in (queries, keys, values)], axis=2
    ).reshape(rows_in, heads_total * 3 * HEAD_DIM)
    local_qkv = lax.all_to_all(stacked, "uly", split_axis=1, concat_axis=0, tiled=True)
    local_qkv = local_qkv.reshape(local_qkv.shape[0], -1, 3, HEAD_DIM)
    local_q, local_k, local_v = (
        local_qkv[:, :, i].reshape(local_qkv.shape[0], -1) for i in range(3)
    )
    block_rows, channels = local_q.shape
    heads_here = channels // HEAD_DIM
    maxlen = block_rows // 2
    rows_q = min(512, block_rows)
    window = rows_q + 2 * maxlen
    conv_half = KERNEL // 2
    block_count = block_rows // rows_q
    score_scale = HEAD_DIM ** (-0.5)
    frame_total = lax.axis_size("blk") * block_rows
    first_frame = lax.axis_index("blk") * block_rows
    seg_ext = segment_ids(
        lengths,
        first_frame - maxlen + jnp.arange(block_rows + 2 * maxlen, dtype=jnp.int32),
        frame_total,
    )
    seg_own = seg_ext[maxlen : maxlen + block_rows]
    seg_conv = seg_ext[maxlen - conv_half : maxlen + block_rows + conv_half]
    near_pairs = extended(jnp.concatenate([local_k, local_v], axis=1), (("blk", 0),), maxlen)
    k_ext = near_pairs[:, :channels].reshape(-1, heads_here, HEAD_DIM)
    v_ext = near_pairs[:, channels:].reshape(-1, heads_here, HEAD_DIM)
    q_heads = local_q.reshape(block_rows, heads_here, HEAD_DIM)
    starts = jnp.arange(block_count, dtype=jnp.int32) * rows_q

    assert heads_here == 1
    lo_t, hi_t = tile_ranges(lengths, first_frame - maxlen, block_rows + 2 * maxlen, block_rows)
    qseg_col = seg_own[:, None].astype(jnp.int32)
    kseg_row = seg_ext[None, :].astype(jnp.int32)
    k_flat = k_ext.reshape(-1, HEAD_DIM)
    v_flat = v_ext.reshape(-1, HEAD_DIM)
    attended, row_tops, row_totals = vmem_call(
        forward_kernel,
        2,
        5,
        (
            jax.ShapeDtypeStruct((block_rows, HEAD_DIM), jnp.bfloat16),
            jax.ShapeDtypeStruct((block_rows, 1), jnp.float32),
            jax.ShapeDtypeStruct((block_rows, 1), jnp.float32),
        ),
    )(lo_t, hi_t, local_q, k_flat, v_flat, qseg_col, kseg_row)
    frame_at = first_frame + jnp.arange(block_rows, dtype=jnp.int32)
    seg_start, seg_end = segment_bounds(lengths, frame_at)
    lo_off = (seg_start - frame_at)[None, :].astype(jnp.int32)
    hi_off = (seg_end - frame_at)[None, :].astype(jnp.int32)
    weight_t = conv_weight.T
    att_t = attended.T
    conv_out_t, grad_conv_t = vmem_call(
        conv_forward_kernel,
        0,
        6,
        (
            jax.ShapeDtypeStruct((HEAD_DIM, block_rows), jnp.bfloat16),
            jax.ShapeDtypeStruct((HEAD_DIM, block_rows), jnp.float32),
        ),
    )(padded_rims(att_t, conv_half), weight_t, norm_gain[:, None], cotangent, lo_off, hi_off)
    grad_att_t, delta_row = vmem_call(
        conv_backward_kernel,
        0,
        5,
        (
            jax.ShapeDtypeStruct((HEAD_DIM, block_rows), jnp.bfloat16),
            jax.ShapeDtypeStruct((1, block_rows), jnp.float32),
        ),
    )(padded_rims(grad_conv_t, conv_half), weight_t, att_t, lo_off, hi_off)
    grad_attended = grad_att_t.T
    row_delta = delta_row.T

    grad_q, dk_ext, dv_ext = vmem_call(
        backward_kernel,
        2,
        9,
        (
            jax.ShapeDtypeStruct((block_rows, HEAD_DIM), jnp.bfloat16),
            jax.ShapeDtypeStruct((block_rows + 2 * maxlen, HEAD_DIM), jnp.float32),
            jax.ShapeDtypeStruct((block_rows + 2 * maxlen, HEAD_DIM), jnp.float32),
        ),
    )(
        lo_t,
        hi_t,
        local_q,
        k_flat,
        v_flat,
        grad_attended,
        qseg_col,
        kseg_row,
        row_tops,
        1.0 / row_totals,
        row_delta,
    )
    ext_terms = jnp.concatenate([dk_ext, dv_ext], axis=1)
    received = []
    for rim_part, direction in ((ext_terms[:maxlen], -1), (ext_terms[maxlen + block_rows :], 1)):
        received.append(
            passed_along(rim_part.astype(jnp.bfloat16), "blk", direction).astype(rim_part.dtype)
        )
    key_grads = ext_terms[maxlen : maxlen + block_rows] + jnp.concatenate(
        [received[1], received[0]], axis=0
    )
    grad_queries = grad_q.reshape(block_rows, channels)
    grad_keys = key_grads[:, :channels].astype(jnp.bfloat16)
    grad_values = key_grads[:, channels:].astype(jnp.bfloat16)
    return (conv_out_t, grad_queries.T, grad_keys.T, grad_values.T)


def solution(mesh):
    in_specs = (
        P(("blk", "uly"), None),
        P(("blk", "uly"), None),
        P(("blk", "uly"), None),
        P(),
        P(None, "uly"),
        P("uly"),
        P("uly", "blk"),
    )
    out_specs = (P("uly", "blk"), P("uly", "blk"), P("uly", "blk"), P("uly", "blk"))
    return jax.shard_map(
        on_device, mesh=mesh, in_specs=in_specs, out_specs=out_specs, check_vma=False
    )
```

```python
import jax
import jax.numpy as jnp
import functools
from jax import lax
from jax.experimental import pallas as pl
from jax.experimental.pallas import tpu as pltpu
from jax.sharding import PartitionSpec as P

KERNEL = 31
HEAD_DIM = 64


def extended(block, sides, width):
    for axis, dim in sides:
        count = lax.axis_size(axis)
        forward = [(i, i + 1) for i in range(count - 1)]
        backward = [(target, source) for source, target in forward]
        low = lax.ppermute(
            lax.slice_in_dim(block, block.shape[dim] - width, None, axis=dim), axis, forward
        )
        high = lax.ppermute(lax.slice_in_dim(block, 0, width, axis=dim), axis, backward)
        block = jnp.concatenate([low, block, high], axis=dim)
    return block


def passed_along(block, axis, distance):
    devices = range(lax.axis_size(axis))
    route = [(i - distance, i) for i in devices if i - distance in devices]
    return lax.ppermute(block, axis, route)


def segment_ids(lengths, frames, frame_total):
    starts = jnp.cumsum(lengths) - lengths
    seg_ids = jnp.sum((starts[None, :] <= frames[:, None]).astype(jnp.int32), axis=1) - 1
    inside = (frames >= 0) & (frames < frame_total)
    return jnp.where(inside, seg_ids, -1)


def rows_at(values_in, row_start, row_count):
    return lax.dynamic_slice_in_dim(values_in, row_start, row_count, 0)


def masked_scores(query_rows, key_rows, query_seg, key_seg):
    scores = HEAD_DIM ** (-0.5) * jnp.einsum(
        "rhe,she->hrs", query_rows, key_rows, preferred_element_type=jnp.float32
    )
    same_seg = (query_seg[:, None] == key_seg[None, :])[None]
    return (scores, same_seg)


def weights_of(scores, same_seg, row_top, row_total):
    return jnp.where(same_seg, jnp.exp(scores - row_top), 0.0) / row_total


TILE_Q = 256
TILE_K = 256
NT = (((1,), (1,)), ((), ()))
TN = (((0,), (0,)), ((), ()))


def forward_kernel(lo_ref, hi_ref, q_ref, k_ref, v_ref, qseg_ref, kseg_ref, o_ref, m_ref, l_ref):
    scale = HEAD_DIM ** (-0.5)

    def q_body(i, carry):
        r0 = pl.multiple_of(i * TILE_Q, TILE_Q)
        q = q_ref[pl.ds(r0, TILE_Q), :]
        qs = qseg_ref[pl.ds(r0, TILE_Q), :]

        def k_body(j, c):
            m, l, acc = c
            c0 = pl.multiple_of(j * TILE_K, TILE_K)
            k = k_ref[pl.ds(c0, TILE_K), :]
            v = v_ref[pl.ds(c0, TILE_K), :]
            ks = kseg_ref[:, pl.ds(c0, TILE_K)]
            s = scale * lax.dot_general(q, k, NT, preferred_element_type=jnp.float32)
            mask = qs == ks
            m_new = jnp.maximum(m, jnp.max(jnp.where(mask, s, -1e30), axis=1, keepdims=True))
            alpha = jnp.exp(m - m_new)
            p = jnp.where(mask, jnp.exp(s - m_new), 0.0)
            l = alpha * l + jnp.sum(p, axis=1, keepdims=True)
            acc = alpha * acc + jnp.dot(
                p.astype(jnp.bfloat16), v, preferred_element_type=jnp.float32
            )
            return (m_new, l, acc)

        init = (
            jnp.full((TILE_Q, 1), -1e30, jnp.float32),
            jnp.zeros((TILE_Q, 1), jnp.float32),
            jnp.zeros((TILE_Q, HEAD_DIM), jnp.float32),
        )
        m, l, acc = lax.fori_loop(lo_ref[i], hi_ref[i], k_body, init)
        o_ref[pl.ds(r0, TILE_Q), :] = (acc / l).astype(o_ref.dtype)
        m_ref[pl.ds(r0, TILE_Q), :] = m
        l_ref[pl.ds(r0, TILE_Q), :] = l
        return carry

    lax.fori_loop(0, q_ref.shape[0] // TILE_Q, q_body, 0)


def backward_kernel(
    lo_ref, hi_ref, q_ref, k_ref, v_ref, do_ref, qt_ref, dot_ref, qseg_ref, kseg_ref, m_ref,
    il_ref, d_ref, dq_ref, dk_ref, dv_ref,
):
    scale = HEAD_DIM ** (-0.5)
    dk_ref[...] = jnp.zeros_like(dk_ref)
    dv_ref[...] = jnp.zeros_like(dv_ref)

    def q_body(i, carry):
        r0 = pl.multiple_of(i * TILE_Q, TILE_Q)
        q = q_ref[pl.ds(r0, TILE_Q), :]
        do = do_ref[pl.ds(r0, TILE_Q), :]
        qs = qseg_ref[pl.ds(r0, TILE_Q), :]
        m = m_ref[pl.ds(r0, TILE_Q), :]
        il = il_ref[pl.ds(r0, TILE_Q), :]
        dlt = d_ref[pl.ds(r0, TILE_Q), :]
        q_t = qt_ref[:, pl.ds(r0, TILE_Q)]
        do_t = dot_ref[:, pl.ds(r0, TILE_Q)]

        def k_body(j, dq):
            c0 = pl.multiple_of(j * TILE_K, TILE_K)
            k = k_ref[pl.ds(c0, TILE_K), :]
            v = v_ref[pl.ds(c0, TILE_K), :]
            ks = kseg_ref[:, pl.ds(c0, TILE_K)]
            s = scale * lax.dot_general(q, k, NT, preferred_element_type=jnp.float32)
            mask = qs == ks
            p = jnp.where(mask, jnp.exp(s - m) * il, 0.0)
            dp = lax.dot_general(do, v, NT, preferred_element_type=jnp.float32)
            ds = (p * (dp - dlt)).astype(jnp.bfloat16)
            dk_ref[:, pl.ds(c0, TILE_K)] += jnp.dot(q_t, ds, preferred_element_type=jnp.float32)
            dv_ref[:, pl.ds(c0, TILE_K)] += jnp.dot(
                do_t, p.astype(jnp.bfloat16), preferred_element_type=jnp.float32
            )
            return dq + jnp.dot(ds, k, preferred_element_type=jnp.float32)

        dq = lax.fori_loop(
            lo_ref[i], hi_ref[i], k_body, jnp.zeros((TILE_Q, HEAD_DIM), jnp.float32)
        )
        dq_ref[pl.ds(r0, TILE_Q), :] = (scale * dq).astype(dq_ref.dtype)
        return carry

    lax.fori_loop(0, q_ref.shape[0] // TILE_Q, q_body, 0)
    dk_ref[...] = scale * dk_ref[...]


def vmem_call(kernel, n_smem, n_vmem, out_shape):
    return pl.pallas_call(
        kernel,
        out_shape=out_shape,
        in_specs=[pl.BlockSpec(memory_space=pltpu.SMEM)] * n_smem
        + [pl.BlockSpec(memory_space=pltpu.VMEM)] * n_vmem,
        out_specs=[pl.BlockSpec(memory_space=pltpu.VMEM)] * len(out_shape),
    )


def segment_bounds(lengths, frames):
    ends = jnp.cumsum(lengths)
    starts = ends - lengths
    seg_start = jnp.max(jnp.where(starts[None, :] <= frames[:, None], starts[None, :], 0), axis=1)
    big = jnp.iinfo(jnp.int32).max
    seg_end = jnp.min(jnp.where(ends[None, :] > frames[:, None], ends[None, :], big), axis=1)
    return (seg_start, jnp.minimum(seg_end, ends[-1]))


def tile_ranges(lengths, base, ext_rows, block_rows):
    frames = base + (ext_rows - block_rows) // 2 + jnp.arange(block_rows, dtype=jnp.int32)
    seg_start, seg_end = segment_bounds(lengths, frames)
    lo = (seg_start[::TILE_Q] - base) // TILE_K
    hi = (seg_end[TILE_Q - 1 :: TILE_Q] - base + TILE_K - 1) // TILE_K
    lo = jnp.clip(lo, 0, ext_rows // TILE_K).astype(jnp.int32)
    hi = jnp.clip(hi, lo, ext_rows // TILE_K).astype(jnp.int32)
    return (lo, hi)


CONV_PAD = 128
CONV_CHUNK = 256


def conv_chunk(x_ref, wt_ref, lo, hi, c0, sign):
    window = x_ref[:, pl.ds(c0, CONV_CHUNK + 2 * CONV_PAD)]
    width = window.shape[1]
    total = jnp.zeros((window.shape[0], CONV_CHUNK), jnp.float32)
    for tap in range(KERNEL):
        d = sign * (tap - KERNEL // 2)
        shifted = pltpu.roll(window, (width - d) % width, 1) if d else window
        keep = (lo <= d) & (d < hi)
        total = total + wt_ref[:, tap : tap + 1] * jnp.where(
            keep, shifted[:, CONV_PAD : CONV_PAD + CONV_CHUNK], 0.0
        )
    return total


def conv_forward_kernel(x_ref, wt_ref, gain_ref, cot_ref, lo_ref, hi_ref, out_ref, gc_ref):
    gain = gain_ref[...]

    def body(c, carry):
        c0 = pl.multiple_of(c * CONV_CHUNK, CONV_CHUNK)
        cols = pl.ds(c0, CONV_CHUNK)
        conv_sum = conv_chunk(x_ref, wt_ref, lo_ref[:, cols], hi_ref[:, cols], c0, 1)
        spread = jnp.sqrt(jnp.mean(conv_sum * conv_sum, axis=0, keepdims=True) + 1e-05)
        normed = conv_sum / spread
        pre_act = normed * gain
        gate = 1.0 / (1.0 + jnp.exp(-pre_act))
        out_ref[:, cols] = (pre_act * gate).astype(out_ref.dtype)
        grad_pre = cot_ref[:, cols].astype(jnp.float32) * gate * (1.0 + pre_act * (1.0 - gate))
        weighted = grad_pre * gain
        gc_ref[:, cols] = (
            weighted - normed * jnp.mean(weighted * normed, axis=0, keepdims=True)
        ) / spread
        return carry

    lax.fori_loop(0, out_ref.shape[1] // CONV_CHUNK, body, 0)


def conv_backward_kernel(y_ref, wt_ref, att_ref, lo_ref, hi_ref, ga_ref, delta_ref):
    def body(c, carry):
        c0 = pl.multiple_of(c * CONV_CHUNK, CONV_CHUNK)
        cols = pl.ds(c0, CONV_CHUNK)
        grad_sum = conv_chunk(y_ref, wt_ref, lo_ref[:, cols], hi_ref[:, cols], c0, -1)
        grad_att = grad_sum.astype(ga_ref.dtype)
        ga_ref[:, cols] = grad_att
        delta_ref[:, cols] = jnp.sum(
            grad_att.astype(jnp.float32) * att_ref[:, cols].astype(jnp.float32),
            axis=0,
            keepdims=True,
        )
        return carry

    lax.fori_loop(0, ga_ref.shape[1] // CONV_CHUNK, body, 0)


def padded_rims(block, half):
    count = lax.axis_size("blk")
    forward = [(i, i + 1) for i in range(count - 1)]
    backward = [(target, source) for source, target in forward]
    low = lax.ppermute(block[:, block.shape[1] - half :], "blk", forward)
    high = lax.ppermute(block[:, :half], "blk", backward)
    gap = jnp.zeros((block.shape[0], CONV_PAD - half), jnp.float32)
    return jnp.concatenate(
        [gap, low.astype(jnp.float32), block.astype(jnp.float32), high.astype(jnp.float32), gap],
        axis=1,
    )


def on_device(queries, keys, values, lengths, conv_weight, norm_gain, cotangent):
    rows_in, width = queries.shape
    heads_total = width // HEAD_DIM
    stacked = jnp.stack(
        [a.reshape(rows_in, heads_total, HEAD_DIM) for a in (queries, keys, values)], axis=2
    ).reshape(rows_in, heads_total * 3 * HEAD_DIM)
    local_qkv = lax.all_to_all(stacked, "uly", split_axis=1, concat_axis=0, tiled=True)
    local_qkv = local_qkv.reshape(local_qkv.shape[0], -1, 3, HEAD_DIM)
    local_q, local_k, local_v = (
        local_qkv[:, :, i].reshape(local_qkv.shape[0], -1) for i in range(3)
    )
    block_rows, channels = local_q.shape
    heads_here = channels // HEAD_DIM
    maxlen = block_rows // 2
    rows_q = min(512, block_rows)
    window = rows_q + 2 * maxlen
    conv_half = KERNEL // 2
    block_count = block_rows // rows_q
    score_scale = HEAD_DIM ** (-0.5)
    frame_total = lax.axis_size("blk") * block_rows
    first_frame = lax.axis_index("blk") * block_rows
    seg_ext = segment_ids(
        lengths,
        first_frame - maxlen + jnp.arange(block_rows + 2 * maxlen, dtype=jnp.int32),
        frame_total,
    )
    seg_own = seg_ext[maxlen : maxlen + block_rows]
    seg_conv = seg_ext[maxlen - conv_half : maxlen + block_rows + conv_half]
    near_pairs = extended(jnp.concatenate([local_k, local_v], axis=1), (("blk", 0),), maxlen)
    k_ext = near_pairs[:, :channels].reshape(-1, heads_here, HEAD_DIM)
    v_ext = near_pairs[:, channels:].reshape(-1, heads_here, HEAD_DIM)
    q_heads = local_q.reshape(block_rows, heads_here, HEAD_DIM)
    starts = jnp.arange(block_count, dtype=jnp.int32) * rows_q

    assert heads_here == 1
    lo_t, hi_t = tile_ranges(lengths, first_frame - maxlen, block_rows + 2 * maxlen, block_rows)
    qseg_col = seg_own[:, None].astype(jnp.int32)
    kseg_row = seg_ext[None, :].astype(jnp.int32)
    k_flat = k_ext.reshape(-1, HEAD_DIM)
    v_flat = v_ext.reshape(-1, HEAD_DIM)
    attended, row_tops, row_totals = vmem_call(
        forward_kernel,
        2,
        5,
        (
            jax.ShapeDtypeStruct((block_rows, HEAD_DIM), jnp.bfloat16),
            jax.ShapeDtypeStruct((block_rows, 1), jnp.float32),
            jax.ShapeDtypeStruct((block_rows, 1), jnp.float32),
        ),
    )(lo_t, hi_t, local_q, k_flat, v_flat, qseg_col, kseg_row)
    frame_at = first_frame + jnp.arange(block_rows, dtype=jnp.int32)
    seg_start, seg_end = segment_bounds(lengths, frame_at)
    lo_off = (seg_start - frame_at)[None, :].astype(jnp.int32)
    hi_off = (seg_end - frame_at)[None, :].astype(jnp.int32)
    weight_t = conv_weight.T
    att_t = attended.T
    conv_out_t, grad_conv_t = vmem_call(
        conv_forward_kernel,
        0,
        6,
        (
            jax.ShapeDtypeStruct((HEAD_DIM, block_rows), jnp.bfloat16),
            jax.ShapeDtypeStruct((HEAD_DIM, block_rows), jnp.float32),
        ),
    )(padded_rims(att_t, conv_half), weight_t, norm_gain[:, None], cotangent, lo_off, hi_off)
    grad_att_t, delta_row = vmem_call(
        conv_backward_kernel,
        0,
        5,
        (
            jax.ShapeDtypeStruct((HEAD_DIM, block_rows), jnp.bfloat16),
            jax.ShapeDtypeStruct((1, block_rows), jnp.float32),
        ),
    )(padded_rims(grad_conv_t, conv_half), weight_t, att_t, lo_off, hi_off)
    grad_attended = grad_att_t.T
    row_delta = delta_row.T

    ext_rows = block_rows + 2 * maxlen
    grad_q, dk_t, dv_t = vmem_call(
        backward_kernel,
        2,
        11,
        (
            jax.ShapeDtypeStruct((block_rows, HEAD_DIM), jnp.bfloat16),
            jax.ShapeDtypeStruct((HEAD_DIM, ext_rows), jnp.float32),
            jax.ShapeDtypeStruct((HEAD_DIM, ext_rows), jnp.float32),
        ),
    )(
        lo_t,
        hi_t,
        local_q,
        k_flat,
        v_flat,
        grad_attended,
        local_q.T,
        grad_att_t,
        qseg_col,
        kseg_row,
        row_tops,
        1.0 / row_totals,
        row_delta,
    )
    ext_terms = jnp.concatenate([dk_t, dv_t], axis=0)
    received = []
    for rim_part, direction in ((ext_terms[:, :maxlen], -1), (ext_terms[:, maxlen + block_rows :], 1)):
        received.append(
            passed_along(rim_part.astype(jnp.bfloat16), "blk", direction).astype(rim_part.dtype)
        )
    key_grads = ext_terms[:, maxlen : maxlen + block_rows] + jnp.concatenate(
        [received[1], received[0]], axis=1
    )
    grad_queries = grad_q.reshape(block_rows, channels)
    grad_keys = key_grads[:HEAD_DIM].astype(jnp.bfloat16)
    grad_values = key_grads[HEAD_DIM:].astype(jnp.bfloat16)
    return (conv_out_t, grad_queries.T, grad_keys, grad_values)


def solution(mesh):
    in_specs = (
        P(("blk", "uly"), None),
        P(("blk", "uly"), None),
        P(("blk", "uly"), None),
        P(),
        P(None, "uly"),
        P("uly"),
        P("uly", "blk"),
    )
    out_specs = (P("uly", "blk"), P("uly", "blk"), P("uly", "blk"), P("uly", "blk"))
    return jax.shard_map(
        on_device, mesh=mesh, in_specs=in_specs, out_specs=out_specs, check_vma=False
    )
```

```python
import jax
import jax.numpy as jnp
import functools
from jax import lax
from jax.experimental import pallas as pl
from jax.experimental.pallas import tpu as pltpu
from jax.sharding import PartitionSpec as P

KERNEL = 31
HEAD_DIM = 64


def extended(block, sides, width):
    for axis, dim in sides:
        count = lax.axis_size(axis)
        forward = [(i, i + 1) for i in range(count - 1)]
        backward = [(target, source) for source, target in forward]
        low = lax.ppermute(
            lax.slice_in_dim(block, block.shape[dim] - width, None, axis=dim), axis, forward
        )
        high = lax.ppermute(lax.slice_in_dim(block, 0, width, axis=dim), axis, backward)
        block = jnp.concatenate([low, block, high], axis=dim)
    return block


def passed_along(block, axis, distance):
    devices = range(lax.axis_size(axis))
    route = [(i - distance, i) for i in devices if i - distance in devices]
    return lax.ppermute(block, axis, route)


def segment_ids(lengths, frames, frame_total):
    starts = jnp.cumsum(lengths) - lengths
    seg_ids = jnp.sum((starts[None, :] <= frames[:, None]).astype(jnp.int32), axis=1) - 1
    inside = (frames >= 0) & (frames < frame_total)
    return jnp.where(inside, seg_ids, -1)


def rows_at(values_in, row_start, row_count):
    return lax.dynamic_slice_in_dim(values_in, row_start, row_count, 0)


def masked_scores(query_rows, key_rows, query_seg, key_seg):
    scores = HEAD_DIM ** (-0.5) * jnp.einsum(
        "rhe,she->hrs", query_rows, key_rows, preferred_element_type=jnp.float32
    )
    same_seg = (query_seg[:, None] == key_seg[None, :])[None]
    return (scores, same_seg)


def weights_of(scores, same_seg, row_top, row_total):
    return jnp.where(same_seg, jnp.exp(scores - row_top), 0.0) / row_total


TILE_Q = 256
TILE_K = 256
NT = (((1,), (1,)), ((), ()))
TN = (((0,), (0,)), ((), ()))


def forward_kernel(lo_ref, hi_ref, q_ref, k_ref, v_ref, qseg_ref, kseg_ref, o_ref, m_ref, l_ref):
    scale = HEAD_DIM ** (-0.5)

    def q_body(i, carry):
        r0 = pl.multiple_of(i * TILE_Q, TILE_Q)
        q = q_ref[pl.ds(r0, TILE_Q), :]
        qs = qseg_ref[pl.ds(r0, TILE_Q), :]

        def k_body(j, c):
            m, l, acc = c
            c0 = pl.multiple_of(j * TILE_K, TILE_K)
            k = k_ref[pl.ds(c0, TILE_K), :]
            v = v_ref[pl.ds(c0, TILE_K), :]
            ks = kseg_ref[:, pl.ds(c0, TILE_K)]
            s = scale * lax.dot_general(q, k, NT, preferred_element_type=jnp.float32)
            mask = qs == ks
            m_new = jnp.maximum(m, jnp.max(jnp.where(mask, s, -1e30), axis=1, keepdims=True))
            alpha = jnp.exp(m - m_new)
            p = jnp.where(mask, jnp.exp(s - m_new), 0.0)
            l = alpha * l + jnp.sum(p, axis=1, keepdims=True)
            acc = alpha * acc + jnp.dot(
                p.astype(jnp.bfloat16), v, preferred_element_type=jnp.float32
            )
            return (m_new, l, acc)

        init = (
            jnp.full((TILE_Q, 1), -1e30, jnp.float32),
            jnp.zeros((TILE_Q, 1), jnp.float32),
            jnp.zeros((TILE_Q, HEAD_DIM), jnp.float32),
        )
        m, l, acc = lax.fori_loop(lo_ref[i], hi_ref[i], k_body, init)
        o_ref[pl.ds(r0, TILE_Q), :] = (acc / l).astype(o_ref.dtype)
        m_ref[pl.ds(r0, TILE_Q), :] = m
        l_ref[pl.ds(r0, TILE_Q), :] = l
        return carry

    lax.fori_loop(0, q_ref.shape[0] // TILE_Q, q_body, 0)


def backward_kernel(
    lo_ref, hi_ref, q_ref, k_ref, v_ref, do_ref, qt_ref, dot_ref, qseg_ref, kseg_ref, m_ref,
    il_ref, d_ref, dq_ref, dk_ref, dv_ref,
):
    scale = HEAD_DIM ** (-0.5)
    dk_ref[...] = jnp.zeros_like(dk_ref)
    dv_ref[...] = jnp.zeros_like(dv_ref)

    def q_body(i, carry):
        r0 = pl.multiple_of(i * TILE_Q, TILE_Q)
        q = q_ref[pl.ds(r0, TILE_Q), :]
        do = do_ref[pl.ds(r0, TILE_Q), :]
        qs = qseg_ref[pl.ds(r0, TILE_Q), :]
        m = m_ref[pl.ds(r0, TILE_Q), :]
        il = il_ref[pl.ds(r0, TILE_Q), :]
        dlt = d_ref[pl.ds(r0, TILE_Q), :]
        q_t = qt_ref[:, pl.ds(r0, TILE_Q)]
        do_t = dot_ref[:, pl.ds(r0, TILE_Q)]

        def k_body(j, dq):
            c0 = pl.multiple_of(j * TILE_K, TILE_K)
            k = k_ref[pl.ds(c0, TILE_K), :]
            v = v_ref[pl.ds(c0, TILE_K), :]
            ks = kseg_ref[:, pl.ds(c0, TILE_K)]
            s = scale * lax.dot_general(q, k, NT, preferred_element_type=jnp.float32)
            mask = qs == ks
            p = jnp.where(mask, jnp.exp(s - m) * il, 0.0)
            dp = lax.dot_general(do, v, NT, preferred_element_type=jnp.float32)
            ds = (p * (dp - dlt)).astype(jnp.bfloat16)
            dk_ref[:, pl.ds(c0, TILE_K)] += jnp.dot(q_t, ds, preferred_element_type=jnp.float32)
            dv_ref[:, pl.ds(c0, TILE_K)] += jnp.dot(
                do_t, p.astype(jnp.bfloat16), preferred_element_type=jnp.float32
            )
            return dq + jnp.dot(ds, k, preferred_element_type=jnp.float32)

        dq = lax.fori_loop(
            lo_ref[i], hi_ref[i], k_body, jnp.zeros((TILE_Q, HEAD_DIM), jnp.float32)
        )
        dq_ref[pl.ds(r0, TILE_Q), :] = (scale * dq).astype(dq_ref.dtype)
        return carry

    lax.fori_loop(0, q_ref.shape[0] // TILE_Q, q_body, 0)
    dk_ref[...] = scale * dk_ref[...]


def vmem_call(kernel, n_smem, n_vmem, out_shape):
    return pl.pallas_call(
        kernel,
        out_shape=out_shape,
        in_specs=[pl.BlockSpec(memory_space=pltpu.SMEM)] * n_smem
        + [pl.BlockSpec(memory_space=pltpu.VMEM)] * n_vmem,
        out_specs=[pl.BlockSpec(memory_space=pltpu.VMEM)] * len(out_shape),
    )


def segment_bounds(lengths, frames):
    ends = jnp.cumsum(lengths)
    starts = ends - lengths
    seg_start = jnp.max(jnp.where(starts[None, :] <= frames[:, None], starts[None, :], 0), axis=1)
    big = jnp.iinfo(jnp.int32).max
    seg_end = jnp.min(jnp.where(ends[None, :] > frames[:, None], ends[None, :], big), axis=1)
    return (seg_start, jnp.minimum(seg_end, ends[-1]))


def tile_ranges(lengths, base, ext_rows, block_rows):
    frames = base + (ext_rows - block_rows) // 2 + jnp.arange(block_rows, dtype=jnp.int32)
    seg_start, seg_end = segment_bounds(lengths, frames)
    lo = (seg_start[::TILE_Q] - base) // TILE_K
    hi = (seg_end[TILE_Q - 1 :: TILE_Q] - base + TILE_K - 1) // TILE_K
    lo = jnp.clip(lo, 0, ext_rows // TILE_K).astype(jnp.int32)
    hi = jnp.clip(hi, lo, ext_rows // TILE_K).astype(jnp.int32)
    return (lo, hi)


CONV_PAD = 128
CONV_CHUNK = 256


def conv_chunk(x_ref, wt_ref, lo, hi, c0, sign):
    window = x_ref[:, pl.ds(c0, CONV_CHUNK + 2 * CONV_PAD)]
    width = window.shape[1]
    total = jnp.zeros((window.shape[0], CONV_CHUNK), jnp.float32)
    for tap in range(KERNEL):
        d = sign * (tap - KERNEL // 2)
        shifted = pltpu.roll(window, (width - d) % width, 1) if d else window
        keep = (lo <= d) & (d < hi)
        total = total + wt_ref[:, tap : tap + 1] * jnp.where(
            keep, shifted[:, CONV_PAD : CONV_PAD + CONV_CHUNK], 0.0
        )
    return total


def conv_forward_kernel(x_ref, wt_ref, gain_ref, cot_ref, lo_ref, hi_ref, out_ref, gc_ref):
    gain = gain_ref[...]

    def body(c, carry):
        c0 = pl.multiple_of(c * CONV_CHUNK, CONV_CHUNK)
        cols = pl.ds(c0, CONV_CHUNK)
        conv_sum = conv_chunk(x_ref, wt_ref, lo_ref[:, cols], hi_ref[:, cols], c0, 1)
        spread = jnp.sqrt(jnp.mean(conv_sum * conv_sum, axis=0, keepdims=True) + 1e-05)
        normed = conv_sum / spread
        pre_act = normed * gain
        gate = 1.0 / (1.0 + jnp.exp(-pre_act))
        out_ref[:, cols] = (pre_act * gate).astype(out_ref.dtype)
        grad_pre = cot_ref[:, cols].astype(jnp.float32) * gate * (1.0 + pre_act * (1.0 - gate))
        weighted = grad_pre * gain
        gc_ref[:, cols] = (
            weighted - normed * jnp.mean(weighted * normed, axis=0, keepdims=True)
        ) / spread
        return carry

    lax.fori_loop(0, out_ref.shape[1] // CONV_CHUNK, body, 0)


def conv_backward_kernel(y_ref, wt_ref, att_ref, lo_ref, hi_ref, ga_ref, delta_ref):
    def body(c, carry):
        c0 = pl.multiple_of(c * CONV_CHUNK, CONV_CHUNK)
        cols = pl.ds(c0, CONV_CHUNK)
        grad_sum = conv_chunk(y_ref, wt_ref, lo_ref[:, cols], hi_ref[:, cols], c0, -1)
        grad_att = grad_sum.astype(ga_ref.dtype)
        ga_ref[:, cols] = grad_att
        delta_ref[:, cols] = jnp.sum(
            grad_att.astype(jnp.float32) * att_ref[:, cols].astype(jnp.float32),
            axis=0,
            keepdims=True,
        )
        return carry

    lax.fori_loop(0, ga_ref.shape[1] // CONV_CHUNK, body, 0)


def padded_rims(block, half):
    count = lax.axis_size("blk")
    forward = [(i, i + 1) for i in range(count - 1)]
    backward = [(target, source) for source, target in forward]
    low = lax.ppermute(block[:, block.shape[1] - half :], "blk", forward)
    high = lax.ppermute(block[:, :half], "blk", backward)
    gap = jnp.zeros((block.shape[0], CONV_PAD - half), jnp.float32)
    return jnp.concatenate(
        [gap, low.astype(jnp.float32), block.astype(jnp.float32), high.astype(jnp.float32), gap],
        axis=1,
    )


def on_device(queries, keys, values, lengths, conv_weight, norm_gain, cotangent):
    rows_in, width = queries.shape
    heads_total = width // HEAD_DIM
    stacked = jnp.stack(
        [a.reshape(rows_in, heads_total, HEAD_DIM) for a in (queries, keys, values)], axis=2
    )
    stacked = jnp.transpose(stacked, (1, 0, 2, 3)).reshape(heads_total, rows_in * 3 * HEAD_DIM)
    local_qkv = lax.all_to_all(stacked, "uly", split_axis=0, concat_axis=0, tiled=True)
    local_qkv = local_qkv.reshape(-1, heads_total // lax.axis_size("uly"), 3, HEAD_DIM)
    local_q, local_k, local_v = (
        local_qkv[:, :, i].reshape(local_qkv.shape[0], -1) for i in range(3)
    )
    block_rows, channels = local_q.shape
    heads_here = channels // HEAD_DIM
    maxlen = block_rows // 2
    rows_q = min(512, block_rows)
    window = rows_q + 2 * maxlen
    conv_half = KERNEL // 2
    block_count = block_rows // rows_q
    score_scale = HEAD_DIM ** (-0.5)
    frame_total = lax.axis_size("blk") * block_rows
    first_frame = lax.axis_index("blk") * block_rows
    seg_ext = segment_ids(
        lengths,
        first_frame - maxlen + jnp.arange(block_rows + 2 * maxlen, dtype=jnp.int32),
        frame_total,
    )
    seg_own = seg_ext[maxlen : maxlen + block_rows]
    seg_conv = seg_ext[maxlen - conv_half : maxlen + block_rows + conv_half]
    near_pairs = extended(jnp.concatenate([local_k, local_v], axis=1), (("blk", 0),), maxlen)
    k_ext = near_pairs[:, :channels].reshape(-1, heads_here, HEAD_DIM)
    v_ext = near_pairs[:, channels:].reshape(-1, heads_here, HEAD_DIM)
    q_heads = local_q.reshape(block_rows, heads_here, HEAD_DIM)
    starts = jnp.arange(block_count, dtype=jnp.int32) * rows_q

    assert heads_here == 1
    lo_t, hi_t = tile_ranges(lengths, first_frame - maxlen, block_rows + 2 * maxlen, block_rows)
    qseg_col = seg_own[:, None].astype(jnp.int32)
    kseg_row = seg_ext[None, :].astype(jnp.int32)
    k_flat = k_ext.reshape(-1, HEAD_DIM)
    v_flat = v_ext.reshape(-1, HEAD_DIM)
    attended, row_tops, row_totals = vmem_call(
        forward_kernel,
        2,
        5,
        (
            jax.ShapeDtypeStruct((block_rows, HEAD_DIM), jnp.bfloat16),
            jax.ShapeDtypeStruct((block_rows, 1), jnp.float32),
            jax.ShapeDtypeStruct((block_rows, 1), jnp.float32),
        ),
    )(lo_t, hi_t, local_q, k_flat, v_flat, qseg_col, kseg_row)
    frame_at = first_frame + jnp.arange(block_rows, dtype=jnp.int32)
    seg_start, seg_end = segment_bounds(lengths, frame_at)
    lo_off = (seg_start - frame_at)[None, :].astype(jnp.int32)
    hi_off = (seg_end - frame_at)[None, :].astype(jnp.int32)
    weight_t = conv_weight.T
    att_t = attended.T
    conv_out_t, grad_conv_t = vmem_call(
        conv_forward_kernel,
        0,
        6,
        (
            jax.ShapeDtypeStruct((HEAD_DIM, block_rows), jnp.bfloat16),
            jax.ShapeDtypeStruct((HEAD_DIM, block_rows), jnp.float32),
        ),
    )(padded_rims(att_t, conv_half), weight_t, norm_gain[:, None], cotangent, lo_off, hi_off)
    grad_att_t, delta_row = vmem_call(
        conv_backward_kernel,
        0,
        5,
        (
            jax.ShapeDtypeStruct((HEAD_DIM, block_rows), jnp.bfloat16),
            jax.ShapeDtypeStruct((1, block_rows), jnp.float32),
        ),
    )(padded_rims(grad_conv_t, conv_half), weight_t, att_t, lo_off, hi_off)
    grad_attended = grad_att_t.T
    row_delta = delta_row.T

    ext_rows = block_rows + 2 * maxlen
    grad_q, dk_t, dv_t = vmem_call(
        backward_kernel,
        2,
        11,
        (
            jax.ShapeDtypeStruct((block_rows, HEAD_DIM), jnp.bfloat16),
            jax.ShapeDtypeStruct((HEAD_DIM, ext_rows), jnp.float32),
            jax.ShapeDtypeStruct((HEAD_DIM, ext_rows), jnp.float32),
        ),
    )(
        lo_t,
        hi_t,
        local_q,
        k_flat,
        v_flat,
        grad_attended,
        local_q.T,
        grad_att_t,
        qseg_col,
        kseg_row,
        row_tops,
        1.0 / row_totals,
        row_delta,
    )
    ext_terms = jnp.concatenate([dk_t, dv_t], axis=0)
    received = []
    for rim_part, direction in ((ext_terms[:, :maxlen], -1), (ext_terms[:, maxlen + block_rows :], 1)):
        received.append(
            passed_along(rim_part.astype(jnp.bfloat16), "blk", direction).astype(rim_part.dtype)
        )
    key_grads = ext_terms[:, maxlen : maxlen + block_rows] + jnp.concatenate(
        [received[1], received[0]], axis=1
    )
    grad_queries = grad_q.reshape(block_rows, channels)
    grad_keys = key_grads[:HEAD_DIM].astype(jnp.bfloat16)
    grad_values = key_grads[HEAD_DIM:].astype(jnp.bfloat16)
    return (conv_out_t, grad_queries.T, grad_keys, grad_values)


def solution(mesh):
    in_specs = (
        P(("blk", "uly"), None),
        P(("blk", "uly"), None),
        P(("blk", "uly"), None),
        P(),
        P(None, "uly"),
        P("uly"),
        P("uly", "blk"),
    )
    out_specs = (P("uly", "blk"), P("uly", "blk"), P("uly", "blk"), P("uly", "blk"))
    return jax.shard_map(
        on_device, mesh=mesh, in_specs=in_specs, out_specs=out_specs, check_vma=False
    )
```

```python
import jax
import jax.numpy as jnp
import functools
from jax import lax
from jax.experimental import pallas as pl
from jax.experimental.pallas import tpu as pltpu
from jax.sharding import PartitionSpec as P

KERNEL = 31
HEAD_DIM = 64


def extended(block, sides, width):
    for axis, dim in sides:
        count = lax.axis_size(axis)
        forward = [(i, i + 1) for i in range(count - 1)]
        backward = [(target, source) for source, target in forward]
        low = lax.ppermute(
            lax.slice_in_dim(block, block.shape[dim] - width, None, axis=dim), axis, forward
        )
        high = lax.ppermute(lax.slice_in_dim(block, 0, width, axis=dim), axis, backward)
        block = jnp.concatenate([low, block, high], axis=dim)
    return block


def passed_along(block, axis, distance):
    devices = range(lax.axis_size(axis))
    route = [(i - distance, i) for i in devices if i - distance in devices]
    return lax.ppermute(block, axis, route)


def segment_ids(lengths, frames, frame_total):
    starts = jnp.cumsum(lengths) - lengths
    seg_ids = jnp.sum((starts[None, :] <= frames[:, None]).astype(jnp.int32), axis=1) - 1
    inside = (frames >= 0) & (frames < frame_total)
    return jnp.where(inside, seg_ids, -1)


def rows_at(values_in, row_start, row_count):
    return lax.dynamic_slice_in_dim(values_in, row_start, row_count, 0)


def masked_scores(query_rows, key_rows, query_seg, key_seg):
    scores = HEAD_DIM ** (-0.5) * jnp.einsum(
        "rhe,she->hrs", query_rows, key_rows, preferred_element_type=jnp.float32
    )
    same_seg = (query_seg[:, None] == key_seg[None, :])[None]
    return (scores, same_seg)


def weights_of(scores, same_seg, row_top, row_total):
    return jnp.where(same_seg, jnp.exp(scores - row_top), 0.0) / row_total


TILE_Q = 256
TILE_K = 512
NT = (((1,), (1,)), ((), ()))
TN = (((0,), (0,)), ((), ()))


def forward_kernel(lo_ref, hi_ref, q_ref, k_ref, v_ref, qseg_ref, kseg_ref, o_ref, m_ref, l_ref):
    scale = HEAD_DIM ** (-0.5)

    def q_body(i, carry):
        r0 = pl.multiple_of(i * TILE_Q, TILE_Q)
        q = q_ref[pl.ds(r0, TILE_Q), :]
        qs = qseg_ref[pl.ds(r0, TILE_Q), :]

        def k_body(j, c):
            m, l, acc = c
            c0 = pl.multiple_of(j * TILE_K, TILE_K)
            k = k_ref[pl.ds(c0, TILE_K), :]
            v = v_ref[pl.ds(c0, TILE_K), :]
            ks = kseg_ref[:, pl.ds(c0, TILE_K)]
            s = scale * lax.dot_general(q, k, NT, preferred_element_type=jnp.float32)
            mask = qs == ks
            m_new = jnp.maximum(m, jnp.max(jnp.where(mask, s, -1e30), axis=1, keepdims=True))
            alpha = jnp.exp(m - m_new)
            p = jnp.where(mask, jnp.exp(s - m_new), 0.0)
            l = alpha * l + jnp.sum(p, axis=1, keepdims=True)
            acc = alpha * acc + jnp.dot(
                p.astype(jnp.bfloat16), v, preferred_element_type=jnp.float32
            )
            return (m_new, l, acc)

        init = (
            jnp.full((TILE_Q, 1), -1e30, jnp.float32),
            jnp.zeros((TILE_Q, 1), jnp.float32),
            jnp.zeros((TILE_Q, HEAD_DIM), jnp.float32),
        )
        m, l, acc = lax.fori_loop(lo_ref[i], hi_ref[i], k_body, init)
        o_ref[pl.ds(r0, TILE_Q), :] = (acc / l).astype(o_ref.dtype)
        m_ref[pl.ds(r0, TILE_Q), :] = m
        l_ref[pl.ds(r0, TILE_Q), :] = l
        return carry

    lax.fori_loop(0, q_ref.shape[0] // TILE_Q, q_body, 0)


def backward_kernel(
    lo_ref, hi_ref, q_ref, k_ref, v_ref, do_ref, qt_ref, dot_ref, qseg_ref, kseg_ref, m_ref,
    il_ref, d_ref, dq_ref, dk_ref, dv_ref,
):
    scale = HEAD_DIM ** (-0.5)
    dk_ref[...] = jnp.zeros_like(dk_ref)
    dv_ref[...] = jnp.zeros_like(dv_ref)

    def q_body(i, carry):
        r0 = pl.multiple_of(i * TILE_Q, TILE_Q)
        q = q_ref[pl.ds(r0, TILE_Q), :]
        do = do_ref[pl.ds(r0, TILE_Q), :]
        qs = qseg_ref[pl.ds(r0, TILE_Q), :]
        m = m_ref[pl.ds(r0, TILE_Q), :]
        il = il_ref[pl.ds(r0, TILE_Q), :]
        dlt = d_ref[pl.ds(r0, TILE_Q), :]
        q_t = qt_ref[:, pl.ds(r0, TILE_Q)]
        do_t = dot_ref[:, pl.ds(r0, TILE_Q)]

        def k_body(j, dq):
            c0 = pl.multiple_of(j * TILE_K, TILE_K)
            k = k_ref[pl.ds(c0, TILE_K), :]
            v = v_ref[pl.ds(c0, TILE_K), :]
            ks = kseg_ref[:, pl.ds(c0, TILE_K)]
            s = scale * lax.dot_general(q, k, NT, preferred_element_type=jnp.float32)
            mask = qs == ks
            p = jnp.where(mask, jnp.exp(s - m) * il, 0.0)
            dp = lax.dot_general(do, v, NT, preferred_element_type=jnp.float32)
            ds = (p * (dp - dlt)).astype(jnp.bfloat16)
            dk_ref[:, pl.ds(c0, TILE_K)] += jnp.dot(q_t, ds, preferred_element_type=jnp.float32)
            dv_ref[:, pl.ds(c0, TILE_K)] += jnp.dot(
                do_t, p.astype(jnp.bfloat16), preferred_element_type=jnp.float32
            )
            return dq + jnp.dot(ds, k, preferred_element_type=jnp.float32)

        dq = lax.fori_loop(
            lo_ref[i], hi_ref[i], k_body, jnp.zeros((TILE_Q, HEAD_DIM), jnp.float32)
        )
        dq_ref[pl.ds(r0, TILE_Q), :] = (scale * dq).astype(dq_ref.dtype)
        return carry

    lax.fori_loop(0, q_ref.shape[0] // TILE_Q, q_body, 0)
    dk_ref[...] = scale * dk_ref[...]


def vmem_call(kernel, n_smem, n_vmem, out_shape):
    return pl.pallas_call(
        kernel,
        out_shape=out_shape,
        in_specs=[pl.BlockSpec(memory_space=pltpu.SMEM)] * n_smem
        + [pl.BlockSpec(memory_space=pltpu.VMEM)] * n_vmem,
        out_specs=[pl.BlockSpec(memory_space=pltpu.VMEM)] * len(out_shape),
    )


def segment_bounds(lengths, frames):
    ends = jnp.cumsum(lengths)
    starts = ends - lengths
    seg_start = jnp.max(jnp.where(starts[None, :] <= frames[:, None], starts[None, :], 0), axis=1)
    big = jnp.iinfo(jnp.int32).max
    seg_end = jnp.min(jnp.where(ends[None, :] > frames[:, None], ends[None, :], big), axis=1)
    return (seg_start, jnp.minimum(seg_end, ends[-1]))


def tile_ranges(lengths, base, ext_rows, block_rows):
    frames = base + (ext_rows - block_rows) // 2 + jnp.arange(block_rows, dtype=jnp.int32)
    seg_start, seg_end = segment_bounds(lengths, frames)
    lo = (seg_start[::TILE_Q] - base) // TILE_K
    hi = (seg_end[TILE_Q - 1 :: TILE_Q] - base + TILE_K - 1) // TILE_K
    lo = jnp.clip(lo, 0, ext_rows // TILE_K).astype(jnp.int32)
    hi = jnp.clip(hi, lo, ext_rows // TILE_K).astype(jnp.int32)
    return (lo, hi)


CONV_PAD = 128
CONV_CHUNK = 256


def conv_chunk(x_ref, wt_ref, lo, hi, c0, sign):
    window = x_ref[:, pl.ds(c0, CONV_CHUNK + 2 * CONV_PAD)]
    width = window.shape[1]
    total = jnp.zeros((window.shape[0], CONV_CHUNK), jnp.float32)
    for tap in range(KERNEL):
        d = sign * (tap - KERNEL // 2)
        shifted = pltpu.roll(window, (width - d) % width, 1) if d else window
        keep = (lo <= d) & (d < hi)
        total = total + wt_ref[:, tap : tap + 1] * jnp.where(
            keep, shifted[:, CONV_PAD : CONV_PAD + CONV_CHUNK], 0.0
        )
    return total


def conv_forward_kernel(x_ref, wt_ref, gain_ref, cot_ref, lo_ref, hi_ref, out_ref, gc_ref):
    gain = gain_ref[...]

    def body(c, carry):
        c0 = pl.multiple_of(c * CONV_CHUNK, CONV_CHUNK)
        cols = pl.ds(c0, CONV_CHUNK)
        conv_sum = conv_chunk(x_ref, wt_ref, lo_ref[:, cols], hi_ref[:, cols], c0, 1)
        spread = jnp.sqrt(jnp.mean(conv_sum * conv_sum, axis=0, keepdims=True) + 1e-05)
        normed = conv_sum / spread
        pre_act = normed * gain
        gate = 1.0 / (1.0 + jnp.exp(-pre_act))
        out_ref[:, cols] = (pre_act * gate).astype(out_ref.dtype)
        grad_pre = cot_ref[:, cols].astype(jnp.float32) * gate * (1.0 + pre_act * (1.0 - gate))
        weighted = grad_pre * gain
        gc_ref[:, cols] = (
            weighted - normed * jnp.mean(weighted * normed, axis=0, keepdims=True)
        ) / spread
        return carry

    lax.fori_loop(0, out_ref.shape[1] // CONV_CHUNK, body, 0)


def conv_backward_kernel(y_ref, wt_ref, att_ref, lo_ref, hi_ref, ga_ref, delta_ref):
    def body(c, carry):
        c0 = pl.multiple_of(c * CONV_CHUNK, CONV_CHUNK)
        cols = pl.ds(c0, CONV_CHUNK)
        grad_sum = conv_chunk(y_ref, wt_ref, lo_ref[:, cols], hi_ref[:, cols], c0, -1)
        grad_att = grad_sum.astype(ga_ref.dtype)
        ga_ref[:, cols] = grad_att
        delta_ref[:, cols] = jnp.sum(
            grad_att.astype(jnp.float32) * att_ref[:, cols].astype(jnp.float32),
            axis=0,
            keepdims=True,
        )
        return carry

    lax.fori_loop(0, ga_ref.shape[1] // CONV_CHUNK, body, 0)


def padded_rims(block, half):
    count = lax.axis_size("blk")
    forward = [(i, i + 1) for i in range(count - 1)]
    backward = [(target, source) for source, target in forward]
    low = lax.ppermute(block[:, block.shape[1] - half :], "blk", forward)
    high = lax.ppermute(block[:, :half], "blk", backward)
    gap = jnp.zeros((block.shape[0], CONV_PAD - half), jnp.float32)
    return jnp.concatenate(
        [gap, low.astype(jnp.float32), block.astype(jnp.float32), high.astype(jnp.float32), gap],
        axis=1,
    )


def on_device(queries, keys, values, lengths, conv_weight, norm_gain, cotangent):
    rows_in, width = queries.shape
    heads_total = width // HEAD_DIM
    stacked = jnp.stack(
        [a.reshape(rows_in, heads_total, HEAD_DIM) for a in (queries, keys, values)], axis=2
    ).reshape(rows_in, heads_total * 3 * HEAD_DIM)
    local_qkv = lax.all_to_all(stacked, "uly", split_axis=1, concat_axis=0, tiled=True)
    local_qkv = local_qkv.reshape(local_qkv.shape[0], -1, 3, HEAD_DIM)
    local_q, local_k, local_v = (
        local_qkv[:, :, i].reshape(local_qkv.shape[0], -1) for i in range(3)
    )
    block_rows, channels = local_q.shape
    heads_here = channels // HEAD_DIM
    maxlen = block_rows // 2
    rows_q = min(512, block_rows)
    window = rows_q + 2 * maxlen
    conv_half = KERNEL // 2
    block_count = block_rows // rows_q
    score_scale = HEAD_DIM ** (-0.5)
    frame_total = lax.axis_size("blk") * block_rows
    first_frame = lax.axis_index("blk") * block_rows
    seg_ext = segment_ids(
        lengths,
        first_frame - maxlen + jnp.arange(block_rows + 2 * maxlen, dtype=jnp.int32),
        frame_total,
    )
    seg_own = seg_ext[maxlen : maxlen + block_rows]
    seg_conv = seg_ext[maxlen - conv_half : maxlen + block_rows + conv_half]
    near_pairs = extended(jnp.concatenate([local_k, local_v], axis=1), (("blk", 0),), maxlen)
    k_ext = near_pairs[:, :channels].reshape(-1, heads_here, HEAD_DIM)
    v_ext = near_pairs[:, channels:].reshape(-1, heads_here, HEAD_DIM)
    q_heads = local_q.reshape(block_rows, heads_here, HEAD_DIM)
    starts = jnp.arange(block_count, dtype=jnp.int32) * rows_q

    assert heads_here == 1
    lo_t, hi_t = tile_ranges(lengths, first_frame - maxlen, block_rows + 2 * maxlen, block_rows)
    qseg_col = seg_own[:, None].astype(jnp.int32)
    kseg_row = seg_ext[None, :].astype(jnp.int32)
    k_flat = k_ext.reshape(-1, HEAD_DIM)
    v_flat = v_ext.reshape(-1, HEAD_DIM)
    attended, row_tops, row_totals = vmem_call(
        forward_kernel,
        2,
        5,
        (
            jax.ShapeDtypeStruct((block_rows, HEAD_DIM), jnp.bfloat16),
            jax.ShapeDtypeStruct((block_rows, 1), jnp.float32),
            jax.ShapeDtypeStruct((block_rows, 1), jnp.float32),
        ),
    )(lo_t, hi_t, local_q, k_flat, v_flat, qseg_col, kseg_row)
    frame_at = first_frame + jnp.arange(block_rows, dtype=jnp.int32)
    seg_start, seg_end = segment_bounds(lengths, frame_at)
    lo_off = (seg_start - frame_at)[None, :].astype(jnp.int32)
    hi_off = (seg_end - frame_at)[None, :].astype(jnp.int32)
    weight_t = conv_weight.T
    att_t = attended.T
    conv_out_t, grad_conv_t = vmem_call(
        conv_forward_kernel,
        0,
        6,
        (
            jax.ShapeDtypeStruct((HEAD_DIM, block_rows), jnp.bfloat16),
            jax.ShapeDtypeStruct((HEAD_DIM, block_rows), jnp.float32),
        ),
    )(padded_rims(att_t, conv_half), weight_t, norm_gain[:, None], cotangent, lo_off, hi_off)
    grad_att_t, delta_row = vmem_call(
        conv_backward_kernel,
        0,
        5,
        (
            jax.ShapeDtypeStruct((HEAD_DIM, block_rows), jnp.bfloat16),
            jax.ShapeDtypeStruct((1, block_rows), jnp.float32),
        ),
    )(padded_rims(grad_conv_t, conv_half), weight_t, att_t, lo_off, hi_off)
    grad_attended = grad_att_t.T
    row_delta = delta_row.T

    ext_rows = block_rows + 2 * maxlen
    grad_q, dk_t, dv_t = vmem_call(
        backward_kernel,
        2,
        11,
        (
            jax.ShapeDtypeStruct((block_rows, HEAD_DIM), jnp.bfloat16),
            jax.ShapeDtypeStruct((HEAD_DIM, ext_rows), jnp.float32),
            jax.ShapeDtypeStruct((HEAD_DIM, ext_rows), jnp.float32),
        ),
    )(
        lo_t,
        hi_t,
        local_q,
        k_flat,
        v_flat,
        grad_attended,
        local_q.T,
        grad_att_t,
        qseg_col,
        kseg_row,
        row_tops,
        1.0 / row_totals,
        row_delta,
    )
    ext_terms = jnp.concatenate([dk_t, dv_t], axis=0)
    received = []
    for rim_part, direction in ((ext_terms[:, :maxlen], -1), (ext_terms[:, maxlen + block_rows :], 1)):
        received.append(
            passed_along(rim_part.astype(jnp.bfloat16), "blk", direction).astype(rim_part.dtype)
        )
    key_grads = ext_terms[:, maxlen : maxlen + block_rows] + jnp.concatenate(
        [received[1], received[0]], axis=1
    )
    grad_queries = grad_q.reshape(block_rows, channels)
    grad_keys = key_grads[:HEAD_DIM].astype(jnp.bfloat16)
    grad_values = key_grads[HEAD_DIM:].astype(jnp.bfloat16)
    return (conv_out_t, grad_queries.T, grad_keys, grad_values)


def solution(mesh):
    in_specs = (
        P(("blk", "uly"), None),
        P(("blk", "uly"), None),
        P(("blk", "uly"), None),
        P(),
        P(None, "uly"),
        P("uly"),
        P("uly", "blk"),
    )
    out_specs = (P("uly", "blk"), P("uly", "blk"), P("uly", "blk"), P("uly", "blk"))
    return jax.shard_map(
        on_device, mesh=mesh, in_specs=in_specs, out_specs=out_specs, check_vma=False
    )
```

```python
import jax
import jax.numpy as jnp
import functools
from jax import lax
from jax.experimental import pallas as pl
from jax.experimental.pallas import tpu as pltpu
from jax.sharding import PartitionSpec as P

KERNEL = 31
HEAD_DIM = 64


def extended(block, sides, width):
    for axis, dim in sides:
        count = lax.axis_size(axis)
        forward = [(i, i + 1) for i in range(count - 1)]
        backward = [(target, source) for source, target in forward]
        low = lax.ppermute(
            lax.slice_in_dim(block, block.shape[dim] - width, None, axis=dim), axis, forward
        )
        high = lax.ppermute(lax.slice_in_dim(block, 0, width, axis=dim), axis, backward)
        block = jnp.concatenate([low, block, high], axis=dim)
    return block


def passed_along(block, axis, distance):
    devices = range(lax.axis_size(axis))
    route = [(i - distance, i) for i in devices if i - distance in devices]
    return lax.ppermute(block, axis, route)


def segment_ids(lengths, frames, frame_total):
    starts = jnp.cumsum(lengths) - lengths
    seg_ids = jnp.sum((starts[None, :] <= frames[:, None]).astype(jnp.int32), axis=1) - 1
    inside = (frames >= 0) & (frames < frame_total)
    return jnp.where(inside, seg_ids, -1)


def rows_at(values_in, row_start, row_count):
    return lax.dynamic_slice_in_dim(values_in, row_start, row_count, 0)


def masked_scores(query_rows, key_rows, query_seg, key_seg):
    scores = HEAD_DIM ** (-0.5) * jnp.einsum(
        "rhe,she->hrs", query_rows, key_rows, preferred_element_type=jnp.float32
    )
    same_seg = (query_seg[:, None] == key_seg[None, :])[None]
    return (scores, same_seg)


def weights_of(scores, same_seg, row_top, row_total):
    return jnp.where(same_seg, jnp.exp(scores - row_top), 0.0) / row_total


TILE_Q = 512
TILE_K = 512
NT = (((1,), (1,)), ((), ()))
TN = (((0,), (0,)), ((), ()))


def forward_kernel(lo_ref, hi_ref, q_ref, k_ref, v_ref, qseg_ref, kseg_ref, o_ref, m_ref, l_ref):
    scale = HEAD_DIM ** (-0.5)

    def q_body(i, carry):
        r0 = pl.multiple_of(i * TILE_Q, TILE_Q)
        q = q_ref[pl.ds(r0, TILE_Q), :]
        qs = qseg_ref[pl.ds(r0, TILE_Q), :]

        def k_body(j, c):
            m, l, acc = c
            c0 = pl.multiple_of(j * TILE_K, TILE_K)
            k = k_ref[pl.ds(c0, TILE_K), :]
            v = v_ref[pl.ds(c0, TILE_K), :]
            ks = kseg_ref[:, pl.ds(c0, TILE_K)]
            s = scale * lax.dot_general(q, k, NT, preferred_element_type=jnp.float32)
            mask = qs == ks
            m_new = jnp.maximum(m, jnp.max(jnp.where(mask, s, -1e30), axis=1, keepdims=True))
            alpha = jnp.exp(m - m_new)
            p = jnp.where(mask, jnp.exp(s - m_new), 0.0)
            l = alpha * l + jnp.sum(p, axis=1, keepdims=True)
            acc = alpha * acc + jnp.dot(
                p.astype(jnp.bfloat16), v, preferred_element_type=jnp.float32
            )
            return (m_new, l, acc)

        init = (
            jnp.full((TILE_Q, 1), -1e30, jnp.float32),
            jnp.zeros((TILE_Q, 1), jnp.float32),
            jnp.zeros((TILE_Q, HEAD_DIM), jnp.float32),
        )
        m, l, acc = lax.fori_loop(lo_ref[i], hi_ref[i], k_body, init)
        o_ref[pl.ds(r0, TILE_Q), :] = (acc / l).astype(o_ref.dtype)
        m_ref[pl.ds(r0, TILE_Q), :] = m
        l_ref[pl.ds(r0, TILE_Q), :] = l
        return carry

    lax.fori_loop(0, q_ref.shape[0] // TILE_Q, q_body, 0)


def backward_kernel(
    lo_ref, hi_ref, q_ref, k_ref, v_ref, do_ref, qt_ref, dot_ref, qseg_ref, kseg_ref, m_ref,
    il_ref, d_ref, dq_ref, dk_ref, dv_ref,
):
    scale = HEAD_DIM ** (-0.5)
    dk_ref[...] = jnp.zeros_like(dk_ref)
    dv_ref[...] = jnp.zeros_like(dv_ref)

    def q_body(i, carry):
        r0 = pl.multiple_of(i * TILE_Q, TILE_Q)
        q = q_ref[pl.ds(r0, TILE_Q), :]
        do = do_ref[pl.ds(r0, TILE_Q), :]
        qs = qseg_ref[pl.ds(r0, TILE_Q), :]
        m = m_ref[pl.ds(r0, TILE_Q), :]
        il = il_ref[pl.ds(r0, TILE_Q), :]
        dlt = d_ref[pl.ds(r0, TILE_Q), :]
        q_t = qt_ref[:, pl.ds(r0, TILE_Q)]
        do_t = dot_ref[:, pl.ds(r0, TILE_Q)]

        def k_body(j, dq):
            c0 = pl.multiple_of(j * TILE_K, TILE_K)
            k = k_ref[pl.ds(c0, TILE_K), :]
            v = v_ref[pl.ds(c0, TILE_K), :]
            ks = kseg_ref[:, pl.ds(c0, TILE_K)]
            s = scale * lax.dot_general(q, k, NT, preferred_element_type=jnp.float32)
            mask = qs == ks
            p = jnp.where(mask, jnp.exp(s - m) * il, 0.0)
            dp = lax.dot_general(do, v, NT, preferred_element_type=jnp.float32)
            ds = (p * (dp - dlt)).astype(jnp.bfloat16)
            dk_ref[:, pl.ds(c0, TILE_K)] += jnp.dot(q_t, ds, preferred_element_type=jnp.float32)
            dv_ref[:, pl.ds(c0, TILE_K)] += jnp.dot(
                do_t, p.astype(jnp.bfloat16), preferred_element_type=jnp.float32
            )
            return dq + jnp.dot(ds, k, preferred_element_type=jnp.float32)

        dq = lax.fori_loop(
            lo_ref[i], hi_ref[i], k_body, jnp.zeros((TILE_Q, HEAD_DIM), jnp.float32)
        )
        dq_ref[pl.ds(r0, TILE_Q), :] = (scale * dq).astype(dq_ref.dtype)
        return carry

    lax.fori_loop(0, q_ref.shape[0] // TILE_Q, q_body, 0)
    dk_ref[...] = scale * dk_ref[...]


def vmem_call(kernel, n_smem, n_vmem, out_shape):
    return pl.pallas_call(
        kernel,
        out_shape=out_shape,
        in_specs=[pl.BlockSpec(memory_space=pltpu.SMEM)] * n_smem
        + [pl.BlockSpec(memory_space=pltpu.VMEM)] * n_vmem,
        out_specs=[pl.BlockSpec(memory_space=pltpu.VMEM)] * len(out_shape),
    )


def segment_bounds(lengths, frames):
    ends = jnp.cumsum(lengths)
    starts = ends - lengths
    seg_start = jnp.max(jnp.where(starts[None, :] <= frames[:, None], starts[None, :], 0), axis=1)
    big = jnp.iinfo(jnp.int32).max
    seg_end = jnp.min(jnp.where(ends[None, :] > frames[:, None], ends[None, :], big), axis=1)
    return (seg_start, jnp.minimum(seg_end, ends[-1]))


def tile_ranges(lengths, base, ext_rows, block_rows):
    frames = base + (ext_rows - block_rows) // 2 + jnp.arange(block_rows, dtype=jnp.int32)
    seg_start, seg_end = segment_bounds(lengths, frames)
    lo = (seg_start[::TILE_Q] - base) // TILE_K
    hi = (seg_end[TILE_Q - 1 :: TILE_Q] - base + TILE_K - 1) // TILE_K
    lo = jnp.clip(lo, 0, ext_rows // TILE_K).astype(jnp.int32)
    hi = jnp.clip(hi, lo, ext_rows // TILE_K).astype(jnp.int32)
    return (lo, hi)


CONV_PAD = 128
CONV_CHUNK = 256


def conv_chunk(x_ref, wt_ref, lo, hi, c0, sign):
    window = x_ref[:, pl.ds(c0, CONV_CHUNK + 2 * CONV_PAD)]
    width = window.shape[1]
    total = jnp.zeros((window.shape[0], CONV_CHUNK), jnp.float32)
    for tap in range(KERNEL):
        d = sign * (tap - KERNEL // 2)
        shifted = pltpu.roll(window, (width - d) % width, 1) if d else window
        keep = (lo <= d) & (d < hi)
        total = total + wt_ref[:, tap : tap + 1] * jnp.where(
            keep, shifted[:, CONV_PAD : CONV_PAD + CONV_CHUNK], 0.0
        )
    return total


def conv_forward_kernel(x_ref, wt_ref, gain_ref, cot_ref, lo_ref, hi_ref, out_ref, gc_ref):
    gain = gain_ref[...]

    def body(c, carry):
        c0 = pl.multiple_of(c * CONV_CHUNK, CONV_CHUNK)
        cols = pl.ds(c0, CONV_CHUNK)
        conv_sum = conv_chunk(x_ref, wt_ref, lo_ref[:, cols], hi_ref[:, cols], c0, 1)
        spread = jnp.sqrt(jnp.mean(conv_sum * conv_sum, axis=0, keepdims=True) + 1e-05)
        normed = conv_sum / spread
        pre_act = normed * gain
        gate = 1.0 / (1.0 + jnp.exp(-pre_act))
        out_ref[:, cols] = (pre_act * gate).astype(out_ref.dtype)
        grad_pre = cot_ref[:, cols].astype(jnp.float32) * gate * (1.0 + pre_act * (1.0 - gate))
        weighted = grad_pre * gain
        gc_ref[:, cols] = (
            weighted - normed * jnp.mean(weighted * normed, axis=0, keepdims=True)
        ) / spread
        return carry

    lax.fori_loop(0, out_ref.shape[1] // CONV_CHUNK, body, 0)


def conv_backward_kernel(y_ref, wt_ref, att_ref, lo_ref, hi_ref, ga_ref, delta_ref):
    def body(c, carry):
        c0 = pl.multiple_of(c * CONV_CHUNK, CONV_CHUNK)
        cols = pl.ds(c0, CONV_CHUNK)
        grad_sum = conv_chunk(y_ref, wt_ref, lo_ref[:, cols], hi_ref[:, cols], c0, -1)
        grad_att = grad_sum.astype(ga_ref.dtype)
        ga_ref[:, cols] = grad_att
        delta_ref[:, cols] = jnp.sum(
            grad_att.astype(jnp.float32) * att_ref[:, cols].astype(jnp.float32),
            axis=0,
            keepdims=True,
        )
        return carry

    lax.fori_loop(0, ga_ref.shape[1] // CONV_CHUNK, body, 0)


def padded_rims(block, half):
    count = lax.axis_size("blk")
    forward = [(i, i + 1) for i in range(count - 1)]
    backward = [(target, source) for source, target in forward]
    low = lax.ppermute(block[:, block.shape[1] - half :], "blk", forward)
    high = lax.ppermute(block[:, :half], "blk", backward)
    gap = jnp.zeros((block.shape[0], CONV_PAD - half), jnp.float32)
    return jnp.concatenate(
        [gap, low.astype(jnp.float32), block.astype(jnp.float32), high.astype(jnp.float32), gap],
        axis=1,
    )


def on_device(queries, keys, values, lengths, conv_weight, norm_gain, cotangent):
    rows_in, width = queries.shape
    heads_total = width // HEAD_DIM
    stacked = jnp.stack(
        [a.reshape(rows_in, heads_total, HEAD_DIM) for a in (queries, keys, values)], axis=2
    ).reshape(rows_in, heads_total * 3 * HEAD_DIM)
    local_qkv = lax.all_to_all(stacked, "uly", split_axis=1, concat_axis=0, tiled=True)
    local_qkv = local_qkv.reshape(local_qkv.shape[0], -1, 3, HEAD_DIM)
    local_q, local_k, local_v = (
        local_qkv[:, :, i].reshape(local_qkv.shape[0], -1) for i in range(3)
    )
    block_rows, channels = local_q.shape
    heads_here = channels // HEAD_DIM
    maxlen = block_rows // 2
    rows_q = min(512, block_rows)
    window = rows_q + 2 * maxlen
    conv_half = KERNEL // 2
    block_count = block_rows // rows_q
    score_scale = HEAD_DIM ** (-0.5)
    frame_total = lax.axis_size("blk") * block_rows
    first_frame = lax.axis_index("blk") * block_rows
    seg_ext = segment_ids(
        lengths,
        first_frame - maxlen + jnp.arange(block_rows + 2 * maxlen, dtype=jnp.int32),
        frame_total,
    )
    seg_own = seg_ext[maxlen : maxlen + block_rows]
    seg_conv = seg_ext[maxlen - conv_half : maxlen + block_rows + conv_half]
    near_pairs = extended(jnp.concatenate([local_k, local_v], axis=1), (("blk", 0),), maxlen)
    k_ext = near_pairs[:, :channels].reshape(-1, heads_here, HEAD_DIM)
    v_ext = near_pairs[:, channels:].reshape(-1, heads_here, HEAD_DIM)
    q_heads = local_q.reshape(block_rows, heads_here, HEAD_DIM)
    starts = jnp.arange(block_count, dtype=jnp.int32) * rows_q

    assert heads_here == 1
    lo_t, hi_t = tile_ranges(lengths, first_frame - maxlen, block_rows + 2 * maxlen, block_rows)
    qseg_col = seg_own[:, None].astype(jnp.int32)
    kseg_row = seg_ext[None, :].astype(jnp.int32)
    k_flat = k_ext.reshape(-1, HEAD_DIM)
    v_flat = v_ext.reshape(-1, HEAD_DIM)
    attended, row_tops, row_totals = vmem_call(
        forward_kernel,
        2,
        5,
        (
            jax.ShapeDtypeStruct((block_rows, HEAD_DIM), jnp.bfloat16),
            jax.ShapeDtypeStruct((block_rows, 1), jnp.float32),
            jax.ShapeDtypeStruct((block_rows, 1), jnp.float32),
        ),
    )(lo_t, hi_t, local_q, k_flat, v_flat, qseg_col, kseg_row)
    frame_at = first_frame + jnp.arange(block_rows, dtype=jnp.int32)
    seg_start, seg_end = segment_bounds(lengths, frame_at)
    lo_off = (seg_start - frame_at)[None, :].astype(jnp.int32)
    hi_off = (seg_end - frame_at)[None, :].astype(jnp.int32)
    weight_t = conv_weight.T
    att_t = attended.T
    conv_out_t, grad_conv_t = vmem_call(
        conv_forward_kernel,
        0,
        6,
        (
            jax.ShapeDtypeStruct((HEAD_DIM, block_rows), jnp.bfloat16),
            jax.ShapeDtypeStruct((HEAD_DIM, block_rows), jnp.float32),
        ),
    )(padded_rims(att_t, conv_half), weight_t, norm_gain[:, None], cotangent, lo_off, hi_off)
    grad_att_t, delta_row = vmem_call(
        conv_backward_kernel,
        0,
        5,
        (
            jax.ShapeDtypeStruct((HEAD_DIM, block_rows), jnp.bfloat16),
            jax.ShapeDtypeStruct((1, block_rows), jnp.float32),
        ),
    )(padded_rims(grad_conv_t, conv_half), weight_t, att_t, lo_off, hi_off)
    grad_attended = grad_att_t.T
    row_delta = delta_row.T

    ext_rows = block_rows + 2 * maxlen
    grad_q, dk_t, dv_t = vmem_call(
        backward_kernel,
        2,
        11,
        (
            jax.ShapeDtypeStruct((block_rows, HEAD_DIM), jnp.bfloat16),
            jax.ShapeDtypeStruct((HEAD_DIM, ext_rows), jnp.float32),
            jax.ShapeDtypeStruct((HEAD_DIM, ext_rows), jnp.float32),
        ),
    )(
        lo_t,
        hi_t,
        local_q,
        k_flat,
        v_flat,
        grad_attended,
        local_q.T,
        grad_att_t,
        qseg_col,
        kseg_row,
        row_tops,
        1.0 / row_totals,
        row_delta,
    )
    ext_terms = jnp.concatenate([dk_t, dv_t], axis=0)
    received = []
    for rim_part, direction in ((ext_terms[:, :maxlen], -1), (ext_terms[:, maxlen + block_rows :], 1)):
        received.append(
            passed_along(rim_part.astype(jnp.bfloat16), "blk", direction).astype(rim_part.dtype)
        )
    key_grads = ext_terms[:, maxlen : maxlen + block_rows] + jnp.concatenate(
        [received[1], received[0]], axis=1
    )
    grad_queries = grad_q.reshape(block_rows, channels)
    grad_keys = key_grads[:HEAD_DIM].astype(jnp.bfloat16)
    grad_values = key_grads[HEAD_DIM:].astype(jnp.bfloat16)
    return (conv_out_t, grad_queries.T, grad_keys, grad_values)


def solution(mesh):
    in_specs = (
        P(("blk", "uly"), None),
        P(("blk", "uly"), None),
        P(("blk", "uly"), None),
        P(),
        P(None, "uly"),
        P("uly"),
        P("uly", "blk"),
    )
    out_specs = (P("uly", "blk"), P("uly", "blk"), P("uly", "blk"), P("uly", "blk"))
    return jax.shard_map(
        on_device, mesh=mesh, in_specs=in_specs, out_specs=out_specs, check_vma=False
    )
```

```python
import jax
import jax.numpy as jnp
import functools
from jax import lax
from jax.experimental import pallas as pl
from jax.experimental.pallas import tpu as pltpu
from jax.sharding import PartitionSpec as P

KERNEL = 31
HEAD_DIM = 64


def extended(block, sides, width):
    for axis, dim in sides:
        count = lax.axis_size(axis)
        forward = [(i, i + 1) for i in range(count - 1)]
        backward = [(target, source) for source, target in forward]
        low = lax.ppermute(
            lax.slice_in_dim(block, block.shape[dim] - width, None, axis=dim), axis, forward
        )
        high = lax.ppermute(lax.slice_in_dim(block, 0, width, axis=dim), axis, backward)
        block = jnp.concatenate([low, block, high], axis=dim)
    return block


def passed_along(block, axis, distance):
    devices = range(lax.axis_size(axis))
    route = [(i - distance, i) for i in devices if i - distance in devices]
    return lax.ppermute(block, axis, route)


def segment_ids(lengths, frames, frame_total):
    starts = jnp.cumsum(lengths) - lengths
    seg_ids = jnp.sum((starts[None, :] <= frames[:, None]).astype(jnp.int32), axis=1) - 1
    inside = (frames >= 0) & (frames < frame_total)
    return jnp.where(inside, seg_ids, -1)


def rows_at(values_in, row_start, row_count):
    return lax.dynamic_slice_in_dim(values_in, row_start, row_count, 0)


def masked_scores(query_rows, key_rows, query_seg, key_seg):
    scores = HEAD_DIM ** (-0.5) * jnp.einsum(
        "rhe,she->hrs", query_rows, key_rows, preferred_element_type=jnp.float32
    )
    same_seg = (query_seg[:, None] == key_seg[None, :])[None]
    return (scores, same_seg)


def weights_of(scores, same_seg, row_top, row_total):
    return jnp.where(same_seg, jnp.exp(scores - row_top), 0.0) / row_total


TILE_Q = 512
TILE_K = 512
NT = (((1,), (1,)), ((), ()))
TN = (((0,), (0,)), ((), ()))


def forward_kernel(lo_ref, hi_ref, q_ref, k_ref, v_ref, qseg_ref, kseg_ref, o_ref, m_ref, l_ref):
    scale = HEAD_DIM ** (-0.5)

    def q_body(i, carry):
        r0 = pl.multiple_of(i * TILE_Q, TILE_Q)
        q = q_ref[pl.ds(r0, TILE_Q), :] * jnp.asarray(scale, q_ref.dtype)
        qs = qseg_ref[pl.ds(r0, TILE_Q), :]

        def k_body(j, c):
            m, l, acc = c
            c0 = pl.multiple_of(j * TILE_K, TILE_K)
            k = k_ref[pl.ds(c0, TILE_K), :]
            v = v_ref[pl.ds(c0, TILE_K), :]
            ks = kseg_ref[:, pl.ds(c0, TILE_K)]
            s = lax.dot_general(q, k, NT, preferred_element_type=jnp.float32)
            s = jnp.where(qs == ks, s, -1e30)
            m_new = jnp.maximum(m, jnp.max(s, axis=1, keepdims=True))
            alpha = jnp.exp(m - m_new)
            p = jnp.exp(s - m_new)
            l = alpha * l + jnp.sum(p, axis=1, keepdims=True)
            acc = alpha * acc + jnp.dot(
                p.astype(jnp.bfloat16), v, preferred_element_type=jnp.float32
            )
            return (m_new, l, acc)

        init = (
            jnp.full((TILE_Q, 1), -1e30, jnp.float32),
            jnp.zeros((TILE_Q, 1), jnp.float32),
            jnp.zeros((TILE_Q, HEAD_DIM), jnp.float32),
        )
        m, l, acc = lax.fori_loop(lo_ref[i], hi_ref[i], k_body, init)
        o_ref[pl.ds(r0, TILE_Q), :] = (acc / l).astype(o_ref.dtype)
        m_ref[pl.ds(r0, TILE_Q), :] = m
        l_ref[pl.ds(r0, TILE_Q), :] = l
        return carry

    lax.fori_loop(0, q_ref.shape[0] // TILE_Q, q_body, 0)


def backward_kernel(
    lo_ref, hi_ref, q_ref, k_ref, v_ref, do_ref, qt_ref, dot_ref, qseg_ref, kseg_ref, lse_ref,
    d_ref, dq_ref, dk_ref, dv_ref,
):
    scale = HEAD_DIM ** (-0.5)
    dk_ref[...] = jnp.zeros_like(dk_ref)
    dv_ref[...] = jnp.zeros_like(dv_ref)

    def q_body(i, carry):
        r0 = pl.multiple_of(i * TILE_Q, TILE_Q)
        q = q_ref[pl.ds(r0, TILE_Q), :] * jnp.asarray(scale, q_ref.dtype)
        do = do_ref[pl.ds(r0, TILE_Q), :]
        qs = qseg_ref[pl.ds(r0, TILE_Q), :]
        lse = lse_ref[pl.ds(r0, TILE_Q), :]
        dlt = d_ref[pl.ds(r0, TILE_Q), :]
        q_t = qt_ref[:, pl.ds(r0, TILE_Q)]
        do_t = dot_ref[:, pl.ds(r0, TILE_Q)]

        def k_body(j, dq):
            c0 = pl.multiple_of(j * TILE_K, TILE_K)
            k = k_ref[pl.ds(c0, TILE_K), :]
            v = v_ref[pl.ds(c0, TILE_K), :]
            ks = kseg_ref[:, pl.ds(c0, TILE_K)]
            s = lax.dot_general(q, k, NT, preferred_element_type=jnp.float32)
            p = jnp.exp(jnp.where(qs == ks, s, -1e30) - lse)
            dp = lax.dot_general(do, v, NT, preferred_element_type=jnp.float32)
            ds = (p * (dp - dlt)).astype(jnp.bfloat16)
            dk_ref[:, pl.ds(c0, TILE_K)] += jnp.dot(q_t, ds, preferred_element_type=jnp.float32)
            dv_ref[:, pl.ds(c0, TILE_K)] += jnp.dot(
                do_t, p.astype(jnp.bfloat16), preferred_element_type=jnp.float32
            )
            return dq + jnp.dot(ds, k, preferred_element_type=jnp.float32)

        dq = lax.fori_loop(
            lo_ref[i], hi_ref[i], k_body, jnp.zeros((TILE_Q, HEAD_DIM), jnp.float32)
        )
        dq_ref[pl.ds(r0, TILE_Q), :] = (scale * dq).astype(dq_ref.dtype)
        return carry

    lax.fori_loop(0, q_ref.shape[0] // TILE_Q, q_body, 0)
    dk_ref[...] = scale * dk_ref[...]


def vmem_call(kernel, n_smem, n_vmem, out_shape):
    return pl.pallas_call(
        kernel,
        out_shape=out_shape,
        in_specs=[pl.BlockSpec(memory_space=pltpu.SMEM)] * n_smem
        + [pl.BlockSpec(memory_space=pltpu.VMEM)] * n_vmem,
        out_specs=[pl.BlockSpec(memory_space=pltpu.VMEM)] * len(out_shape),
    )


def segment_bounds(lengths, frames):
    ends = jnp.cumsum(lengths)
    starts = ends - lengths
    seg_start = jnp.max(jnp.where(starts[None, :] <= frames[:, None], starts[None, :], 0), axis=1)
    big = jnp.iinfo(jnp.int32).max
    seg_end = jnp.min(jnp.where(ends[None, :] > frames[:, None], ends[None, :], big), axis=1)
    return (seg_start, jnp.minimum(seg_end, ends[-1]))


def tile_ranges(lengths, base, ext_rows, block_rows):
    frames = base + (ext_rows - block_rows) // 2 + jnp.arange(block_rows, dtype=jnp.int32)
    seg_start, seg_end = segment_bounds(lengths, frames)
    lo = (seg_start[::TILE_Q] - base) // TILE_K
    hi = (seg_end[TILE_Q - 1 :: TILE_Q] - base + TILE_K - 1) // TILE_K
    lo = jnp.clip(lo, 0, ext_rows // TILE_K).astype(jnp.int32)
    hi = jnp.clip(hi, lo, ext_rows // TILE_K).astype(jnp.int32)
    return (lo, hi)


CONV_PAD = 128
CONV_CHUNK = 256


def conv_chunk(x_ref, wt_ref, lo, hi, c0, sign):
    window = x_ref[:, pl.ds(c0, CONV_CHUNK + 2 * CONV_PAD)]
    width = window.shape[1]
    total = jnp.zeros((window.shape[0], CONV_CHUNK), jnp.float32)
    for tap in range(KERNEL):
        d = sign * (tap - KERNEL // 2)
        shifted = pltpu.roll(window, (width - d) % width, 1) if d else window
        keep = (lo <= d) & (d < hi)
        total = total + wt_ref[:, tap : tap + 1] * jnp.where(
            keep, shifted[:, CONV_PAD : CONV_PAD + CONV_CHUNK], 0.0
        )
    return total


def conv_forward_kernel(x_ref, wt_ref, gain_ref, cot_ref, lo_ref, hi_ref, out_ref, gc_ref):
    gain = gain_ref[...]

    def body(c, carry):
        c0 = pl.multiple_of(c * CONV_CHUNK, CONV_CHUNK)
        cols = pl.ds(c0, CONV_CHUNK)
        conv_sum = conv_chunk(x_ref, wt_ref, lo_ref[:, cols], hi_ref[:, cols], c0, 1)
        spread = jnp.sqrt(jnp.mean(conv_sum * conv_sum, axis=0, keepdims=True) + 1e-05)
        normed = conv_sum / spread
        pre_act = normed * gain
        gate = 1.0 / (1.0 + jnp.exp(-pre_act))
        out_ref[:, cols] = (pre_act * gate).astype(out_ref.dtype)
        grad_pre = cot_ref[:, cols].astype(jnp.float32) * gate * (1.0 + pre_act * (1.0 - gate))
        weighted = grad_pre * gain
        gc_ref[:, cols] = (
            weighted - normed * jnp.mean(weighted * normed, axis=0, keepdims=True)
        ) / spread
        return carry

    lax.fori_loop(0, out_ref.shape[1] // CONV_CHUNK, body, 0)


def conv_backward_kernel(y_ref, wt_ref, att_ref, lo_ref, hi_ref, ga_ref, delta_ref):
    def body(c, carry):
        c0 = pl.multiple_of(c * CONV_CHUNK, CONV_CHUNK)
        cols = pl.ds(c0, CONV_CHUNK)
        grad_sum = conv_chunk(y_ref, wt_ref, lo_ref[:, cols], hi_ref[:, cols], c0, -1)
        grad_att = grad_sum.astype(ga_ref.dtype)
        ga_ref[:, cols] = grad_att
        delta_ref[:, cols] = jnp.sum(
            grad_att.astype(jnp.float32) * att_ref[:, cols].astype(jnp.float32),
            axis=0,
            keepdims=True,
        )
        return carry

    lax.fori_loop(0, ga_ref.shape[1] // CONV_CHUNK, body, 0)


def padded_rims(block, half):
    count = lax.axis_size("blk")
    forward = [(i, i + 1) for i in range(count - 1)]
    backward = [(target, source) for source, target in forward]
    low = lax.ppermute(block[:, block.shape[1] - half :], "blk", forward)
    high = lax.ppermute(block[:, :half], "blk", backward)
    gap = jnp.zeros((block.shape[0], CONV_PAD - half), jnp.float32)
    return jnp.concatenate(
        [gap, low.astype(jnp.float32), block.astype(jnp.float32), high.astype(jnp.float32), gap],
        axis=1,
    )


def on_device(queries, keys, values, lengths, conv_weight, norm_gain, cotangent):
    rows_in, width = queries.shape
    heads_total = width // HEAD_DIM
    stacked = jnp.stack(
        [a.reshape(rows_in, heads_total, HEAD_DIM) for a in (queries, keys, values)], axis=2
    ).reshape(rows_in, heads_total * 3 * HEAD_DIM)
    local_qkv = lax.all_to_all(stacked, "uly", split_axis=1, concat_axis=0, tiled=True)
    local_qkv = local_qkv.reshape(local_qkv.shape[0], -1, 3, HEAD_DIM)
    local_q, local_k, local_v = (
        local_qkv[:, :, i].reshape(local_qkv.shape[0], -1) for i in range(3)
    )
    block_rows, channels = local_q.shape
    heads_here = channels // HEAD_DIM
    maxlen = block_rows // 2
    rows_q = min(512, block_rows)
    window = rows_q + 2 * maxlen
    conv_half = KERNEL // 2
    block_count = block_rows // rows_q
    score_scale = HEAD_DIM ** (-0.5)
    frame_total = lax.axis_size("blk") * block_rows
    first_frame = lax.axis_index("blk") * block_rows
    seg_ext = segment_ids(
        lengths,
        first_frame - maxlen + jnp.arange(block_rows + 2 * maxlen, dtype=jnp.int32),
        frame_total,
    )
    seg_own = seg_ext[maxlen : maxlen + block_rows]
    seg_conv = seg_ext[maxlen - conv_half : maxlen + block_rows + conv_half]
    near_pairs = extended(jnp.concatenate([local_k, local_v], axis=1), (("blk", 0),), maxlen)
    k_ext = near_pairs[:, :channels].reshape(-1, heads_here, HEAD_DIM)
    v_ext = near_pairs[:, channels:].reshape(-1, heads_here, HEAD_DIM)
    q_heads = local_q.reshape(block_rows, heads_here, HEAD_DIM)
    starts = jnp.arange(block_count, dtype=jnp.int32) * rows_q

    assert heads_here == 1
    lo_t, hi_t = tile_ranges(lengths, first_frame - maxlen, block_rows + 2 * maxlen, block_rows)
    qseg_col = seg_own[:, None].astype(jnp.int32)
    kseg_row = seg_ext[None, :].astype(jnp.int32)
    k_flat = k_ext.reshape(-1, HEAD_DIM)
    v_flat = v_ext.reshape(-1, HEAD_DIM)
    attended, row_tops, row_totals = vmem_call(
        forward_kernel,
        2,
        5,
        (
            jax.ShapeDtypeStruct((block_rows, HEAD_DIM), jnp.bfloat16),
            jax.ShapeDtypeStruct((block_rows, 1), jnp.float32),
            jax.ShapeDtypeStruct((block_rows, 1), jnp.float32),
        ),
    )(lo_t, hi_t, local_q, k_flat, v_flat, qseg_col, kseg_row)
    frame_at = first_frame + jnp.arange(block_rows, dtype=jnp.int32)
    seg_start, seg_end = segment_bounds(lengths, frame_at)
    lo_off = (seg_start - frame_at)[None, :].astype(jnp.int32)
    hi_off = (seg_end - frame_at)[None, :].astype(jnp.int32)
    weight_t = conv_weight.T
    att_t = attended.T
    conv_out_t, grad_conv_t = vmem_call(
        conv_forward_kernel,
        0,
        6,
        (
            jax.ShapeDtypeStruct((HEAD_DIM, block_rows), jnp.bfloat16),
            jax.ShapeDtypeStruct((HEAD_DIM, block_rows), jnp.float32),
        ),
    )(padded_rims(att_t, conv_half), weight_t, norm_gain[:, None], cotangent, lo_off, hi_off)
    grad_att_t, delta_row = vmem_call(
        conv_backward_kernel,
        0,
        5,
        (
            jax.ShapeDtypeStruct((HEAD_DIM, block_rows), jnp.bfloat16),
            jax.ShapeDtypeStruct((1, block_rows), jnp.float32),
        ),
    )(padded_rims(grad_conv_t, conv_half), weight_t, att_t, lo_off, hi_off)
    grad_attended = grad_att_t.T
    row_delta = delta_row.T

    ext_rows = block_rows + 2 * maxlen
    grad_q, dk_t, dv_t = vmem_call(
        backward_kernel,
        2,
        10,
        (
            jax.ShapeDtypeStruct((block_rows, HEAD_DIM), jnp.bfloat16),
            jax.ShapeDtypeStruct((HEAD_DIM, ext_rows), jnp.float32),
            jax.ShapeDtypeStruct((HEAD_DIM, ext_rows), jnp.float32),
        ),
    )(
        lo_t,
        hi_t,
        local_q,
        k_flat,
        v_flat,
        grad_attended,
        local_q.T,
        grad_att_t,
        qseg_col,
        kseg_row,
        row_tops + jnp.log(row_totals),
        row_delta,
    )
    ext_terms = jnp.concatenate([dk_t, dv_t], axis=0)
    received = []
    for rim_part, direction in ((ext_terms[:, :maxlen], -1), (ext_terms[:, maxlen + block_rows :], 1)):
        received.append(
            passed_along(rim_part.astype(jnp.bfloat16), "blk", direction).astype(rim_part.dtype)
        )
    key_grads = ext_terms[:, maxlen : maxlen + block_rows] + jnp.concatenate(
        [received[1], received[0]], axis=1
    )
    grad_queries = grad_q.reshape(block_rows, channels)
    grad_keys = key_grads[:HEAD_DIM].astype(jnp.bfloat16)
    grad_values = key_grads[HEAD_DIM:].astype(jnp.bfloat16)
    return (conv_out_t, grad_queries.T, grad_keys, grad_values)


def solution(mesh):
    in_specs = (
        P(("blk", "uly"), None),
        P(("blk", "uly"), None),
        P(("blk", "uly"), None),
        P(),
        P(None, "uly"),
        P("uly"),
        P("uly", "blk"),
    )
    out_specs = (P("uly", "blk"), P("uly", "blk"), P("uly", "blk"), P("uly", "blk"))
    return jax.shard_map(
        on_device, mesh=mesh, in_specs=in_specs, out_specs=out_specs, check_vma=False
    )
```

```python
import jax
import jax.numpy as jnp
import functools
from jax import lax
from jax.experimental import pallas as pl
from jax.experimental.pallas import tpu as pltpu
from jax.sharding import PartitionSpec as P

KERNEL = 31
HEAD_DIM = 64


def extended(block, sides, width):
    for axis, dim in sides:
        count = lax.axis_size(axis)
        forward = [(i, i + 1) for i in range(count - 1)]
        backward = [(target, source) for source, target in forward]
        low = lax.ppermute(
            lax.slice_in_dim(block, block.shape[dim] - width, None, axis=dim), axis, forward
        )
        high = lax.ppermute(lax.slice_in_dim(block, 0, width, axis=dim), axis, backward)
        block = jnp.concatenate([low, block, high], axis=dim)
    return block


def passed_along(block, axis, distance):
    devices = range(lax.axis_size(axis))
    route = [(i - distance, i) for i in devices if i - distance in devices]
    return lax.ppermute(block, axis, route)


def segment_ids(lengths, frames, frame_total):
    starts = jnp.cumsum(lengths) - lengths
    seg_ids = jnp.sum((starts[None, :] <= frames[:, None]).astype(jnp.int32), axis=1) - 1
    inside = (frames >= 0) & (frames < frame_total)
    return jnp.where(inside, seg_ids, -1)


def rows_at(values_in, row_start, row_count):
    return lax.dynamic_slice_in_dim(values_in, row_start, row_count, 0)


def masked_scores(query_rows, key_rows, query_seg, key_seg):
    scores = HEAD_DIM ** (-0.5) * jnp.einsum(
        "rhe,she->hrs", query_rows, key_rows, preferred_element_type=jnp.float32
    )
    same_seg = (query_seg[:, None] == key_seg[None, :])[None]
    return (scores, same_seg)


def weights_of(scores, same_seg, row_top, row_total):
    return jnp.where(same_seg, jnp.exp(scores - row_top), 0.0) / row_total


TILE_Q = 512
TILE_K = 512
NT = (((1,), (1,)), ((), ()))
TN = (((0,), (0,)), ((), ()))


def forward_kernel(lo_ref, hi_ref, q_ref, k_ref, v_ref, qseg_ref, kseg_ref, o_ref, m_ref, l_ref):
    scale = HEAD_DIM ** (-0.5)

    def q_body(i, carry):
        r0 = pl.multiple_of(i * TILE_Q, TILE_Q)
        q = q_ref[pl.ds(r0, TILE_Q), :] * jnp.asarray(scale, q_ref.dtype)
        qs = qseg_ref[pl.ds(r0, TILE_Q), :]

        def k_body(j, c):
            m, l, acc = c
            c0 = pl.multiple_of(j * TILE_K, TILE_K)
            k = k_ref[pl.ds(c0, TILE_K), :]
            v = v_ref[pl.ds(c0, TILE_K), :]
            ks = kseg_ref[:, pl.ds(c0, TILE_K)]
            s = lax.dot_general(q, k, NT, preferred_element_type=jnp.float32)
            s = jnp.where(qs == ks, s, -1e30)
            m_new = jnp.maximum(m, jnp.max(s, axis=1, keepdims=True))
            alpha = jnp.exp(m - m_new)
            p = jnp.exp(s - m_new)
            l = alpha * l + jnp.sum(p, axis=1, keepdims=True)
            acc = alpha * acc + jnp.dot(
                p.astype(jnp.bfloat16), v, preferred_element_type=jnp.float32
            )
            return (m_new, l, acc)

        init = (
            jnp.full((TILE_Q, 1), -1e30, jnp.float32),
            jnp.zeros((TILE_Q, 1), jnp.float32),
            jnp.zeros((TILE_Q, HEAD_DIM), jnp.float32),
        )
        m, l, acc = lax.fori_loop(lo_ref[i], hi_ref[i], k_body, init)
        o_ref[pl.ds(r0, TILE_Q), :] = (acc / l).astype(o_ref.dtype)
        m_ref[pl.ds(r0, TILE_Q), :] = m
        l_ref[pl.ds(r0, TILE_Q), :] = l
        return carry

    lax.fori_loop(0, q_ref.shape[0] // TILE_Q, q_body, 0)


def backward_kernel(
    lo_ref, hi_ref, q_ref, k_ref, v_ref, do_ref, qt_ref, dot_ref, qseg_ref, kseg_ref, lse_ref,
    d_ref, dq_ref, dk_ref, dv_ref,
):
    scale = HEAD_DIM ** (-0.5)
    dk_ref[...] = jnp.zeros_like(dk_ref)
    dv_ref[...] = jnp.zeros_like(dv_ref)

    def q_body(i, carry):
        r0 = pl.multiple_of(i * TILE_Q, TILE_Q)
        q = q_ref[pl.ds(r0, TILE_Q), :] * jnp.asarray(scale, q_ref.dtype)
        do = do_ref[pl.ds(r0, TILE_Q), :]
        qs = qseg_ref[pl.ds(r0, TILE_Q), :]
        lse = lse_ref[pl.ds(r0, TILE_Q), :]
        dlt = d_ref[pl.ds(r0, TILE_Q), :]
        q_t = qt_ref[:, pl.ds(r0, TILE_Q)]
        do_t = dot_ref[:, pl.ds(r0, TILE_Q)]

        def k_body(j, dq):
            c0 = pl.multiple_of(j * TILE_K, TILE_K)
            k = k_ref[pl.ds(c0, TILE_K), :]
            v = v_ref[pl.ds(c0, TILE_K), :]
            ks = kseg_ref[:, pl.ds(c0, TILE_K)]
            s = lax.dot_general(q, k, NT, preferred_element_type=jnp.float32)
            p = jnp.exp(jnp.where(qs == ks, s, -1e30) - lse)
            dp = lax.dot_general(do, v, NT, preferred_element_type=jnp.float32)
            ds = (p * (dp - dlt)).astype(jnp.bfloat16)
            dk_ref[:, pl.ds(c0, TILE_K)] += jnp.dot(q_t, ds, preferred_element_type=jnp.float32)
            dv_ref[:, pl.ds(c0, TILE_K)] += jnp.dot(
                do_t, p.astype(jnp.bfloat16), preferred_element_type=jnp.float32
            )
            return dq + jnp.dot(ds, k, preferred_element_type=jnp.float32)

        dq = lax.fori_loop(
            lo_ref[i], hi_ref[i], k_body, jnp.zeros((TILE_Q, HEAD_DIM), jnp.float32)
        )
        dq_ref[pl.ds(r0, TILE_Q), :] = (scale * dq).astype(dq_ref.dtype)
        return carry

    lax.fori_loop(0, q_ref.shape[0] // TILE_Q, q_body, 0)
    dk_ref[...] = scale * dk_ref[...]


def vmem_call(kernel, n_smem, n_vmem, out_shape, scratch=()):
    return pl.pallas_call(
        kernel,
        out_shape=out_shape,
        scratch_shapes=list(scratch),
        in_specs=[pl.BlockSpec(memory_space=pltpu.SMEM)] * n_smem
        + [pl.BlockSpec(memory_space=pltpu.VMEM)] * n_vmem,
        out_specs=[pl.BlockSpec(memory_space=pltpu.VMEM)] * len(out_shape),
    )


def segment_bounds(lengths, frames):
    ends = jnp.cumsum(lengths)
    starts = ends - lengths
    seg_start = jnp.max(jnp.where(starts[None, :] <= frames[:, None], starts[None, :], 0), axis=1)
    big = jnp.iinfo(jnp.int32).max
    seg_end = jnp.min(jnp.where(ends[None, :] > frames[:, None], ends[None, :], big), axis=1)
    return (seg_start, jnp.minimum(seg_end, ends[-1]))


def tile_ranges(lengths, base, ext_rows, block_rows):
    frames = base + (ext_rows - block_rows) // 2 + jnp.arange(block_rows, dtype=jnp.int32)
    seg_start, seg_end = segment_bounds(lengths, frames)
    lo = (seg_start[::TILE_Q] - base) // TILE_K
    hi = (seg_end[TILE_Q - 1 :: TILE_Q] - base + TILE_K - 1) // TILE_K
    lo = jnp.clip(lo, 0, ext_rows // TILE_K).astype(jnp.int32)
    hi = jnp.clip(hi, lo, ext_rows // TILE_K).astype(jnp.int32)
    return (lo, hi)


CONV_PAD = 128
CONV_CHUNK = 256


def conv_group(x_ref, wb_ref, mask_ref, c0, g8, sign):
    win = [x_ref[pl.ds(g8, 8), pl.ds(c0 + 128 * i, 128)] for i in range(4)]
    lane = lax.broadcasted_iota(jnp.int32, (8, 128), 1)
    total = [jnp.zeros((8, 128), jnp.float32) for _ in range(2)]
    for tap in range(KERNEL):
        d = sign * (tap - KERNEL // 2)
        if d == 0:
            outs = [win[1], win[2]]
        elif d > 0:
            r = [pltpu.roll(win[i], 128 - d, 1) for i in (1, 2, 3)]
            outs = [jnp.where(lane < 128 - d, r[k], r[k + 1]) for k in range(2)]
        else:
            r = [pltpu.roll(win[i], -d, 1) for i in (0, 1, 2)]
            outs = [jnp.where(lane >= -d, r[k + 1], r[k]) for k in range(2)]
        w = wb_ref[tap, pl.ds(g8, 8), :]
        for k in range(2):
            total[k] = total[k] + w * (mask_ref[tap, :, pl.ds(128 * k, 128)] * outs[k])
    return jnp.concatenate(total, axis=1)


def conv_chunk(x_ref, wb_ref, lo, hi, c0, sign, mask_ref, cs_ref):
    for tap in range(KERNEL):
        d = sign * (tap - KERNEL // 2)
        keep = ((lo <= d) & (d < hi)).astype(jnp.float32)
        mask_ref[tap] = jnp.broadcast_to(keep, (8, CONV_CHUNK))

    def group(g, carry):
        g8 = pl.multiple_of(g * 8, 8)
        cs_ref[pl.ds(g8, 8), :] = conv_group(x_ref, wb_ref, mask_ref, c0, g8, sign)
        return carry

    lax.fori_loop(0, cs_ref.shape[0] // 8, group, 0)
    return cs_ref[...]


def conv_forward_kernel(
    x_ref, wt_ref, gain_ref, cot_ref, lo_ref, hi_ref, out_ref, gc_ref, mask_ref, cs_ref
):
    gain = gain_ref[...]

    def body(c, carry):
        c0 = pl.multiple_of(c * CONV_CHUNK, CONV_CHUNK)
        cols = pl.ds(c0, CONV_CHUNK)
        conv_sum = conv_chunk(
            x_ref, wt_ref, lo_ref[:, cols], hi_ref[:, cols], c0, 1, mask_ref, cs_ref
        )
        spread = jnp.sqrt(jnp.mean(conv_sum * conv_sum, axis=0, keepdims=True) + 1e-05)
        normed = conv_sum / spread
        pre_act = normed * gain
        gate = 1.0 / (1.0 + jnp.exp(-pre_act))
        out_ref[:, cols] = (pre_act * gate).astype(out_ref.dtype)
        grad_pre = cot_ref[:, cols].astype(jnp.float32) * gate * (1.0 + pre_act * (1.0 - gate))
        weighted = grad_pre * gain
        gc_ref[:, cols] = (
            weighted - normed * jnp.mean(weighted * normed, axis=0, keepdims=True)
        ) / spread
        return carry

    lax.fori_loop(0, out_ref.shape[1] // CONV_CHUNK, body, 0)


def conv_backward_kernel(
    y_ref, wt_ref, att_ref, lo_ref, hi_ref, ga_ref, delta_ref, mask_ref, cs_ref
):
    def body(c, carry):
        c0 = pl.multiple_of(c * CONV_CHUNK, CONV_CHUNK)
        cols = pl.ds(c0, CONV_CHUNK)
        grad_sum = conv_chunk(
            y_ref, wt_ref, lo_ref[:, cols], hi_ref[:, cols], c0, -1, mask_ref, cs_ref
        )
        grad_att = grad_sum.astype(ga_ref.dtype)
        ga_ref[:, cols] = grad_att
        delta_ref[:, cols] = jnp.sum(
            grad_att.astype(jnp.float32) * att_ref[:, cols].astype(jnp.float32),
            axis=0,
            keepdims=True,
        )
        return carry

    lax.fori_loop(0, ga_ref.shape[1] // CONV_CHUNK, body, 0)


def padded_rims(block, half):
    count = lax.axis_size("blk")
    forward = [(i, i + 1) for i in range(count - 1)]
    backward = [(target, source) for source, target in forward]
    low = lax.ppermute(block[:, block.shape[1] - half :], "blk", forward)
    high = lax.ppermute(block[:, :half], "blk", backward)
    gap = jnp.zeros((block.shape[0], CONV_PAD - half), jnp.float32)
    return jnp.concatenate(
        [gap, low.astype(jnp.float32), block.astype(jnp.float32), high.astype(jnp.float32), gap],
        axis=1,
    )


def on_device(queries, keys, values, lengths, conv_weight, norm_gain, cotangent):
    rows_in, width = queries.shape
    heads_total = width // HEAD_DIM
    stacked = jnp.stack(
        [a.reshape(rows_in, heads_total, HEAD_DIM) for a in (queries, keys, values)], axis=2
    ).reshape(rows_in, heads_total * 3 * HEAD_DIM)
    local_qkv = lax.all_to_all(stacked, "uly", split_axis=1, concat_axis=0, tiled=True)
    local_qkv = local_qkv.reshape(local_qkv.shape[0], -1, 3, HEAD_DIM)
    local_q, local_k, local_v = (
        local_qkv[:, :, i].reshape(local_qkv.shape[0], -1) for i in range(3)
    )
    block_rows, channels = local_q.shape
    heads_here = channels // HEAD_DIM
    maxlen = block_rows // 2
    rows_q = min(512, block_rows)
    window = rows_q + 2 * maxlen
    conv_half = KERNEL // 2
    block_count = block_rows // rows_q
    score_scale = HEAD_DIM ** (-0.5)
    frame_total = lax.axis_size("blk") * block_rows
    first_frame = lax.axis_index("blk") * block_rows
    seg_ext = segment_ids(
        lengths,
        first_frame - maxlen + jnp.arange(block_rows + 2 * maxlen, dtype=jnp.int32),
        frame_total,
    )
    seg_own = seg_ext[maxlen : maxlen + block_rows]
    seg_conv = seg_ext[maxlen - conv_half : maxlen + block_rows + conv_half]
    near_pairs = extended(jnp.concatenate([local_k, local_v], axis=1), (("blk", 0),), maxlen)
    k_ext = near_pairs[:, :channels].reshape(-1, heads_here, HEAD_DIM)
    v_ext = near_pairs[:, channels:].reshape(-1, heads_here, HEAD_DIM)
    q_heads = local_q.reshape(block_rows, heads_here, HEAD_DIM)
    starts = jnp.arange(block_count, dtype=jnp.int32) * rows_q

    assert heads_here == 1
    lo_t, hi_t = tile_ranges(lengths, first_frame - maxlen, block_rows + 2 * maxlen, block_rows)
    qseg_col = seg_own[:, None].astype(jnp.int32)
    kseg_row = seg_ext[None, :].astype(jnp.int32)
    k_flat = k_ext.reshape(-1, HEAD_DIM)
    v_flat = v_ext.reshape(-1, HEAD_DIM)
    attended, row_tops, row_totals = vmem_call(
        forward_kernel,
        2,
        5,
        (
            jax.ShapeDtypeStruct((block_rows, HEAD_DIM), jnp.bfloat16),
            jax.ShapeDtypeStruct((block_rows, 1), jnp.float32),
            jax.ShapeDtypeStruct((block_rows, 1), jnp.float32),
        ),
    )(lo_t, hi_t, local_q, k_flat, v_flat, qseg_col, kseg_row)
    frame_at = first_frame + jnp.arange(block_rows, dtype=jnp.int32)
    seg_start, seg_end = segment_bounds(lengths, frame_at)
    lo_off = (seg_start - frame_at)[None, :].astype(jnp.int32)
    hi_off = (seg_end - frame_at)[None, :].astype(jnp.int32)
    weight_t = jnp.broadcast_to(conv_weight[:, :, None], conv_weight.shape + (128,))
    conv_scratch = (
        pltpu.VMEM((KERNEL, 8, CONV_CHUNK), jnp.float32),
        pltpu.VMEM((HEAD_DIM, CONV_CHUNK), jnp.float32),
    )
    att_t = attended.T
    conv_out_t, grad_conv_t = vmem_call(
        conv_forward_kernel,
        0,
        6,
        (
            jax.ShapeDtypeStruct((HEAD_DIM, block_rows), jnp.bfloat16),
            jax.ShapeDtypeStruct((HEAD_DIM, block_rows), jnp.float32),
        ),
        conv_scratch,
    )(padded_rims(att_t, conv_half), weight_t, norm_gain[:, None], cotangent, lo_off, hi_off)
    grad_att_t, delta_row = vmem_call(
        conv_backward_kernel,
        0,
        5,
        (
            jax.ShapeDtypeStruct((HEAD_DIM, block_rows), jnp.bfloat16),
            jax.ShapeDtypeStruct((1, block_rows), jnp.float32),
        ),
        conv_scratch,
    )(padded_rims(grad_conv_t, conv_half), weight_t, att_t, lo_off, hi_off)
    grad_attended = grad_att_t.T
    row_delta = delta_row.T

    ext_rows = block_rows + 2 * maxlen
    grad_q, dk_t, dv_t = vmem_call(
        backward_kernel,
        2,
        10,
        (
            jax.ShapeDtypeStruct((block_rows, HEAD_DIM), jnp.bfloat16),
            jax.ShapeDtypeStruct((HEAD_DIM, ext_rows), jnp.float32),
            jax.ShapeDtypeStruct((HEAD_DIM, ext_rows), jnp.float32),
        ),
    )(
        lo_t,
        hi_t,
        local_q,
        k_flat,
        v_flat,
        grad_attended,
        local_q.T,
        grad_att_t,
        qseg_col,
        kseg_row,
        row_tops + jnp.log(row_totals),
        row_delta,
    )
    ext_terms = jnp.concatenate([dk_t, dv_t], axis=0)
    received = []
    for rim_part, direction in ((ext_terms[:, :maxlen], -1), (ext_terms[:, maxlen + block_rows :], 1)):
        received.append(
            passed_along(rim_part.astype(jnp.bfloat16), "blk", direction).astype(rim_part.dtype)
        )
    key_grads = ext_terms[:, maxlen : maxlen + block_rows] + jnp.concatenate(
        [received[1], received[0]], axis=1
    )
    grad_queries = grad_q.reshape(block_rows, channels)
    grad_keys = key_grads[:HEAD_DIM].astype(jnp.bfloat16)
    grad_values = key_grads[HEAD_DIM:].astype(jnp.bfloat16)
    return (conv_out_t, grad_queries.T, grad_keys, grad_values)


def solution(mesh):
    in_specs = (
        P(("blk", "uly"), None),
        P(("blk", "uly"), None),
        P(("blk", "uly"), None),
        P(),
        P(None, "uly"),
        P("uly"),
        P("uly", "blk"),
    )
    out_specs = (P("uly", "blk"), P("uly", "blk"), P("uly", "blk"), P("uly", "blk"))
    return jax.shard_map(
        on_device, mesh=mesh, in_specs=in_specs, out_specs=out_specs, check_vma=False
    )
```

```python
import jax
import jax.numpy as jnp
import functools
from jax import lax
from jax.experimental import pallas as pl
from jax.experimental.pallas import tpu as pltpu
from jax.sharding import PartitionSpec as P

KERNEL = 31
HEAD_DIM = 64


def extended(block, sides, width):
    for axis, dim in sides:
        count = lax.axis_size(axis)
        forward = [(i, i + 1) for i in range(count - 1)]
        backward = [(target, source) for source, target in forward]
        low = lax.ppermute(
            lax.slice_in_dim(block, block.shape[dim] - width, None, axis=dim), axis, forward
        )
        high = lax.ppermute(lax.slice_in_dim(block, 0, width, axis=dim), axis, backward)
        block = jnp.concatenate([low, block, high], axis=dim)
    return block


def passed_along(block, axis, distance):
    devices = range(lax.axis_size(axis))
    route = [(i - distance, i) for i in devices if i - distance in devices]
    return lax.ppermute(block, axis, route)


def segment_ids(lengths, frames, frame_total):
    starts = jnp.cumsum(lengths) - lengths
    seg_ids = jnp.sum((starts[None, :] <= frames[:, None]).astype(jnp.int32), axis=1) - 1
    inside = (frames >= 0) & (frames < frame_total)
    return jnp.where(inside, seg_ids, -1)


def rows_at(values_in, row_start, row_count):
    return lax.dynamic_slice_in_dim(values_in, row_start, row_count, 0)


def masked_scores(query_rows, key_rows, query_seg, key_seg):
    scores = HEAD_DIM ** (-0.5) * jnp.einsum(
        "rhe,she->hrs", query_rows, key_rows, preferred_element_type=jnp.float32
    )
    same_seg = (query_seg[:, None] == key_seg[None, :])[None]
    return (scores, same_seg)


def weights_of(scores, same_seg, row_top, row_total):
    return jnp.where(same_seg, jnp.exp(scores - row_top), 0.0) / row_total


TILE_Q = 512
TILE_K = 512
NT = (((1,), (1,)), ((), ()))
TN = (((0,), (0,)), ((), ()))


def forward_kernel(lo_ref, hi_ref, q_ref, k_ref, v_ref, qseg_ref, kseg_ref, o_ref, m_ref, l_ref):
    scale = HEAD_DIM ** (-0.5)

    def q_body(i, carry):
        r0 = pl.multiple_of(i * TILE_Q, TILE_Q)
        q = q_ref[pl.ds(r0, TILE_Q), :] * jnp.asarray(scale, q_ref.dtype)
        qs = qseg_ref[pl.ds(r0, TILE_Q), :]

        def k_body(j, c):
            m, acc = c
            c0 = pl.multiple_of(j * TILE_K, TILE_K)
            k = k_ref[pl.ds(c0, TILE_K), :]
            v = v_ref[pl.ds(c0, TILE_K), :]
            ks = kseg_ref[:, pl.ds(c0, TILE_K)]
            s = lax.dot_general(q, k, NT, preferred_element_type=jnp.float32)
            s = jnp.where(qs == ks, s, -1e30)
            m_new = jnp.maximum(m, jnp.max(s, axis=1, keepdims=True))
            alpha = jnp.exp(m - m_new)
            p = jnp.exp(s - m_new)
            acc = alpha * acc + jnp.dot(
                p.astype(jnp.bfloat16), v, preferred_element_type=jnp.float32
            )
            return (m_new, acc)

        init = (
            jnp.full((TILE_Q, 1), -1e30, jnp.float32),
            jnp.zeros((TILE_Q, v_ref.shape[1]), jnp.float32),
        )
        m, acc = lax.fori_loop(lo_ref[i], hi_ref[i], k_body, init)
        l = acc[:, HEAD_DIM : HEAD_DIM + 1]
        o_ref[pl.ds(r0, TILE_Q), :] = (acc[:, :HEAD_DIM] / l).astype(o_ref.dtype)
        m_ref[pl.ds(r0, TILE_Q), :] = m
        l_ref[pl.ds(r0, TILE_Q), :] = l
        return carry

    lax.fori_loop(0, q_ref.shape[0] // TILE_Q, q_body, 0)


def backward_kernel(
    lo_ref, hi_ref, q_ref, k_ref, v_ref, do_ref, qt_ref, dot_ref, qseg_ref, kseg_ref, lse_ref,
    d_ref, dq_ref, dk_ref, dv_ref,
):
    scale = HEAD_DIM ** (-0.5)
    dk_ref[...] = jnp.zeros_like(dk_ref)
    dv_ref[...] = jnp.zeros_like(dv_ref)

    def q_body(i, carry):
        r0 = pl.multiple_of(i * TILE_Q, TILE_Q)
        q = q_ref[pl.ds(r0, TILE_Q), :] * jnp.asarray(scale, q_ref.dtype)
        do = do_ref[pl.ds(r0, TILE_Q), :]
        qs = qseg_ref[pl.ds(r0, TILE_Q), :]
        lse = lse_ref[pl.ds(r0, TILE_Q), :]
        dlt = d_ref[pl.ds(r0, TILE_Q), :]
        q_t = qt_ref[:, pl.ds(r0, TILE_Q)]
        do_t = dot_ref[:, pl.ds(r0, TILE_Q)]

        def k_body(j, dq):
            c0 = pl.multiple_of(j * TILE_K, TILE_K)
            k = k_ref[pl.ds(c0, TILE_K), :]
            v = v_ref[pl.ds(c0, TILE_K), :]
            ks = kseg_ref[:, pl.ds(c0, TILE_K)]
            s = lax.dot_general(q, k, NT, preferred_element_type=jnp.float32)
            p = jnp.exp(jnp.where(qs == ks, s, -1e30) - lse)
            dp = lax.dot_general(do, v, NT, preferred_element_type=jnp.float32)
            ds = (p * (dp - dlt)).astype(jnp.bfloat16)
            dk_ref[:, pl.ds(c0, TILE_K)] += jnp.dot(q_t, ds, preferred_element_type=jnp.float32)
            dv_ref[:, pl.ds(c0, TILE_K)] += jnp.dot(
                do_t, p.astype(jnp.bfloat16), preferred_element_type=jnp.float32
            )
            return dq + jnp.dot(ds, k, preferred_element_type=jnp.float32)

        dq = lax.fori_loop(
            lo_ref[i], hi_ref[i], k_body, jnp.zeros((TILE_Q, HEAD_DIM), jnp.float32)
        )
        dq_ref[pl.ds(r0, TILE_Q), :] = (scale * dq).astype(dq_ref.dtype)
        return carry

    lax.fori_loop(0, q_ref.shape[0] // TILE_Q, q_body, 0)
    dk_ref[...] = scale * dk_ref[...]


def vmem_call(kernel, n_smem, n_vmem, out_shape):
    return pl.pallas_call(
        kernel,
        out_shape=out_shape,
        in_specs=[pl.BlockSpec(memory_space=pltpu.SMEM)] * n_smem
        + [pl.BlockSpec(memory_space=pltpu.VMEM)] * n_vmem,
        out_specs=[pl.BlockSpec(memory_space=pltpu.VMEM)] * len(out_shape),
    )


def segment_bounds(lengths, frames):
    ends = jnp.cumsum(lengths)
    starts = ends - lengths
    seg_start = jnp.max(jnp.where(starts[None, :] <= frames[:, None], starts[None, :], 0), axis=1)
    big = jnp.iinfo(jnp.int32).max
    seg_end = jnp.min(jnp.where(ends[None, :] > frames[:, None], ends[None, :], big), axis=1)
    return (seg_start, jnp.minimum(seg_end, ends[-1]))


def with_ones(v):
    rows = v.shape[0]
    ones = jnp.ones((rows, 1), v.dtype)
    return jnp.concatenate([v, ones, jnp.zeros((rows, 127 - v.shape[1]), v.dtype)], axis=1)


def tile_ranges(lengths, base, ext_rows, block_rows):
    frames = base + (ext_rows - block_rows) // 2 + jnp.arange(block_rows, dtype=jnp.int32)
    seg_start, seg_end = segment_bounds(lengths, frames)
    lo = (seg_start[::TILE_Q] - base) // TILE_K
    hi = (seg_end[TILE_Q - 1 :: TILE_Q] - base + TILE_K - 1) // TILE_K
    lo = jnp.clip(lo, 0, ext_rows // TILE_K).astype(jnp.int32)
    hi = jnp.clip(hi, lo, ext_rows // TILE_K).astype(jnp.int32)
    return (lo, hi)


CONV_PAD = 128
CONV_CHUNK = 256


def conv_chunk(x_ref, wt_ref, lo, hi, c0, sign):
    window = x_ref[:, pl.ds(c0, CONV_CHUNK + 2 * CONV_PAD)]
    width = window.shape[1]
    total = jnp.zeros((window.shape[0], CONV_CHUNK), jnp.float32)
    for tap in range(KERNEL):
        d = sign * (tap - KERNEL // 2)
        shifted = pltpu.roll(window, (width - d) % width, 1) if d else window
        keep = (lo <= d) & (d < hi)
        total = total + wt_ref[:, tap : tap + 1] * jnp.where(
            keep, shifted[:, CONV_PAD : CONV_PAD + CONV_CHUNK], 0.0
        )
    return total


def conv_forward_kernel(x_ref, wt_ref, gain_ref, cot_ref, lo_ref, hi_ref, out_ref, gc_ref):
    gain = gain_ref[...]

    def body(c, carry):
        c0 = pl.multiple_of(c * CONV_CHUNK, CONV_CHUNK)
        cols = pl.ds(c0, CONV_CHUNK)
        conv_sum = conv_chunk(x_ref, wt_ref, lo_ref[:, cols], hi_ref[:, cols], c0, 1)
        spread = jnp.sqrt(jnp.mean(conv_sum * conv_sum, axis=0, keepdims=True) + 1e-05)
        normed = conv_sum / spread
        pre_act = normed * gain
        gate = 1.0 / (1.0 + jnp.exp(-pre_act))
        out_ref[:, cols] = (pre_act * gate).astype(out_ref.dtype)
        grad_pre = cot_ref[:, cols].astype(jnp.float32) * gate * (1.0 + pre_act * (1.0 - gate))
        weighted = grad_pre * gain
        gc_ref[:, cols] = (
            weighted - normed * jnp.mean(weighted * normed, axis=0, keepdims=True)
        ) / spread
        return carry

    lax.fori_loop(0, out_ref.shape[1] // CONV_CHUNK, body, 0)


def conv_backward_kernel(y_ref, wt_ref, att_ref, lo_ref, hi_ref, ga_ref, delta_ref):
    def body(c, carry):
        c0 = pl.multiple_of(c * CONV_CHUNK, CONV_CHUNK)
        cols = pl.ds(c0, CONV_CHUNK)
        grad_sum = conv_chunk(y_ref, wt_ref, lo_ref[:, cols], hi_ref[:, cols], c0, -1)
        grad_att = grad_sum.astype(ga_ref.dtype)
        ga_ref[:, cols] = grad_att
        delta_ref[:, cols] = jnp.sum(
            grad_att.astype(jnp.float32) * att_ref[:, cols].astype(jnp.float32),
            axis=0,
            keepdims=True,
        )
        return carry

    lax.fori_loop(0, ga_ref.shape[1] // CONV_CHUNK, body, 0)


def padded_rims(block, half):
    count = lax.axis_size("blk")
    forward = [(i, i + 1) for i in range(count - 1)]
    backward = [(target, source) for source, target in forward]
    low = lax.ppermute(block[:, block.shape[1] - half :], "blk", forward)
    high = lax.ppermute(block[:, :half], "blk", backward)
    gap = jnp.zeros((block.shape[0], CONV_PAD - half), jnp.float32)
    return jnp.concatenate(
        [gap, low.astype(jnp.float32), block.astype(jnp.float32), high.astype(jnp.float32), gap],
        axis=1,
    )


def on_device(queries, keys, values, lengths, conv_weight, norm_gain, cotangent):
    rows_in, width = queries.shape
    heads_total = width // HEAD_DIM
    stacked = jnp.stack(
        [a.reshape(rows_in, heads_total, HEAD_DIM) for a in (queries, keys, values)], axis=2
    ).reshape(rows_in, heads_total * 3 * HEAD_DIM)
    local_qkv = lax.all_to_all(stacked, "uly", split_axis=1, concat_axis=0, tiled=True)
    local_qkv = local_qkv.reshape(local_qkv.shape[0], -1, 3, HEAD_DIM)
    local_q, local_k, local_v = (
        local_qkv[:, :, i].reshape(local_qkv.shape[0], -1) for i in range(3)
    )
    block_rows, channels = local_q.shape
    heads_here = channels // HEAD_DIM
    maxlen = block_rows // 2
    rows_q = min(512, block_rows)
    window = rows_q + 2 * maxlen
    conv_half = KERNEL // 2
    block_count = block_rows // rows_q
    score_scale = HEAD_DIM ** (-0.5)
    frame_total = lax.axis_size("blk") * block_rows
    first_frame = lax.axis_index("blk") * block_rows
    seg_ext = segment_ids(
        lengths,
        first_frame - maxlen + jnp.arange(block_rows + 2 * maxlen, dtype=jnp.int32),
        frame_total,
    )
    seg_own = seg_ext[maxlen : maxlen + block_rows]
    seg_conv = seg_ext[maxlen - conv_half : maxlen + block_rows + conv_half]
    near_pairs = extended(jnp.concatenate([local_k, local_v], axis=1), (("blk", 0),), maxlen)
    k_ext = near_pairs[:, :channels].reshape(-1, heads_here, HEAD_DIM)
    v_ext = near_pairs[:, channels:].reshape(-1, heads_here, HEAD_DIM)
    q_heads = local_q.reshape(block_rows, heads_here, HEAD_DIM)
    starts = jnp.arange(block_count, dtype=jnp.int32) * rows_q

    assert heads_here == 1
    lo_t, hi_t = tile_ranges(lengths, first_frame - maxlen, block_rows + 2 * maxlen, block_rows)
    qseg_col = seg_own[:, None].astype(jnp.int32)
    kseg_row = seg_ext[None, :].astype(jnp.int32)
    k_flat = k_ext.reshape(-1, HEAD_DIM)
    v_flat = v_ext.reshape(-1, HEAD_DIM)
    attended, row_tops, row_totals = vmem_call(
        forward_kernel,
        2,
        5,
        (
            jax.ShapeDtypeStruct((block_rows, HEAD_DIM), jnp.bfloat16),
            jax.ShapeDtypeStruct((block_rows, 1), jnp.float32),
            jax.ShapeDtypeStruct((block_rows, 1), jnp.float32),
        ),
    )(lo_t, hi_t, local_q, k_flat, with_ones(v_flat), qseg_col, kseg_row)
    frame_at = first_frame + jnp.arange(block_rows, dtype=jnp.int32)
    seg_start, seg_end = segment_bounds(lengths, frame_at)
    lo_off = (seg_start - frame_at)[None, :].astype(jnp.int32)
    hi_off = (seg_end - frame_at)[None, :].astype(jnp.int32)
    weight_t = conv_weight.T
    att_t = attended.T
    conv_out_t, grad_conv_t = vmem_call(
        conv_forward_kernel,
        0,
        6,
        (
            jax.ShapeDtypeStruct((HEAD_DIM, block_rows), jnp.bfloat16),
            jax.ShapeDtypeStruct((HEAD_DIM, block_rows), jnp.float32),
        ),
    )(padded_rims(att_t, conv_half), weight_t, norm_gain[:, None], cotangent, lo_off, hi_off)
    grad_att_t, delta_row = vmem_call(
        conv_backward_kernel,
        0,
        5,
        (
            jax.ShapeDtypeStruct((HEAD_DIM, block_rows), jnp.bfloat16),
            jax.ShapeDtypeStruct((1, block_rows), jnp.float32),
        ),
    )(padded_rims(grad_conv_t, conv_half), weight_t, att_t, lo_off, hi_off)
    grad_attended = grad_att_t.T
    row_delta = delta_row.T

    ext_rows = block_rows + 2 * maxlen
    grad_q, dk_t, dv_t = vmem_call(
        backward_kernel,
        2,
        10,
        (
            jax.ShapeDtypeStruct((block_rows, HEAD_DIM), jnp.bfloat16),
            jax.ShapeDtypeStruct((HEAD_DIM, ext_rows), jnp.float32),
            jax.ShapeDtypeStruct((HEAD_DIM, ext_rows), jnp.float32),
        ),
    )(
        lo_t,
        hi_t,
        local_q,
        k_flat,
        v_flat,
        grad_attended,
        local_q.T,
        grad_att_t,
        qseg_col,
        kseg_row,
        row_tops + jnp.log(row_totals),
        row_delta,
    )
    ext_terms = jnp.concatenate([dk_t, dv_t], axis=0)
    received = []
    for rim_part, direction in ((ext_terms[:, :maxlen], -1), (ext_terms[:, maxlen + block_rows :], 1)):
        received.append(
            passed_along(rim_part.astype(jnp.bfloat16), "blk", direction).astype(rim_part.dtype)
        )
    key_grads = ext_terms[:, maxlen : maxlen + block_rows] + jnp.concatenate(
        [received[1], received[0]], axis=1
    )
    grad_queries = grad_q.reshape(block_rows, channels)
    grad_keys = key_grads[:HEAD_DIM].astype(jnp.bfloat16)
    grad_values = key_grads[HEAD_DIM:].astype(jnp.bfloat16)
    return (conv_out_t, grad_queries.T, grad_keys, grad_values)


def solution(mesh):
    in_specs = (
        P(("blk", "uly"), None),
        P(("blk", "uly"), None),
        P(("blk", "uly"), None),
        P(),
        P(None, "uly"),
        P("uly"),
        P("uly", "blk"),
    )
    out_specs = (P("uly", "blk"), P("uly", "blk"), P("uly", "blk"), P("uly", "blk"))
    return jax.shard_map(
        on_device, mesh=mesh, in_specs=in_specs, out_specs=out_specs, check_vma=False
    )
```

```python
import jax
import jax.numpy as jnp
import functools
from jax import lax
from jax.experimental import pallas as pl
from jax.experimental.pallas import tpu as pltpu
from jax.sharding import PartitionSpec as P

KERNEL = 31
HEAD_DIM = 64


def extended(block, sides, width):
    for axis, dim in sides:
        count = lax.axis_size(axis)
        forward = [(i, i + 1) for i in range(count - 1)]
        backward = [(target, source) for source, target in forward]
        low = lax.ppermute(
            lax.slice_in_dim(block, block.shape[dim] - width, None, axis=dim), axis, forward
        )
        high = lax.ppermute(lax.slice_in_dim(block, 0, width, axis=dim), axis, backward)
        block = jnp.concatenate([low, block, high], axis=dim)
    return block


def passed_along(block, axis, distance):
    devices = range(lax.axis_size(axis))
    route = [(i - distance, i) for i in devices if i - distance in devices]
    return lax.ppermute(block, axis, route)


def segment_ids(lengths, frames, frame_total):
    starts = jnp.cumsum(lengths) - lengths
    seg_ids = jnp.sum((starts[None, :] <= frames[:, None]).astype(jnp.int32), axis=1) - 1
    inside = (frames >= 0) & (frames < frame_total)
    return jnp.where(inside, seg_ids, -1)


def rows_at(values_in, row_start, row_count):
    return lax.dynamic_slice_in_dim(values_in, row_start, row_count, 0)


def masked_scores(query_rows, key_rows, query_seg, key_seg):
    scores = HEAD_DIM ** (-0.5) * jnp.einsum(
        "rhe,she->hrs", query_rows, key_rows, preferred_element_type=jnp.float32
    )
    same_seg = (query_seg[:, None] == key_seg[None, :])[None]
    return (scores, same_seg)


def weights_of(scores, same_seg, row_top, row_total):
    return jnp.where(same_seg, jnp.exp(scores - row_top), 0.0) / row_total


TILE_Q = 512
TILE_K = 512
NT = (((1,), (1,)), ((), ()))
TN = (((0,), (0,)), ((), ()))


def forward_kernel(lo_ref, hi_ref, q_ref, kv_ref, qseg_ref, kseg_ref, o_ref, m_ref, l_ref):
    scale = HEAD_DIM ** (-0.5)

    def q_body(i, carry):
        r0 = pl.multiple_of(i * TILE_Q, TILE_Q)
        q = q_ref[pl.ds(r0, TILE_Q), :] * jnp.asarray(scale, q_ref.dtype)
        qs = qseg_ref[pl.ds(r0, TILE_Q), :]

        def k_body(j, c):
            m, l, acc = c
            c0 = pl.multiple_of(j * TILE_K, TILE_K)
            kv = kv_ref[pl.ds(c0, TILE_K), :]
            ks = kseg_ref[:, pl.ds(c0, TILE_K)]
            s = lax.dot_general(q, kv, NT, preferred_element_type=jnp.float32)
            s = jnp.where(qs == ks, s, -1e30)
            m_new = jnp.maximum(m, jnp.max(s, axis=1, keepdims=True))
            alpha = jnp.exp(m - m_new)
            p = jnp.exp(s - m_new)
            l = alpha * l + jnp.sum(p, axis=1, keepdims=True)
            acc = alpha * acc + jnp.dot(
                p.astype(jnp.bfloat16), kv, preferred_element_type=jnp.float32
            )
            return (m_new, l, acc)

        init = (
            jnp.full((TILE_Q, 1), -1e30, jnp.float32),
            jnp.zeros((TILE_Q, 1), jnp.float32),
            jnp.zeros((TILE_Q, kv_ref.shape[1]), jnp.float32),
        )
        m, l, acc = lax.fori_loop(lo_ref[i], hi_ref[i], k_body, init)
        o_ref[pl.ds(r0, TILE_Q), :] = (acc[:, HEAD_DIM:] / l).astype(o_ref.dtype)
        m_ref[pl.ds(r0, TILE_Q), :] = m
        l_ref[pl.ds(r0, TILE_Q), :] = l
        return carry

    lax.fori_loop(0, q_ref.shape[0] // TILE_Q, q_body, 0)


def backward_kernel(
    lo_ref, hi_ref, q_ref, kv_ref, do_ref, qt_ref, dot_ref, qseg_ref, kseg_ref, lse_ref,
    d_ref, dq_ref, dk_ref, dv_ref,
):
    scale = HEAD_DIM ** (-0.5)
    dk_ref[...] = jnp.zeros_like(dk_ref)
    dv_ref[...] = jnp.zeros_like(dv_ref)

    def q_body(i, carry):
        r0 = pl.multiple_of(i * TILE_Q, TILE_Q)
        q = q_ref[pl.ds(r0, TILE_Q), :] * jnp.asarray(scale, q_ref.dtype)
        do = do_ref[pl.ds(r0, TILE_Q), :]
        qs = qseg_ref[pl.ds(r0, TILE_Q), :]
        lse = lse_ref[pl.ds(r0, TILE_Q), :]
        dlt = d_ref[pl.ds(r0, TILE_Q), :]
        q_t = qt_ref[:, pl.ds(r0, TILE_Q)]
        do_t = dot_ref[:, pl.ds(r0, TILE_Q)]

        def k_body(j, dq):
            c0 = pl.multiple_of(j * TILE_K, TILE_K)
            kv = kv_ref[pl.ds(c0, TILE_K), :]
            ks = kseg_ref[:, pl.ds(c0, TILE_K)]
            s = lax.dot_general(q, kv, NT, preferred_element_type=jnp.float32)
            p = jnp.exp(jnp.where(qs == ks, s, -1e30) - lse)
            dp = lax.dot_general(do, kv, NT, preferred_element_type=jnp.float32)
            ds = (p * (dp - dlt)).astype(jnp.bfloat16)
            dk_ref[:, pl.ds(c0, TILE_K)] += jnp.dot(q_t, ds, preferred_element_type=jnp.float32)
            dv_ref[:, pl.ds(c0, TILE_K)] += jnp.dot(
                do_t, p.astype(jnp.bfloat16), preferred_element_type=jnp.float32
            )
            return dq + jnp.dot(ds, kv, preferred_element_type=jnp.float32)

        dq = lax.fori_loop(
            lo_ref[i], hi_ref[i], k_body, jnp.zeros((TILE_Q, kv_ref.shape[1]), jnp.float32)
        )
        dq_ref[pl.ds(r0, TILE_Q), :] = (scale * dq[:, :HEAD_DIM]).astype(dq_ref.dtype)
        return carry

    lax.fori_loop(0, q_ref.shape[0] // TILE_Q, q_body, 0)
    dk_ref[...] = scale * dk_ref[...]


def vmem_call(kernel, n_smem, n_vmem, out_shape):
    return pl.pallas_call(
        kernel,
        out_shape=out_shape,
        in_specs=[pl.BlockSpec(memory_space=pltpu.SMEM)] * n_smem
        + [pl.BlockSpec(memory_space=pltpu.VMEM)] * n_vmem,
        out_specs=[pl.BlockSpec(memory_space=pltpu.VMEM)] * len(out_shape),
    )


def segment_bounds(lengths, frames):
    ends = jnp.cumsum(lengths)
    starts = ends - lengths
    seg_start = jnp.max(jnp.where(starts[None, :] <= frames[:, None], starts[None, :], 0), axis=1)
    big = jnp.iinfo(jnp.int32).max
    seg_end = jnp.min(jnp.where(ends[None, :] > frames[:, None], ends[None, :], big), axis=1)
    return (seg_start, jnp.minimum(seg_end, ends[-1]))


def tile_ranges(lengths, base, ext_rows, block_rows):
    frames = base + (ext_rows - block_rows) // 2 + jnp.arange(block_rows, dtype=jnp.int32)
    seg_start, seg_end = segment_bounds(lengths, frames)
    lo = (seg_start[::TILE_Q] - base) // TILE_K
    hi = (seg_end[TILE_Q - 1 :: TILE_Q] - base + TILE_K - 1) // TILE_K
    lo = jnp.clip(lo, 0, ext_rows // TILE_K).astype(jnp.int32)
    hi = jnp.clip(hi, lo, ext_rows // TILE_K).astype(jnp.int32)
    return (lo, hi)


CONV_PAD = 128
CONV_CHUNK = 256


def conv_chunk(x_ref, wt_ref, lo, hi, c0, sign):
    window = x_ref[:, pl.ds(c0, CONV_CHUNK + 2 * CONV_PAD)]
    width = window.shape[1]
    total = jnp.zeros((window.shape[0], CONV_CHUNK), jnp.float32)
    for tap in range(KERNEL):
        d = sign * (tap - KERNEL // 2)
        shifted = pltpu.roll(window, (width - d) % width, 1) if d else window
        keep = (lo <= d) & (d < hi)
        total = total + wt_ref[:, tap : tap + 1] * jnp.where(
            keep, shifted[:, CONV_PAD : CONV_PAD + CONV_CHUNK], 0.0
        )
    return total


def conv_forward_kernel(x_ref, wt_ref, gain_ref, cot_ref, lo_ref, hi_ref, out_ref, gc_ref):
    gain = gain_ref[...]

    def body(c, carry):
        c0 = pl.multiple_of(c * CONV_CHUNK, CONV_CHUNK)
        cols = pl.ds(c0, CONV_CHUNK)
        conv_sum = conv_chunk(x_ref, wt_ref, lo_ref[:, cols], hi_ref[:, cols], c0, 1)
        spread = jnp.sqrt(jnp.mean(conv_sum * conv_sum, axis=0, keepdims=True) + 1e-05)
        normed = conv_sum / spread
        pre_act = normed * gain
        gate = 1.0 / (1.0 + jnp.exp(-pre_act))
        out_ref[:, cols] = (pre_act * gate).astype(out_ref.dtype)
        grad_pre = cot_ref[:, cols].astype(jnp.float32) * gate * (1.0 + pre_act * (1.0 - gate))
        weighted = grad_pre * gain
        gc_ref[:, cols] = (
            weighted - normed * jnp.mean(weighted * normed, axis=0, keepdims=True)
        ) / spread
        return carry

    lax.fori_loop(0, out_ref.shape[1] // CONV_CHUNK, body, 0)


def conv_backward_kernel(y_ref, wt_ref, att_ref, lo_ref, hi_ref, ga_ref, delta_ref):
    def body(c, carry):
        c0 = pl.multiple_of(c * CONV_CHUNK, CONV_CHUNK)
        cols = pl.ds(c0, CONV_CHUNK)
        grad_sum = conv_chunk(y_ref, wt_ref, lo_ref[:, cols], hi_ref[:, cols], c0, -1)
        grad_att = grad_sum.astype(ga_ref.dtype)
        ga_ref[:, cols] = grad_att
        delta_ref[:, cols] = jnp.sum(
            grad_att.astype(jnp.float32) * att_ref[:, cols].astype(jnp.float32),
            axis=0,
            keepdims=True,
        )
        return carry

    lax.fori_loop(0, ga_ref.shape[1] // CONV_CHUNK, body, 0)


def padded_rims(block, half):
    count = lax.axis_size("blk")
    forward = [(i, i + 1) for i in range(count - 1)]
    backward = [(target, source) for source, target in forward]
    low = lax.ppermute(block[:, block.shape[1] - half :], "blk", forward)
    high = lax.ppermute(block[:, :half], "blk", backward)
    gap = jnp.zeros((block.shape[0], CONV_PAD - half), jnp.float32)
    return jnp.concatenate(
        [gap, low.astype(jnp.float32), block.astype(jnp.float32), high.astype(jnp.float32), gap],
        axis=1,
    )


def on_device(queries, keys, values, lengths, conv_weight, norm_gain, cotangent):
    rows_in, width = queries.shape
    heads_total = width // HEAD_DIM
    stacked = jnp.stack(
        [a.reshape(rows_in, heads_total, HEAD_DIM) for a in (queries, keys, values)], axis=2
    ).reshape(rows_in, heads_total * 3 * HEAD_DIM)
    local_qkv = lax.all_to_all(stacked, "uly", split_axis=1, concat_axis=0, tiled=True)
    local_qkv = local_qkv.reshape(local_qkv.shape[0], -1, 3, HEAD_DIM)
    local_q, local_k, local_v = (
        local_qkv[:, :, i].reshape(local_qkv.shape[0], -1) for i in range(3)
    )
    block_rows, channels = local_q.shape
    heads_here = channels // HEAD_DIM
    maxlen = block_rows // 2
    rows_q = min(512, block_rows)
    window = rows_q + 2 * maxlen
    conv_half = KERNEL // 2
    block_count = block_rows // rows_q
    score_scale = HEAD_DIM ** (-0.5)
    frame_total = lax.axis_size("blk") * block_rows
    first_frame = lax.axis_index("blk") * block_rows
    seg_ext = segment_ids(
        lengths,
        first_frame - maxlen + jnp.arange(block_rows + 2 * maxlen, dtype=jnp.int32),
        frame_total,
    )
    seg_own = seg_ext[maxlen : maxlen + block_rows]
    seg_conv = seg_ext[maxlen - conv_half : maxlen + block_rows + conv_half]
    near_pairs = extended(jnp.concatenate([local_k, local_v], axis=1), (("blk", 0),), maxlen)
    k_ext = near_pairs[:, :channels].reshape(-1, heads_here, HEAD_DIM)
    v_ext = near_pairs[:, channels:].reshape(-1, heads_here, HEAD_DIM)
    q_heads = local_q.reshape(block_rows, heads_here, HEAD_DIM)
    starts = jnp.arange(block_count, dtype=jnp.int32) * rows_q

    assert heads_here == 1
    lo_t, hi_t = tile_ranges(lengths, first_frame - maxlen, block_rows + 2 * maxlen, block_rows)
    qseg_col = seg_own[:, None].astype(jnp.int32)
    kseg_row = seg_ext[None, :].astype(jnp.int32)
    lane_gap = jnp.zeros((block_rows, HEAD_DIM), jnp.bfloat16)
    q_wide = jnp.concatenate([local_q, lane_gap], axis=1)
    attended, row_tops, row_totals = vmem_call(
        forward_kernel,
        2,
        4,
        (
            jax.ShapeDtypeStruct((block_rows, HEAD_DIM), jnp.bfloat16),
            jax.ShapeDtypeStruct((block_rows, 1), jnp.float32),
            jax.ShapeDtypeStruct((block_rows, 1), jnp.float32),
        ),
    )(lo_t, hi_t, q_wide, near_pairs, qseg_col, kseg_row)
    frame_at = first_frame + jnp.arange(block_rows, dtype=jnp.int32)
    seg_start, seg_end = segment_bounds(lengths, frame_at)
    lo_off = (seg_start - frame_at)[None, :].astype(jnp.int32)
    hi_off = (seg_end - frame_at)[None, :].astype(jnp.int32)
    weight_t = conv_weight.T
    att_t = attended.T
    conv_out_t, grad_conv_t = vmem_call(
        conv_forward_kernel,
        0,
        6,
        (
            jax.ShapeDtypeStruct((HEAD_DIM, block_rows), jnp.bfloat16),
            jax.ShapeDtypeStruct((HEAD_DIM, block_rows), jnp.float32),
        ),
    )(padded_rims(att_t, conv_half), weight_t, norm_gain[:, None], cotangent, lo_off, hi_off)
    grad_att_t, delta_row = vmem_call(
        conv_backward_kernel,
        0,
        5,
        (
            jax.ShapeDtypeStruct((HEAD_DIM, block_rows), jnp.bfloat16),
            jax.ShapeDtypeStruct((1, block_rows), jnp.float32),
        ),
    )(padded_rims(grad_conv_t, conv_half), weight_t, att_t, lo_off, hi_off)
    grad_attended = grad_att_t.T
    row_delta = delta_row.T

    ext_rows = block_rows + 2 * maxlen
    grad_q, dk_t, dv_t = vmem_call(
        backward_kernel,
        2,
        9,
        (
            jax.ShapeDtypeStruct((block_rows, HEAD_DIM), jnp.bfloat16),
            jax.ShapeDtypeStruct((HEAD_DIM, ext_rows), jnp.float32),
            jax.ShapeDtypeStruct((HEAD_DIM, ext_rows), jnp.float32),
        ),
    )(
        lo_t,
        hi_t,
        q_wide,
        near_pairs,
        jnp.concatenate([lane_gap, grad_attended], axis=1),
        local_q.T,
        grad_att_t,
        qseg_col,
        kseg_row,
        row_tops + jnp.log(row_totals),
        row_delta,
    )
    ext_terms = jnp.concatenate([dk_t, dv_t], axis=0)
    received = []
    for rim_part, direction in ((ext_terms[:, :maxlen], -1), (ext_terms[:, maxlen + block_rows :], 1)):
        received.append(
            passed_along(rim_part.astype(jnp.bfloat16), "blk", direction).astype(rim_part.dtype)
        )
    key_grads = ext_terms[:, maxlen : maxlen + block_rows] + jnp.concatenate(
        [received[1], received[0]], axis=1
    )
    grad_queries = grad_q.reshape(block_rows, channels)
    grad_keys = key_grads[:HEAD_DIM].astype(jnp.bfloat16)
    grad_values = key_grads[HEAD_DIM:].astype(jnp.bfloat16)
    return (conv_out_t, grad_queries.T, grad_keys, grad_values)


def solution(mesh):
    in_specs = (
        P(("blk", "uly"), None),
        P(("blk", "uly"), None),
        P(("blk", "uly"), None),
        P(),
        P(None, "uly"),
        P("uly"),
        P("uly", "blk"),
    )
    out_specs = (P("uly", "blk"), P("uly", "blk"), P("uly", "blk"), P("uly", "blk"))
    return jax.shard_map(
        on_device, mesh=mesh, in_specs=in_specs, out_specs=out_specs, check_vma=False
    )
```

```python
import jax
import jax.numpy as jnp
import functools
from jax import lax
from jax.experimental import pallas as pl
from jax.experimental.pallas import tpu as pltpu
from jax.sharding import PartitionSpec as P

KERNEL = 31
HEAD_DIM = 64


def extended(block, sides, width):
    for axis, dim in sides:
        count = lax.axis_size(axis)
        forward = [(i, i + 1) for i in range(count - 1)]
        backward = [(target, source) for source, target in forward]
        low = lax.ppermute(
            lax.slice_in_dim(block, block.shape[dim] - width, None, axis=dim), axis, forward
        )
        high = lax.ppermute(lax.slice_in_dim(block, 0, width, axis=dim), axis, backward)
        block = jnp.concatenate([low, block, high], axis=dim)
    return block


def passed_along(block, axis, distance):
    devices = range(lax.axis_size(axis))
    route = [(i - distance, i) for i in devices if i - distance in devices]
    return lax.ppermute(block, axis, route)


def segment_ids(lengths, frames, frame_total):
    starts = jnp.cumsum(lengths) - lengths
    seg_ids = jnp.sum((starts[None, :] <= frames[:, None]).astype(jnp.int32), axis=1) - 1
    inside = (frames >= 0) & (frames < frame_total)
    return jnp.where(inside, seg_ids, -1)


def rows_at(values_in, row_start, row_count):
    return lax.dynamic_slice_in_dim(values_in, row_start, row_count, 0)


def masked_scores(query_rows, key_rows, query_seg, key_seg):
    scores = HEAD_DIM ** (-0.5) * jnp.einsum(
        "rhe,she->hrs", query_rows, key_rows, preferred_element_type=jnp.float32
    )
    same_seg = (query_seg[:, None] == key_seg[None, :])[None]
    return (scores, same_seg)


def weights_of(scores, same_seg, row_top, row_total):
    return jnp.where(same_seg, jnp.exp(scores - row_top), 0.0) / row_total


TILE_Q = 512
TILE_K = 512
NT = (((1,), (1,)), ((), ()))
TN = (((0,), (0,)), ((), ()))


def forward_kernel(lo_ref, hi_ref, q_ref, kv_ref, qseg_ref, kseg_ref, o_ref, lse_ref):
    scale = HEAD_DIM ** (-0.5)

    def q_body(i, carry):
        r0 = pl.multiple_of(i * TILE_Q, TILE_Q)
        q = q_ref[pl.ds(r0, TILE_Q), :] * jnp.asarray(scale, q_ref.dtype)
        qs = qseg_ref[pl.ds(r0, TILE_Q), :]

        def k_body(j, c):
            m, l, acc = c
            c0 = pl.multiple_of(j * TILE_K, TILE_K)
            kv = kv_ref[pl.ds(c0, TILE_K), :]
            ks = kseg_ref[:, pl.ds(c0, TILE_K)]
            s = lax.dot_general(q, kv, NT, preferred_element_type=jnp.float32)
            s = jnp.where(qs == ks, s, -1e30)
            m_new = jnp.maximum(m, jnp.max(s, axis=1, keepdims=True))
            alpha = jnp.exp(m - m_new)
            p = jnp.exp(s - m_new)
            l = alpha * l + jnp.sum(p, axis=1, keepdims=True)
            acc = alpha * acc + jnp.dot(
                p.astype(jnp.bfloat16), kv, preferred_element_type=jnp.float32
            )
            return (m_new, l, acc)

        init = (
            jnp.full((TILE_Q, 1), -1e30, jnp.float32),
            jnp.zeros((TILE_Q, 1), jnp.float32),
            jnp.zeros((TILE_Q, kv_ref.shape[1]), jnp.float32),
        )
        m, l, acc = lax.fori_loop(lo_ref[i], hi_ref[i], k_body, init)
        o_ref[:, pl.ds(r0, TILE_Q)] = (acc / l).T[HEAD_DIM:].astype(o_ref.dtype)
        lse_ref[pl.ds(r0, TILE_Q), :] = m + jnp.log(l)
        return carry

    lax.fori_loop(0, q_ref.shape[0] // TILE_Q, q_body, 0)


def backward_kernel(
    lo_ref, hi_ref, q_ref, kv_ref, do_ref, qt_ref, dot_ref, qseg_ref, kseg_ref, lse_ref,
    d_ref, dq_ref, dk_ref, dv_ref,
):
    scale = HEAD_DIM ** (-0.5)
    dk_ref[...] = jnp.zeros_like(dk_ref)
    dv_ref[...] = jnp.zeros_like(dv_ref)

    def q_body(i, carry):
        r0 = pl.multiple_of(i * TILE_Q, TILE_Q)
        q = q_ref[pl.ds(r0, TILE_Q), :] * jnp.asarray(scale, q_ref.dtype)
        do = do_ref[pl.ds(r0, TILE_Q), :]
        qs = qseg_ref[pl.ds(r0, TILE_Q), :]
        lse = lse_ref[pl.ds(r0, TILE_Q), :]
        dlt = d_ref[pl.ds(r0, TILE_Q), :]
        q_t = qt_ref[:, pl.ds(r0, TILE_Q)]
        do_t = dot_ref[:, pl.ds(r0, TILE_Q)]

        def k_body(j, dq):
            c0 = pl.multiple_of(j * TILE_K, TILE_K)
            kv = kv_ref[pl.ds(c0, TILE_K), :]
            ks = kseg_ref[:, pl.ds(c0, TILE_K)]
            s = lax.dot_general(q, kv, NT, preferred_element_type=jnp.float32)
            p = jnp.exp(jnp.where(qs == ks, s, -1e30) - lse)
            dp = lax.dot_general(do, kv, NT, preferred_element_type=jnp.float32)
            ds = (p * (dp - dlt)).astype(jnp.bfloat16)
            dk_ref[:, pl.ds(c0, TILE_K)] += jnp.dot(q_t, ds, preferred_element_type=jnp.float32)
            dv_ref[:, pl.ds(c0, TILE_K)] += jnp.dot(
                do_t, p.astype(jnp.bfloat16), preferred_element_type=jnp.float32
            )
            return dq + jnp.dot(ds, kv, preferred_element_type=jnp.float32)

        dq = lax.fori_loop(
            lo_ref[i], hi_ref[i], k_body, jnp.zeros((TILE_Q, kv_ref.shape[1]), jnp.float32)
        )
        dq_ref[pl.ds(r0, TILE_Q), :] = (scale * dq[:, :HEAD_DIM]).astype(dq_ref.dtype)
        return carry

    lax.fori_loop(0, q_ref.shape[0] // TILE_Q, q_body, 0)
    dk_ref[...] = scale * dk_ref[...]


def vmem_call(kernel, n_smem, n_vmem, out_shape):
    return pl.pallas_call(
        kernel,
        out_shape=out_shape,
        in_specs=[pl.BlockSpec(memory_space=pltpu.SMEM)] * n_smem
        + [pl.BlockSpec(memory_space=pltpu.VMEM)] * n_vmem,
        out_specs=[pl.BlockSpec(memory_space=pltpu.VMEM)] * len(out_shape),
    )


def segment_bounds(lengths, frames):
    ends = jnp.cumsum(lengths)
    starts = ends - lengths
    seg_start = jnp.max(jnp.where(starts[None, :] <= frames[:, None], starts[None, :], 0), axis=1)
    big = jnp.iinfo(jnp.int32).max
    seg_end = jnp.min(jnp.where(ends[None, :] > frames[:, None], ends[None, :], big), axis=1)
    return (seg_start, jnp.minimum(seg_end, ends[-1]))


def tile_ranges(lengths, base, ext_rows, block_rows):
    frames = base + (ext_rows - block_rows) // 2 + jnp.arange(block_rows, dtype=jnp.int32)
    seg_start, seg_end = segment_bounds(lengths, frames)
    lo = (seg_start[::TILE_Q] - base) // TILE_K
    hi = (seg_end[TILE_Q - 1 :: TILE_Q] - base + TILE_K - 1) // TILE_K
    lo = jnp.clip(lo, 0, ext_rows // TILE_K).astype(jnp.int32)
    hi = jnp.clip(hi, lo, ext_rows // TILE_K).astype(jnp.int32)
    return (lo, hi)


CONV_PAD = 128
CONV_CHUNK = 256


def conv_chunk(x_ref, wt_ref, lo, hi, c0, sign):
    window = x_ref[:, pl.ds(c0, CONV_CHUNK + 2 * CONV_PAD)]
    width = window.shape[1]
    total = jnp.zeros((window.shape[0], CONV_CHUNK), jnp.float32)
    for tap in range(KERNEL):
        d = sign * (tap - KERNEL // 2)
        shifted = pltpu.roll(window, (width - d) % width, 1) if d else window
        keep = (lo <= d) & (d < hi)
        total = total + wt_ref[:, tap : tap + 1] * jnp.where(
            keep, shifted[:, CONV_PAD : CONV_PAD + CONV_CHUNK], 0.0
        )
    return total


def conv_forward_kernel(x_ref, wt_ref, gain_ref, cot_ref, lo_ref, hi_ref, out_ref, gc_ref):
    gain = gain_ref[...]

    def body(c, carry):
        c0 = pl.multiple_of(c * CONV_CHUNK, CONV_CHUNK)
        cols = pl.ds(c0, CONV_CHUNK)
        conv_sum = conv_chunk(x_ref, wt_ref, lo_ref[:, cols], hi_ref[:, cols], c0, 1)
        spread = jnp.sqrt(jnp.mean(conv_sum * conv_sum, axis=0, keepdims=True) + 1e-05)
        normed = conv_sum / spread
        pre_act = normed * gain
        gate = 1.0 / (1.0 + jnp.exp(-pre_act))
        out_ref[:, cols] = (pre_act * gate).astype(out_ref.dtype)
        grad_pre = cot_ref[:, cols].astype(jnp.float32) * gate * (1.0 + pre_act * (1.0 - gate))
        weighted = grad_pre * gain
        gc_ref[:, cols] = (
            weighted - normed * jnp.mean(weighted * normed, axis=0, keepdims=True)
        ) / spread
        return carry

    lax.fori_loop(0, out_ref.shape[1] // CONV_CHUNK, body, 0)


def conv_backward_kernel(y_ref, wt_ref, att_ref, lo_ref, hi_ref, ga_ref, dop_ref, delta_ref):
    def body(c, carry):
        c0 = pl.multiple_of(c * CONV_CHUNK, CONV_CHUNK)
        cols = pl.ds(c0, CONV_CHUNK)
        grad_sum = conv_chunk(y_ref, wt_ref, lo_ref[:, cols], hi_ref[:, cols], c0, -1)
        grad_att = grad_sum.astype(ga_ref.dtype)
        ga_ref[:, cols] = grad_att
        grad_f32 = grad_att.astype(jnp.float32)
        delta = jnp.sum(grad_f32 * att_ref[:, cols].astype(jnp.float32), axis=0, keepdims=True)
        rows = pl.ds(c0, CONV_CHUNK)
        delta_ref[rows, :] = jnp.broadcast_to(delta, (8, CONV_CHUNK)).T[:, :1]
        wide = jnp.concatenate([jnp.zeros_like(grad_f32), grad_f32], axis=0)
        dop_ref[rows, :] = wide.T.astype(dop_ref.dtype)
        return carry

    lax.fori_loop(0, ga_ref.shape[1] // CONV_CHUNK, body, 0)


def padded_rims(block, half):
    count = lax.axis_size("blk")
    forward = [(i, i + 1) for i in range(count - 1)]
    backward = [(target, source) for source, target in forward]
    low = lax.ppermute(block[:, block.shape[1] - half :], "blk", forward)
    high = lax.ppermute(block[:, :half], "blk", backward)
    gap = jnp.zeros((block.shape[0], CONV_PAD - half), jnp.float32)
    return jnp.concatenate(
        [gap, low.astype(jnp.float32), block.astype(jnp.float32), high.astype(jnp.float32), gap],
        axis=1,
    )


def on_device(queries, keys, values, lengths, conv_weight, norm_gain, cotangent):
    rows_in, width = queries.shape
    heads_total = width // HEAD_DIM
    stacked = jnp.stack(
        [a.reshape(rows_in, heads_total, HEAD_DIM) for a in (queries, keys, values)], axis=2
    ).reshape(rows_in, heads_total * 3 * HEAD_DIM)
    local_qkv = lax.all_to_all(stacked, "uly", split_axis=1, concat_axis=0, tiled=True)
    local_qkv = local_qkv.reshape(local_qkv.shape[0], -1, 3, HEAD_DIM)
    local_q, local_k, local_v = (
        local_qkv[:, :, i].reshape(local_qkv.shape[0], -1) for i in range(3)
    )
    block_rows, channels = local_q.shape
    heads_here = channels // HEAD_DIM
    maxlen = block_rows // 2
    rows_q = min(512, block_rows)
    window = rows_q + 2 * maxlen
    conv_half = KERNEL // 2
    block_count = block_rows // rows_q
    score_scale = HEAD_DIM ** (-0.5)
    frame_total = lax.axis_size("blk") * block_rows
    first_frame = lax.axis_index("blk") * block_rows
    seg_ext = segment_ids(
        lengths,
        first_frame - maxlen + jnp.arange(block_rows + 2 * maxlen, dtype=jnp.int32),
        frame_total,
    )
    seg_own = seg_ext[maxlen : maxlen + block_rows]
    seg_conv = seg_ext[maxlen - conv_half : maxlen + block_rows + conv_half]
    near_pairs = extended(jnp.concatenate([local_k, local_v], axis=1), (("blk", 0),), maxlen)
    k_ext = near_pairs[:, :channels].reshape(-1, heads_here, HEAD_DIM)
    v_ext = near_pairs[:, channels:].reshape(-1, heads_here, HEAD_DIM)
    q_heads = local_q.reshape(block_rows, heads_here, HEAD_DIM)
    starts = jnp.arange(block_count, dtype=jnp.int32) * rows_q

    assert heads_here == 1
    lo_t, hi_t = tile_ranges(lengths, first_frame - maxlen, block_rows + 2 * maxlen, block_rows)
    qseg_col = seg_own[:, None].astype(jnp.int32)
    kseg_row = seg_ext[None, :].astype(jnp.int32)
    lane_gap = jnp.zeros((block_rows, HEAD_DIM), jnp.bfloat16)
    q_wide = jnp.concatenate([local_q, lane_gap], axis=1)
    att_t, lse_col = vmem_call(
        forward_kernel,
        2,
        4,
        (
            jax.ShapeDtypeStruct((HEAD_DIM, block_rows), jnp.bfloat16),
            jax.ShapeDtypeStruct((block_rows, 1), jnp.float32),
        ),
    )(lo_t, hi_t, q_wide, near_pairs, qseg_col, kseg_row)
    frame_at = first_frame + jnp.arange(block_rows, dtype=jnp.int32)
    seg_start, seg_end = segment_bounds(lengths, frame_at)
    lo_off = (seg_start - frame_at)[None, :].astype(jnp.int32)
    hi_off = (seg_end - frame_at)[None, :].astype(jnp.int32)
    weight_t = conv_weight.T
    conv_out_t, grad_conv_t = vmem_call(
        conv_forward_kernel,
        0,
        6,
        (
            jax.ShapeDtypeStruct((HEAD_DIM, block_rows), jnp.bfloat16),
            jax.ShapeDtypeStruct((HEAD_DIM, block_rows), jnp.float32),
        ),
    )(padded_rims(att_t, conv_half), weight_t, norm_gain[:, None], cotangent, lo_off, hi_off)
    grad_att_t, grad_wide, row_delta = vmem_call(
        conv_backward_kernel,
        0,
        5,
        (
            jax.ShapeDtypeStruct((HEAD_DIM, block_rows), jnp.bfloat16),
            jax.ShapeDtypeStruct((block_rows, 2 * HEAD_DIM), jnp.bfloat16),
            jax.ShapeDtypeStruct((block_rows, 1), jnp.float32),
        ),
    )(padded_rims(grad_conv_t, conv_half), weight_t, att_t, lo_off, hi_off)

    ext_rows = block_rows + 2 * maxlen
    grad_q, dk_t, dv_t = vmem_call(
        backward_kernel,
        2,
        9,
        (
            jax.ShapeDtypeStruct((block_rows, HEAD_DIM), jnp.bfloat16),
            jax.ShapeDtypeStruct((HEAD_DIM, ext_rows), jnp.float32),
            jax.ShapeDtypeStruct((HEAD_DIM, ext_rows), jnp.float32),
        ),
    )(
        lo_t,
        hi_t,
        q_wide,
        near_pairs,
        grad_wide,
        local_q.T,
        grad_att_t,
        qseg_col,
        kseg_row,
        lse_col,
        row_delta,
    )
    ext_terms = jnp.concatenate([dk_t, dv_t], axis=0)
    received = []
    for rim_part, direction in ((ext_terms[:, :maxlen], -1), (ext_terms[:, maxlen + block_rows :], 1)):
        received.append(
            passed_along(rim_part.astype(jnp.bfloat16), "blk", direction).astype(rim_part.dtype)
        )
    key_grads = ext_terms[:, maxlen : maxlen + block_rows] + jnp.concatenate(
        [received[1], received[0]], axis=1
    )
    grad_queries = grad_q.reshape(block_rows, channels)
    grad_keys = key_grads[:HEAD_DIM].astype(jnp.bfloat16)
    grad_values = key_grads[HEAD_DIM:].astype(jnp.bfloat16)
    return (conv_out_t, grad_queries.T, grad_keys, grad_values)


def solution(mesh):
    in_specs = (
        P(("blk", "uly"), None),
        P(("blk", "uly"), None),
        P(("blk", "uly"), None),
        P(),
        P(None, "uly"),
        P("uly"),
        P("uly", "blk"),
    )
    out_specs = (P("uly", "blk"), P("uly", "blk"), P("uly", "blk"), P("uly", "blk"))
    return jax.shard_map(
        on_device, mesh=mesh, in_specs=in_specs, out_specs=out_specs, check_vma=False
    )
```

```python
import jax
import jax.numpy as jnp
import functools
from jax import lax
from jax.experimental import pallas as pl
from jax.experimental.pallas import tpu as pltpu
from jax.sharding import PartitionSpec as P

KERNEL = 31
HEAD_DIM = 64


def extended(block, sides, width):
    for axis, dim in sides:
        count = lax.axis_size(axis)
        forward = [(i, i + 1) for i in range(count - 1)]
        backward = [(target, source) for source, target in forward]
        low = lax.ppermute(
            lax.slice_in_dim(block, block.shape[dim] - width, None, axis=dim), axis, forward
        )
        high = lax.ppermute(lax.slice_in_dim(block, 0, width, axis=dim), axis, backward)
        block = jnp.concatenate([low, block, high], axis=dim)
    return block


def passed_along(block, axis, distance):
    devices = range(lax.axis_size(axis))
    route = [(i - distance, i) for i in devices if i - distance in devices]
    return lax.ppermute(block, axis, route)


def segment_ids(lengths, frames, frame_total):
    starts = jnp.cumsum(lengths) - lengths
    seg_ids = jnp.sum((starts[None, :] <= frames[:, None]).astype(jnp.int32), axis=1) - 1
    inside = (frames >= 0) & (frames < frame_total)
    return jnp.where(inside, seg_ids, -1)


def rows_at(values_in, row_start, row_count):
    return lax.dynamic_slice_in_dim(values_in, row_start, row_count, 0)


def masked_scores(query_rows, key_rows, query_seg, key_seg):
    scores = HEAD_DIM ** (-0.5) * jnp.einsum(
        "rhe,she->hrs", query_rows, key_rows, preferred_element_type=jnp.float32
    )
    same_seg = (query_seg[:, None] == key_seg[None, :])[None]
    return (scores, same_seg)


def weights_of(scores, same_seg, row_top, row_total):
    return jnp.where(same_seg, jnp.exp(scores - row_top), 0.0) / row_total


TILE_Q = 512
TILE_K = 512
NT = (((1,), (1,)), ((), ()))
TN = (((0,), (0,)), ((), ()))


def forward_kernel(lo_ref, hi_ref, q_ref, kv_ref, qseg_ref, kseg_ref, o_ref, lse_ref):
    scale = HEAD_DIM ** (-0.5)

    def q_body(i, carry):
        r0 = pl.multiple_of(i * TILE_Q, TILE_Q)
        q = q_ref[pl.ds(r0, TILE_Q), :] * jnp.asarray(scale, q_ref.dtype)
        qs = qseg_ref[pl.ds(r0, TILE_Q), :]

        def k_body(j, c):
            m, l, acc = c
            c0 = pl.multiple_of(j * TILE_K, TILE_K)
            kv = kv_ref[pl.ds(c0, TILE_K), :]
            ks = kseg_ref[:, pl.ds(c0, TILE_K)]
            s = lax.dot_general(q, kv, NT, preferred_element_type=jnp.float32)
            s = jnp.where(qs == ks, s, -1e30)
            m_new = jnp.maximum(m, jnp.max(s, axis=1, keepdims=True))
            alpha = jnp.exp(m - m_new)
            p = jnp.exp(s - m_new)
            l = alpha * l + jnp.sum(p, axis=1, keepdims=True)
            acc = alpha * acc + jnp.dot(
                p.astype(jnp.bfloat16), kv, preferred_element_type=jnp.float32
            )
            return (m_new, l, acc)

        init = (
            jnp.full((TILE_Q, 1), -1e30, jnp.float32),
            jnp.zeros((TILE_Q, 1), jnp.float32),
            jnp.zeros((TILE_Q, kv_ref.shape[1]), jnp.float32),
        )
        m, l, acc = lax.fori_loop(lo_ref[i], hi_ref[i], k_body, init)
        o_ref[:, pl.ds(r0, TILE_Q)] = (acc / l).T[HEAD_DIM:].astype(o_ref.dtype)
        lse_ref[pl.ds(r0, TILE_Q), :] = m + jnp.log(l)
        return carry

    lax.fori_loop(0, q_ref.shape[0] // TILE_Q, q_body, 0)


def backward_kernel(
    lo_ref, hi_ref, q_ref, kv_ref, do_ref, qt_ref, dot_ref, qseg_ref, kseg_ref, lse_ref,
    d_ref, dq_ref, dk_ref, dv_ref,
):
    scale = HEAD_DIM ** (-0.5)
    dk_ref[...] = jnp.zeros_like(dk_ref)
    dv_ref[...] = jnp.zeros_like(dv_ref)

    def q_body(i, carry):
        r0 = pl.multiple_of(i * TILE_Q, TILE_Q)
        q = q_ref[pl.ds(r0, TILE_Q), :] * jnp.asarray(scale, q_ref.dtype)
        do = do_ref[pl.ds(r0, TILE_Q), :]
        qs = qseg_ref[pl.ds(r0, TILE_Q), :]
        lse = lse_ref[pl.ds(r0, TILE_Q), :]
        dlt = d_ref[pl.ds(r0, TILE_Q), :]
        q_t = qt_ref[:, pl.ds(r0, TILE_Q)]
        do_t = dot_ref[:, pl.ds(r0, TILE_Q)]

        def k_body(j, dq):
            c0 = pl.multiple_of(j * TILE_K, TILE_K)
            kv = kv_ref[pl.ds(c0, TILE_K), :]
            ks = kseg_ref[:, pl.ds(c0, TILE_K)]
            s = lax.dot_general(q, kv, NT, preferred_element_type=jnp.float32)
            p = jnp.exp(jnp.where(qs == ks, s, -1e30) - lse)
            dp = lax.dot_general(do, kv, NT, preferred_element_type=jnp.float32)
            ds = (p * (dp - dlt)).astype(jnp.bfloat16)
            dk_ref[:, pl.ds(c0, TILE_K)] += jnp.dot(q_t, ds, preferred_element_type=jnp.float32)
            dv_ref[:, pl.ds(c0, TILE_K)] += jnp.dot(
                do_t, p.astype(jnp.bfloat16), preferred_element_type=jnp.float32
            )
            return dq + jnp.dot(ds, kv, preferred_element_type=jnp.float32)

        dq = lax.fori_loop(
            lo_ref[i], hi_ref[i], k_body, jnp.zeros((TILE_Q, kv_ref.shape[1]), jnp.float32)
        )
        dq_ref[pl.ds(r0, TILE_Q), :] = (scale * dq[:, :HEAD_DIM]).astype(dq_ref.dtype)
        return carry

    lax.fori_loop(0, q_ref.shape[0] // TILE_Q, q_body, 0)
    dk_ref[...] = scale * dk_ref[...]


def vmem_call(kernel, n_smem, n_vmem, out_shape):
    return pl.pallas_call(
        kernel,
        out_shape=out_shape,
        in_specs=[pl.BlockSpec(memory_space=pltpu.SMEM)] * n_smem
        + [pl.BlockSpec(memory_space=pltpu.VMEM)] * n_vmem,
        out_specs=[pl.BlockSpec(memory_space=pltpu.VMEM)] * len(out_shape),
    )


def segment_bounds(lengths, frames):
    ends = jnp.cumsum(lengths)
    starts = ends - lengths
    seg_start = jnp.max(jnp.where(starts[None, :] <= frames[:, None], starts[None, :], 0), axis=1)
    big = jnp.iinfo(jnp.int32).max
    seg_end = jnp.min(jnp.where(ends[None, :] > frames[:, None], ends[None, :], big), axis=1)
    return (seg_start, jnp.minimum(seg_end, ends[-1]))


def tile_ranges(lengths, base, ext_rows, block_rows):
    frames = base + (ext_rows - block_rows) // 2 + jnp.arange(block_rows, dtype=jnp.int32)
    seg_start, seg_end = segment_bounds(lengths, frames)
    lo = (seg_start[::TILE_Q] - base) // TILE_K
    hi = (seg_end[TILE_Q - 1 :: TILE_Q] - base + TILE_K - 1) // TILE_K
    lo = jnp.clip(lo, 0, ext_rows // TILE_K).astype(jnp.int32)
    hi = jnp.clip(hi, lo, ext_rows // TILE_K).astype(jnp.int32)
    return (lo, hi)


CONV_PAD = 128
CONV_CHUNK = 256


def conv_chunk(x_ref, wt_ref, lo, hi, c0, sign):
    window = x_ref[:, pl.ds(c0, CONV_CHUNK + 2 * CONV_PAD)]
    width = window.shape[1]
    total = jnp.zeros((window.shape[0], CONV_CHUNK), jnp.float32)
    for tap in range(KERNEL):
        d = sign * (tap - KERNEL // 2)
        shifted = pltpu.roll(window, (width - d) % width, 1) if d else window
        keep = (lo <= d) & (d < hi)
        total = total + wt_ref[:, tap : tap + 1] * jnp.where(
            keep, shifted[:, CONV_PAD : CONV_PAD + CONV_CHUNK], 0.0
        )
    return total


def conv_forward_kernel(x_ref, wt_ref, gain_ref, cot_ref, lo_ref, hi_ref, out_ref, gc_ref):
    gain = gain_ref[...]

    def body(c, carry):
        c0 = pl.multiple_of(c * CONV_CHUNK, CONV_CHUNK)
        cols = pl.ds(c0, CONV_CHUNK)
        conv_sum = conv_chunk(x_ref, wt_ref, lo_ref[:, cols], hi_ref[:, cols], c0, 1)
        spread = jnp.sqrt(jnp.mean(conv_sum * conv_sum, axis=0, keepdims=True) + 1e-05)
        normed = conv_sum / spread
        pre_act = normed * gain
        gate = 1.0 / (1.0 + jnp.exp(-pre_act))
        out_ref[:, cols] = (pre_act * gate).astype(out_ref.dtype)
        grad_pre = cot_ref[:, cols].astype(jnp.float32) * gate * (1.0 + pre_act * (1.0 - gate))
        weighted = grad_pre * gain
        gc_ref[:, cols] = (
            weighted - normed * jnp.mean(weighted * normed, axis=0, keepdims=True)
        ) / spread
        return carry

    lax.fori_loop(0, out_ref.shape[1] // CONV_CHUNK, body, 0)


def conv_backward_kernel(y_ref, wt_ref, att_ref, lo_ref, hi_ref, ga_ref, dop_ref, delta_ref):
    def body(c, carry):
        c0 = pl.multiple_of(c * CONV_CHUNK, CONV_CHUNK)
        cols = pl.ds(c0, CONV_CHUNK)
        grad_sum = conv_chunk(y_ref, wt_ref, lo_ref[:, cols], hi_ref[:, cols], c0, -1)
        grad_att = grad_sum.astype(ga_ref.dtype)
        ga_ref[:, cols] = grad_att
        grad_f32 = grad_att.astype(jnp.float32)
        delta = jnp.sum(grad_f32 * att_ref[:, cols].astype(jnp.float32), axis=0, keepdims=True)
        rows = pl.ds(c0, CONV_CHUNK)
        delta_ref[rows, :] = jnp.broadcast_to(delta, (8, CONV_CHUNK)).T[:, :1]
        wide = jnp.concatenate([jnp.zeros_like(grad_f32), grad_f32], axis=0)
        dop_ref[rows, :] = wide.T.astype(dop_ref.dtype)
        return carry

    lax.fori_loop(0, ga_ref.shape[1] // CONV_CHUNK, body, 0)


def padded_rims(block, half):
    count = lax.axis_size("blk")
    forward = [(i, i + 1) for i in range(count - 1)]
    backward = [(target, source) for source, target in forward]
    low = lax.ppermute(block[:, block.shape[1] - half :], "blk", forward)
    high = lax.ppermute(block[:, :half], "blk", backward)
    gap = jnp.zeros((block.shape[0], CONV_PAD - half), jnp.float32)
    return jnp.concatenate(
        [gap, low.astype(jnp.float32), block.astype(jnp.float32), high.astype(jnp.float32), gap],
        axis=1,
    )


def on_device(queries, keys, values, lengths, conv_weight, norm_gain, cotangent):
    rows_in, width = queries.shape
    heads_total = width // HEAD_DIM
    stacked = jnp.stack([queries, keys, values], axis=0)
    local_qkv = lax.all_to_all(stacked, "uly", split_axis=2, concat_axis=1, tiled=True)
    local_q, local_k, local_v = (local_qkv[i] for i in range(3))
    block_rows, channels = local_q.shape
    heads_here = channels // HEAD_DIM
    maxlen = block_rows // 2
    rows_q = min(512, block_rows)
    window = rows_q + 2 * maxlen
    conv_half = KERNEL // 2
    block_count = block_rows // rows_q
    score_scale = HEAD_DIM ** (-0.5)
    frame_total = lax.axis_size("blk") * block_rows
    first_frame = lax.axis_index("blk") * block_rows
    seg_ext = segment_ids(
        lengths,
        first_frame - maxlen + jnp.arange(block_rows + 2 * maxlen, dtype=jnp.int32),
        frame_total,
    )
    seg_own = seg_ext[maxlen : maxlen + block_rows]
    seg_conv = seg_ext[maxlen - conv_half : maxlen + block_rows + conv_half]
    near_pairs = extended(jnp.concatenate([local_k, local_v], axis=1), (("blk", 0),), maxlen)
    k_ext = near_pairs[:, :channels].reshape(-1, heads_here, HEAD_DIM)
    v_ext = near_pairs[:, channels:].reshape(-1, heads_here, HEAD_DIM)
    q_heads = local_q.reshape(block_rows, heads_here, HEAD_DIM)
    starts = jnp.arange(block_count, dtype=jnp.int32) * rows_q

    assert heads_here == 1
    lo_t, hi_t = tile_ranges(lengths, first_frame - maxlen, block_rows + 2 * maxlen, block_rows)
    qseg_col = seg_own[:, None].astype(jnp.int32)
    kseg_row = seg_ext[None, :].astype(jnp.int32)
    lane_gap = jnp.zeros((block_rows, HEAD_DIM), jnp.bfloat16)
    q_wide = jnp.concatenate([local_q, lane_gap], axis=1)
    att_t, lse_col = vmem_call(
        forward_kernel,
        2,
        4,
        (
            jax.ShapeDtypeStruct((HEAD_DIM, block_rows), jnp.bfloat16),
            jax.ShapeDtypeStruct((block_rows, 1), jnp.float32),
        ),
    )(lo_t, hi_t, q_wide, near_pairs, qseg_col, kseg_row)
    frame_at = first_frame + jnp.arange(block_rows, dtype=jnp.int32)
    seg_start, seg_end = segment_bounds(lengths, frame_at)
    lo_off = (seg_start - frame_at)[None, :].astype(jnp.int32)
    hi_off = (seg_end - frame_at)[None, :].astype(jnp.int32)
    weight_t = conv_weight.T
    conv_out_t, grad_conv_t = vmem_call(
        conv_forward_kernel,
        0,
        6,
        (
            jax.ShapeDtypeStruct((HEAD_DIM, block_rows), jnp.bfloat16),
            jax.ShapeDtypeStruct((HEAD_DIM, block_rows), jnp.float32),
        ),
    )(padded_rims(att_t, conv_half), weight_t, norm_gain[:, None], cotangent, lo_off, hi_off)
    grad_att_t, grad_wide, row_delta = vmem_call(
        conv_backward_kernel,
        0,
        5,
        (
            jax.ShapeDtypeStruct((HEAD_DIM, block_rows), jnp.bfloat16),
            jax.ShapeDtypeStruct((block_rows, 2 * HEAD_DIM), jnp.bfloat16),
            jax.ShapeDtypeStruct((block_rows, 1), jnp.float32),
        ),
    )(padded_rims(grad_conv_t, conv_half), weight_t, att_t, lo_off, hi_off)

    ext_rows = block_rows + 2 * maxlen
    grad_q, dk_t, dv_t = vmem_call(
        backward_kernel,
        2,
        9,
        (
            jax.ShapeDtypeStruct((block_rows, HEAD_DIM), jnp.bfloat16),
            jax.ShapeDtypeStruct((HEAD_DIM, ext_rows), jnp.float32),
            jax.ShapeDtypeStruct((HEAD_DIM, ext_rows), jnp.float32),
        ),
    )(
        lo_t,
        hi_t,
        q_wide,
        near_pairs,
        grad_wide,
        local_q.T,
        grad_att_t,
        qseg_col,
        kseg_row,
        lse_col,
        row_delta,
    )
    ext_terms = jnp.concatenate([dk_t, dv_t], axis=0)
    received = []
    for rim_part, direction in ((ext_terms[:, :maxlen], -1), (ext_terms[:, maxlen + block_rows :], 1)):
        received.append(
            passed_along(rim_part.astype(jnp.bfloat16), "blk", direction).astype(rim_part.dtype)
        )
    key_grads = ext_terms[:, maxlen : maxlen + block_rows] + jnp.concatenate(
        [received[1], received[0]], axis=1
    )
    grad_queries = grad_q.reshape(block_rows, channels)
    grad_keys = key_grads[:HEAD_DIM].astype(jnp.bfloat16)
    grad_values = key_grads[HEAD_DIM:].astype(jnp.bfloat16)
    return (conv_out_t, grad_queries.T, grad_keys, grad_values)


def solution(mesh):
    in_specs = (
        P(("blk", "uly"), None),
        P(("blk", "uly"), None),
        P(("blk", "uly"), None),
        P(),
        P(None, "uly"),
        P("uly"),
        P("uly", "blk"),
    )
    out_specs = (P("uly", "blk"), P("uly", "blk"), P("uly", "blk"), P("uly", "blk"))
    return jax.shard_map(
        on_device, mesh=mesh, in_specs=in_specs, out_specs=out_specs, check_vma=False
    )
```

```python
import jax
import jax.numpy as jnp
import functools
from jax import lax
from jax.experimental import pallas as pl
from jax.experimental.pallas import tpu as pltpu
from jax.sharding import PartitionSpec as P

KERNEL = 31
HEAD_DIM = 64


def extended(block, sides, width):
    for axis, dim in sides:
        count = lax.axis_size(axis)
        forward = [(i, i + 1) for i in range(count - 1)]
        backward = [(target, source) for source, target in forward]
        low = lax.ppermute(
            lax.slice_in_dim(block, block.shape[dim] - width, None, axis=dim), axis, forward
        )
        high = lax.ppermute(lax.slice_in_dim(block, 0, width, axis=dim), axis, backward)
        block = jnp.concatenate([low, block, high], axis=dim)
    return block


def passed_along(block, axis, distance):
    devices = range(lax.axis_size(axis))
    route = [(i - distance, i) for i in devices if i - distance in devices]
    return lax.ppermute(block, axis, route)


def segment_ids(lengths, frames, frame_total):
    starts = jnp.cumsum(lengths) - lengths
    seg_ids = jnp.sum((starts[None, :] <= frames[:, None]).astype(jnp.int32), axis=1) - 1
    inside = (frames >= 0) & (frames < frame_total)
    return jnp.where(inside, seg_ids, -1)


def rows_at(values_in, row_start, row_count):
    return lax.dynamic_slice_in_dim(values_in, row_start, row_count, 0)


def masked_scores(query_rows, key_rows, query_seg, key_seg):
    scores = HEAD_DIM ** (-0.5) * jnp.einsum(
        "rhe,she->hrs", query_rows, key_rows, preferred_element_type=jnp.float32
    )
    same_seg = (query_seg[:, None] == key_seg[None, :])[None]
    return (scores, same_seg)


def weights_of(scores, same_seg, row_top, row_total):
    return jnp.where(same_seg, jnp.exp(scores - row_top), 0.0) / row_total


TILE_Q = 512
TILE_K = 512
NT = (((1,), (1,)), ((), ()))
TN = (((0,), (0,)), ((), ()))


def forward_kernel(lo_ref, hi_ref, q_ref, kv_ref, qseg_ref, kseg_ref, o_ref, lse_ref):
    scale = HEAD_DIM ** (-0.5)

    def q_body(i, carry):
        r0 = pl.multiple_of(i * TILE_Q, TILE_Q)
        q = q_ref[pl.ds(r0, TILE_Q), :] * jnp.asarray(scale, q_ref.dtype)
        qs = qseg_ref[pl.ds(r0, TILE_Q), :]

        def k_body(j, c):
            m, l, acc = c
            c0 = pl.multiple_of(j * TILE_K, TILE_K)
            kv = kv_ref[pl.ds(c0, TILE_K), :]
            ks = kseg_ref[:, pl.ds(c0, TILE_K)]
            s = lax.dot_general(q, kv, NT, preferred_element_type=jnp.float32)
            s = jnp.where(qs == ks, s, -1e30)
            m_new = jnp.maximum(m, jnp.max(s, axis=1, keepdims=True))
            alpha = jnp.exp(m - m_new)
            p = jnp.exp(s - m_new)
            l = alpha * l + jnp.sum(p, axis=1, keepdims=True)
            acc = alpha * acc + jnp.dot(
                p.astype(jnp.bfloat16), kv, preferred_element_type=jnp.float32
            )
            return (m_new, l, acc)

        init = (
            jnp.full((TILE_Q, 1), -1e30, jnp.float32),
            jnp.zeros((TILE_Q, 1), jnp.float32),
            jnp.zeros((TILE_Q, kv_ref.shape[1]), jnp.float32),
        )
        m, l, acc = lax.fori_loop(lo_ref[i], hi_ref[i], k_body, init)
        o_ref[:, pl.ds(r0, TILE_Q)] = (acc / l).T[HEAD_DIM:].astype(o_ref.dtype)
        lse_ref[pl.ds(r0, TILE_Q), :] = m + jnp.log(l)
        return carry

    lax.fori_loop(0, q_ref.shape[0] // TILE_Q, q_body, 0)


def backward_kernel(
    lo_ref, hi_ref, q_ref, kv_ref, do_ref, qt_ref, dot_ref, qseg_ref, kseg_ref, lse_ref,
    d_ref, dq_ref, dk_ref, dv_ref,
):
    scale = HEAD_DIM ** (-0.5)
    dk_ref[...] = jnp.zeros_like(dk_ref)
    dv_ref[...] = jnp.zeros_like(dv_ref)

    def q_body(i, carry):
        r0 = pl.multiple_of(i * TILE_Q, TILE_Q)
        q = q_ref[pl.ds(r0, TILE_Q), :] * jnp.asarray(scale, q_ref.dtype)
        do = do_ref[pl.ds(r0, TILE_Q), :]
        qs = qseg_ref[pl.ds(r0, TILE_Q), :]
        lse = lse_ref[pl.ds(r0, TILE_Q), :]
        dlt = d_ref[pl.ds(r0, TILE_Q), :]
        q_t = qt_ref[:, pl.ds(r0, TILE_Q)]
        do_t = dot_ref[:, pl.ds(r0, TILE_Q)]

        def k_body(j, dq):
            c0 = pl.multiple_of(j * TILE_K, TILE_K)
            kv = kv_ref[pl.ds(c0, TILE_K), :]
            ks = kseg_ref[:, pl.ds(c0, TILE_K)]
            s = lax.dot_general(q, kv, NT, preferred_element_type=jnp.float32)
            p = jnp.exp(jnp.where(qs == ks, s, -1e30) - lse)
            dp = lax.dot_general(do, kv, NT, preferred_element_type=jnp.float32)
            ds = (p * (dp - dlt)).astype(jnp.bfloat16)
            dk_ref[:, pl.ds(c0, TILE_K)] += jnp.dot(q_t, ds, preferred_element_type=jnp.float32)
            dv_ref[:, pl.ds(c0, TILE_K)] += jnp.dot(
                do_t, p.astype(jnp.bfloat16), preferred_element_type=jnp.float32
            )
            return dq + jnp.dot(ds, kv, preferred_element_type=jnp.float32)

        dq = lax.fori_loop(
            lo_ref[i], hi_ref[i], k_body, jnp.zeros((TILE_Q, kv_ref.shape[1]), jnp.float32)
        )
        dq_ref[pl.ds(r0, TILE_Q), :] = (scale * dq[:, :HEAD_DIM]).astype(dq_ref.dtype)
        return carry

    lax.fori_loop(0, q_ref.shape[0] // TILE_Q, q_body, 0)
    dk_ref[...] = scale * dk_ref[...]


def vmem_call(kernel, n_smem, n_vmem, out_shape):
    return pl.pallas_call(
        kernel,
        out_shape=out_shape,
        in_specs=[pl.BlockSpec(memory_space=pltpu.SMEM)] * n_smem
        + [pl.BlockSpec(memory_space=pltpu.VMEM)] * n_vmem,
        out_specs=[pl.BlockSpec(memory_space=pltpu.VMEM)] * len(out_shape),
    )


def segment_bounds(lengths, frames):
    ends = jnp.cumsum(lengths)
    starts = ends - lengths
    seg_start = jnp.max(jnp.where(starts[None, :] <= frames[:, None], starts[None, :], 0), axis=1)
    big = jnp.iinfo(jnp.int32).max
    seg_end = jnp.min(jnp.where(ends[None, :] > frames[:, None], ends[None, :], big), axis=1)
    return (seg_start, jnp.minimum(seg_end, ends[-1]))


def tile_ranges(lengths, base, ext_rows, block_rows):
    frames = base + (ext_rows - block_rows) // 2 + jnp.arange(block_rows, dtype=jnp.int32)
    seg_start, seg_end = segment_bounds(lengths, frames)
    lo = (seg_start[::TILE_Q] - base) // TILE_K
    hi = (seg_end[TILE_Q - 1 :: TILE_Q] - base + TILE_K - 1) // TILE_K
    lo = jnp.clip(lo, 0, ext_rows // TILE_K).astype(jnp.int32)
    hi = jnp.clip(hi, lo, ext_rows // TILE_K).astype(jnp.int32)
    return (lo, hi)


CONV_PAD = 128
CONV_CHUNK = 512


def conv_chunk(x_ref, wt_ref, lo, hi, c0, sign):
    window = x_ref[:, pl.ds(c0, CONV_CHUNK + 2 * CONV_PAD)]
    width = window.shape[1]
    total = jnp.zeros((window.shape[0], CONV_CHUNK), jnp.float32)
    for tap in range(KERNEL):
        d = sign * (tap - KERNEL // 2)
        shifted = pltpu.roll(window, (width - d) % width, 1) if d else window
        keep = (lo <= d) & (d < hi)
        total = total + wt_ref[:, tap : tap + 1] * jnp.where(
            keep, shifted[:, CONV_PAD : CONV_PAD + CONV_CHUNK], 0.0
        )
    return total


def conv_forward_kernel(x_ref, wt_ref, gain_ref, cot_ref, lo_ref, hi_ref, out_ref, gc_ref):
    gain = gain_ref[...]

    def body(c, carry):
        c0 = pl.multiple_of(c * CONV_CHUNK, CONV_CHUNK)
        cols = pl.ds(c0, CONV_CHUNK)
        conv_sum = conv_chunk(x_ref, wt_ref, lo_ref[:, cols], hi_ref[:, cols], c0, 1)
        spread = jnp.sqrt(jnp.mean(conv_sum * conv_sum, axis=0, keepdims=True) + 1e-05)
        normed = conv_sum / spread
        pre_act = normed * gain
        gate = 1.0 / (1.0 + jnp.exp(-pre_act))
        out_ref[:, cols] = (pre_act * gate).astype(out_ref.dtype)
        grad_pre = cot_ref[:, cols].astype(jnp.float32) * gate * (1.0 + pre_act * (1.0 - gate))
        weighted = grad_pre * gain
        gc_ref[:, cols] = (
            weighted - normed * jnp.mean(weighted * normed, axis=0, keepdims=True)
        ) / spread
        return carry

    lax.fori_loop(0, out_ref.shape[1] // CONV_CHUNK, body, 0)


def conv_backward_kernel(y_ref, wt_ref, att_ref, lo_ref, hi_ref, ga_ref, dop_ref, delta_ref):
    def body(c, carry):
        c0 = pl.multiple_of(c * CONV_CHUNK, CONV_CHUNK)
        cols = pl.ds(c0, CONV_CHUNK)
        grad_sum = conv_chunk(y_ref, wt_ref, lo_ref[:, cols], hi_ref[:, cols], c0, -1)
        grad_att = grad_sum.astype(ga_ref.dtype)
        ga_ref[:, cols] = grad_att
        grad_f32 = grad_att.astype(jnp.float32)
        delta = jnp.sum(grad_f32 * att_ref[:, cols].astype(jnp.float32), axis=0, keepdims=True)
        rows = pl.ds(c0, CONV_CHUNK)
        delta_ref[rows, :] = jnp.broadcast_to(delta, (8, CONV_CHUNK)).T[:, :1]
        wide = jnp.concatenate([jnp.zeros_like(grad_f32), grad_f32], axis=0)
        dop_ref[rows, :] = wide.T.astype(dop_ref.dtype)
        return carry

    lax.fori_loop(0, ga_ref.shape[1] // CONV_CHUNK, body, 0)


def padded_rims(block, half):
    count = lax.axis_size("blk")
    forward = [(i, i + 1) for i in range(count - 1)]
    backward = [(target, source) for source, target in forward]
    low = lax.ppermute(block[:, block.shape[1] - half :], "blk", forward)
    high = lax.ppermute(block[:, :half], "blk", backward)
    gap = jnp.zeros((block.shape[0], CONV_PAD - half), jnp.float32)
    return jnp.concatenate(
        [gap, low.astype(jnp.float32), block.astype(jnp.float32), high.astype(jnp.float32), gap],
        axis=1,
    )


def on_device(queries, keys, values, lengths, conv_weight, norm_gain, cotangent):
    rows_in, width = queries.shape
    heads_total = width // HEAD_DIM
    stacked = jnp.stack(
        [a.reshape(rows_in, heads_total, HEAD_DIM) for a in (queries, keys, values)], axis=2
    ).reshape(rows_in, heads_total * 3 * HEAD_DIM)
    local_qkv = lax.all_to_all(stacked, "uly", split_axis=1, concat_axis=0, tiled=True)
    local_qkv = local_qkv.reshape(local_qkv.shape[0], -1, 3, HEAD_DIM)
    local_q, local_k, local_v = (
        local_qkv[:, :, i].reshape(local_qkv.shape[0], -1) for i in range(3)
    )
    block_rows, channels = local_q.shape
    heads_here = channels // HEAD_DIM
    maxlen = block_rows // 2
    rows_q = min(512, block_rows)
    window = rows_q + 2 * maxlen
    conv_half = KERNEL // 2
    block_count = block_rows // rows_q
    score_scale = HEAD_DIM ** (-0.5)
    frame_total = lax.axis_size("blk") * block_rows
    first_frame = lax.axis_index("blk") * block_rows
    seg_ext = segment_ids(
        lengths,
        first_frame - maxlen + jnp.arange(block_rows + 2 * maxlen, dtype=jnp.int32),
        frame_total,
    )
    seg_own = seg_ext[maxlen : maxlen + block_rows]
    seg_conv = seg_ext[maxlen - conv_half : maxlen + block_rows + conv_half]
    near_pairs = extended(jnp.concatenate([local_k, local_v], axis=1), (("blk", 0),), maxlen)
    k_ext = near_pairs[:, :channels].reshape(-1, heads_here, HEAD_DIM)
    v_ext = near_pairs[:, channels:].reshape(-1, heads_here, HEAD_DIM)
    q_heads = local_q.reshape(block_rows, heads_here, HEAD_DIM)
    starts = jnp.arange(block_count, dtype=jnp.int32) * rows_q

    assert heads_here == 1
    lo_t, hi_t = tile_ranges(lengths, first_frame - maxlen, block_rows + 2 * maxlen, block_rows)
    qseg_col = seg_own[:, None].astype(jnp.int32)
    kseg_row = seg_ext[None, :].astype(jnp.int32)
    lane_gap = jnp.zeros((block_rows, HEAD_DIM), jnp.bfloat16)
    q_wide = jnp.concatenate([local_q, lane_gap], axis=1)
    att_t, lse_col = vmem_call(
        forward_kernel,
        2,
        4,
        (
            jax.ShapeDtypeStruct((HEAD_DIM, block_rows), jnp.bfloat16),
            jax.ShapeDtypeStruct((block_rows, 1), jnp.float32),
        ),
    )(lo_t, hi_t, q_wide, near_pairs, qseg_col, kseg_row)
    frame_at = first_frame + jnp.arange(block_rows, dtype=jnp.int32)
    seg_start, seg_end = segment_bounds(lengths, frame_at)
    lo_off = (seg_start - frame_at)[None, :].astype(jnp.int32)
    hi_off = (seg_end - frame_at)[None, :].astype(jnp.int32)
    weight_t = conv_weight.T
    conv_out_t, grad_conv_t = vmem_call(
        conv_forward_kernel,
        0,
        6,
        (
            jax.ShapeDtypeStruct((HEAD_DIM, block_rows), jnp.bfloat16),
            jax.ShapeDtypeStruct((HEAD_DIM, block_rows), jnp.float32),
        ),
    )(padded_rims(att_t, conv_half), weight_t, norm_gain[:, None], cotangent, lo_off, hi_off)
    grad_att_t, grad_wide, row_delta = vmem_call(
        conv_backward_kernel,
        0,
        5,
        (
            jax.ShapeDtypeStruct((HEAD_DIM, block_rows), jnp.bfloat16),
            jax.ShapeDtypeStruct((block_rows, 2 * HEAD_DIM), jnp.bfloat16),
            jax.ShapeDtypeStruct((block_rows, 1), jnp.float32),
        ),
    )(padded_rims(grad_conv_t, conv_half), weight_t, att_t, lo_off, hi_off)

    ext_rows = block_rows + 2 * maxlen
    grad_q, dk_t, dv_t = vmem_call(
        backward_kernel,
        2,
        9,
        (
            jax.ShapeDtypeStruct((block_rows, HEAD_DIM), jnp.bfloat16),
            jax.ShapeDtypeStruct((HEAD_DIM, ext_rows), jnp.float32),
            jax.ShapeDtypeStruct((HEAD_DIM, ext_rows), jnp.float32),
        ),
    )(
        lo_t,
        hi_t,
        q_wide,
        near_pairs,
        grad_wide,
        local_q.T,
        grad_att_t,
        qseg_col,
        kseg_row,
        lse_col,
        row_delta,
    )
    ext_terms = jnp.concatenate([dk_t, dv_t], axis=0)
    received = []
    for rim_part, direction in ((ext_terms[:, :maxlen], -1), (ext_terms[:, maxlen + block_rows :], 1)):
        received.append(
            passed_along(rim_part.astype(jnp.bfloat16), "blk", direction).astype(rim_part.dtype)
        )
    key_grads = ext_terms[:, maxlen : maxlen + block_rows] + jnp.concatenate(
        [received[1], received[0]], axis=1
    )
    grad_queries = grad_q.reshape(block_rows, channels)
    grad_keys = key_grads[:HEAD_DIM].astype(jnp.bfloat16)
    grad_values = key_grads[HEAD_DIM:].astype(jnp.bfloat16)
    return (conv_out_t, grad_queries.T, grad_keys, grad_values)


def solution(mesh):
    in_specs = (
        P(("blk", "uly"), None),
        P(("blk", "uly"), None),
        P(("blk", "uly"), None),
        P(),
        P(None, "uly"),
        P("uly"),
        P("uly", "blk"),
    )
    out_specs = (P("uly", "blk"), P("uly", "blk"), P("uly", "blk"), P("uly", "blk"))
    return jax.shard_map(
        on_device, mesh=mesh, in_specs=in_specs, out_specs=out_specs, check_vma=False
    )
```

```python
import jax
import jax.numpy as jnp
import functools
from jax import lax
from jax.experimental import pallas as pl
from jax.experimental.pallas import tpu as pltpu
from jax.sharding import PartitionSpec as P

KERNEL = 31
HEAD_DIM = 64


def extended(block, sides, width):
    for axis, dim in sides:
        count = lax.axis_size(axis)
        forward = [(i, i + 1) for i in range(count - 1)]
        backward = [(target, source) for source, target in forward]
        low = lax.ppermute(
            lax.slice_in_dim(block, block.shape[dim] - width, None, axis=dim), axis, forward
        )
        high = lax.ppermute(lax.slice_in_dim(block, 0, width, axis=dim), axis, backward)
        block = jnp.concatenate([low, block, high], axis=dim)
    return block


def passed_along(block, axis, distance):
    devices = range(lax.axis_size(axis))
    route = [(i - distance, i) for i in devices if i - distance in devices]
    return lax.ppermute(block, axis, route)


def segment_ids(lengths, frames, frame_total):
    starts = jnp.cumsum(lengths) - lengths
    seg_ids = jnp.sum((starts[None, :] <= frames[:, None]).astype(jnp.int32), axis=1) - 1
    inside = (frames >= 0) & (frames < frame_total)
    return jnp.where(inside, seg_ids, -1)


def rows_at(values_in, row_start, row_count):
    return lax.dynamic_slice_in_dim(values_in, row_start, row_count, 0)


def masked_scores(query_rows, key_rows, query_seg, key_seg):
    scores = HEAD_DIM ** (-0.5) * jnp.einsum(
        "rhe,she->hrs", query_rows, key_rows, preferred_element_type=jnp.float32
    )
    same_seg = (query_seg[:, None] == key_seg[None, :])[None]
    return (scores, same_seg)


def weights_of(scores, same_seg, row_top, row_total):
    return jnp.where(same_seg, jnp.exp(scores - row_top), 0.0) / row_total


TILE_Q = 512
TILE_K = 512
NT = (((1,), (1,)), ((), ()))
TN = (((0,), (0,)), ((), ()))


def forward_kernel(lo_ref, hi_ref, q_ref, kv_ref, qseg_ref, kseg_ref, o_ref, lse_ref):
    scale = HEAD_DIM ** (-0.5)

    def q_body(i, carry):
        r0 = pl.multiple_of(i * TILE_Q, TILE_Q)
        q = q_ref[pl.ds(r0, TILE_Q), :] * jnp.asarray(scale, q_ref.dtype)
        qs = qseg_ref[pl.ds(r0, TILE_Q), :]

        def k_body(j, c):
            m, l, acc = c
            c0 = pl.multiple_of(j * TILE_K, TILE_K)
            kv = kv_ref[pl.ds(c0, TILE_K), :]
            ks = kseg_ref[:, pl.ds(c0, TILE_K)]
            s = lax.dot_general(q, kv, NT, preferred_element_type=jnp.float32)
            s = jnp.where(qs == ks, s, -1e30)
            m_new = jnp.maximum(m, jnp.max(s, axis=1, keepdims=True))
            alpha = jnp.exp(m - m_new)
            p = jnp.exp(s - m_new)
            l = alpha * l + jnp.sum(p, axis=1, keepdims=True)
            acc = alpha * acc + jnp.dot(
                p.astype(jnp.bfloat16), kv, preferred_element_type=jnp.float32
            )
            return (m_new, l, acc)

        init = (
            jnp.full((TILE_Q, 1), -1e30, jnp.float32),
            jnp.zeros((TILE_Q, 1), jnp.float32),
            jnp.zeros((TILE_Q, kv_ref.shape[1]), jnp.float32),
        )
        m, l, acc = lax.fori_loop(lo_ref[i], hi_ref[i], k_body, init)
        o_ref[:, pl.ds(r0, TILE_Q)] = (acc / l).T[HEAD_DIM:].astype(o_ref.dtype)
        lse_ref[pl.ds(r0, TILE_Q), :] = m + jnp.log(l)
        return carry

    lax.fori_loop(0, q_ref.shape[0] // TILE_Q, q_body, 0)


def backward_kernel(
    lo_ref, hi_ref, q_ref, kv_ref, do_ref, qt_ref, dot_ref, qseg_ref, kseg_ref, lse_ref,
    d_ref, dq_ref, dk_ref, dv_ref,
):
    scale = HEAD_DIM ** (-0.5)
    dk_ref[...] = jnp.zeros_like(dk_ref)
    dv_ref[...] = jnp.zeros_like(dv_ref)

    def q_body(i, carry):
        r0 = pl.multiple_of(i * TILE_Q, TILE_Q)
        q = q_ref[pl.ds(r0, TILE_Q), :] * jnp.asarray(scale, q_ref.dtype)
        do = do_ref[pl.ds(r0, TILE_Q), :]
        qs = qseg_ref[pl.ds(r0, TILE_Q), :]
        lse = lse_ref[pl.ds(r0, TILE_Q), :]
        dlt = d_ref[pl.ds(r0, TILE_Q), :]
        q_t = qt_ref[:, pl.ds(r0, TILE_Q)]
        do_t = dot_ref[:, pl.ds(r0, TILE_Q)]

        def k_body(j, dq):
            c0 = pl.multiple_of(j * TILE_K, TILE_K)
            kv = kv_ref[pl.ds(c0, TILE_K), :]
            ks = kseg_ref[:, pl.ds(c0, TILE_K)]
            s = lax.dot_general(q, kv, NT, preferred_element_type=jnp.float32)
            p = jnp.exp(jnp.where(qs == ks, s, -1e30) - lse)
            dp = lax.dot_general(do, kv, NT, preferred_element_type=jnp.float32)
            ds = (p * (dp - dlt)).astype(jnp.bfloat16)
            dk_ref[:, pl.ds(c0, TILE_K)] += jnp.dot(q_t, ds, preferred_element_type=jnp.float32)
            dv_ref[:, pl.ds(c0, TILE_K)] += jnp.dot(
                do_t, p.astype(jnp.bfloat16), preferred_element_type=jnp.float32
            )
            return dq + jnp.dot(ds, kv, preferred_element_type=jnp.float32)

        dq = lax.fori_loop(
            lo_ref[i], hi_ref[i], k_body, jnp.zeros((TILE_Q, kv_ref.shape[1]), jnp.float32)
        )
        dq_ref[pl.ds(r0, TILE_Q), :] = (scale * dq[:, :HEAD_DIM]).astype(dq_ref.dtype)
        return carry

    lax.fori_loop(0, q_ref.shape[0] // TILE_Q, q_body, 0)
    dk_ref[...] = scale * dk_ref[...]


def vmem_call(kernel, n_smem, n_vmem, out_shape):
    return pl.pallas_call(
        kernel,
        out_shape=out_shape,
        in_specs=[pl.BlockSpec(memory_space=pltpu.SMEM)] * n_smem
        + [pl.BlockSpec(memory_space=pltpu.VMEM)] * n_vmem,
        out_specs=[pl.BlockSpec(memory_space=pltpu.VMEM)] * len(out_shape),
    )


def segment_bounds(lengths, frames):
    ends = jnp.cumsum(lengths)
    starts = ends - lengths
    seg_start = jnp.max(jnp.where(starts[None, :] <= frames[:, None], starts[None, :], 0), axis=1)
    big = jnp.iinfo(jnp.int32).max
    seg_end = jnp.min(jnp.where(ends[None, :] > frames[:, None], ends[None, :], big), axis=1)
    return (seg_start, jnp.minimum(seg_end, ends[-1]))


def tile_ranges(lengths, base, ext_rows, block_rows):
    frames = base + (ext_rows - block_rows) // 2 + jnp.arange(block_rows, dtype=jnp.int32)
    seg_start, seg_end = segment_bounds(lengths, frames)
    lo = (seg_start[::TILE_Q] - base) // TILE_K
    hi = (seg_end[TILE_Q - 1 :: TILE_Q] - base + TILE_K - 1) // TILE_K
    lo = jnp.clip(lo, 0, ext_rows // TILE_K).astype(jnp.int32)
    hi = jnp.clip(hi, lo, ext_rows // TILE_K).astype(jnp.int32)
    return (lo, hi)


CONV_PAD = 128
CONV_CHUNK = 1024


def conv_chunk(x_ref, wt_ref, lo, hi, c0, sign):
    window = x_ref[:, pl.ds(c0, CONV_CHUNK + 2 * CONV_PAD)]
    width = window.shape[1]
    total = jnp.zeros((window.shape[0], CONV_CHUNK), jnp.float32)
    for tap in range(KERNEL):
        d = sign * (tap - KERNEL // 2)
        shifted = pltpu.roll(window, (width - d) % width, 1) if d else window
        keep = (lo <= d) & (d < hi)
        total = total + wt_ref[:, tap : tap + 1] * jnp.where(
            keep, shifted[:, CONV_PAD : CONV_PAD + CONV_CHUNK], 0.0
        )
    return total


def conv_forward_kernel(x_ref, wt_ref, gain_ref, cot_ref, lo_ref, hi_ref, out_ref, gc_ref):
    gain = gain_ref[...]

    def body(c, carry):
        c0 = pl.multiple_of(c * CONV_CHUNK, CONV_CHUNK)
        cols = pl.ds(c0, CONV_CHUNK)
        conv_sum = conv_chunk(x_ref, wt_ref, lo_ref[:, cols], hi_ref[:, cols], c0, 1)
        spread = jnp.sqrt(jnp.mean(conv_sum * conv_sum, axis=0, keepdims=True) + 1e-05)
        normed = conv_sum / spread
        pre_act = normed * gain
        gate = 1.0 / (1.0 + jnp.exp(-pre_act))
        out_ref[:, cols] = (pre_act * gate).astype(out_ref.dtype)
        grad_pre = cot_ref[:, cols].astype(jnp.float32) * gate * (1.0 + pre_act * (1.0 - gate))
        weighted = grad_pre * gain
        gc_ref[:, cols] = (
            weighted - normed * jnp.mean(weighted * normed, axis=0, keepdims=True)
        ) / spread
        return carry

    lax.fori_loop(0, out_ref.shape[1] // CONV_CHUNK, body, 0)


def conv_backward_kernel(y_ref, wt_ref, att_ref, lo_ref, hi_ref, ga_ref, dop_ref, delta_ref):
    def body(c, carry):
        c0 = pl.multiple_of(c * CONV_CHUNK, CONV_CHUNK)
        cols = pl.ds(c0, CONV_CHUNK)
        grad_sum = conv_chunk(y_ref, wt_ref, lo_ref[:, cols], hi_ref[:, cols], c0, -1)
        grad_att = grad_sum.astype(ga_ref.dtype)
        ga_ref[:, cols] = grad_att
        grad_f32 = grad_att.astype(jnp.float32)
        delta = jnp.sum(grad_f32 * att_ref[:, cols].astype(jnp.float32), axis=0, keepdims=True)
        rows = pl.ds(c0, CONV_CHUNK)
        delta_ref[rows, :] = jnp.broadcast_to(delta, (8, CONV_CHUNK)).T[:, :1]
        wide = jnp.concatenate([jnp.zeros_like(grad_f32), grad_f32], axis=0)
        dop_ref[rows, :] = wide.T.astype(dop_ref.dtype)
        return carry

    lax.fori_loop(0, ga_ref.shape[1] // CONV_CHUNK, body, 0)


def padded_rims(block, half):
    count = lax.axis_size("blk")
    forward = [(i, i + 1) for i in range(count - 1)]
    backward = [(target, source) for source, target in forward]
    low = lax.ppermute(block[:, block.shape[1] - half :], "blk", forward)
    high = lax.ppermute(block[:, :half], "blk", backward)
    gap = jnp.zeros((block.shape[0], CONV_PAD - half), jnp.float32)
    return jnp.concatenate(
        [gap, low.astype(jnp.float32), block.astype(jnp.float32), high.astype(jnp.float32), gap],
        axis=1,
    )


def on_device(queries, keys, values, lengths, conv_weight, norm_gain, cotangent):
    rows_in, width = queries.shape
    heads_total = width // HEAD_DIM
    stacked = jnp.stack(
        [a.reshape(rows_in, heads_total, HEAD_DIM) for a in (queries, keys, values)], axis=2
    ).reshape(rows_in, heads_total * 3 * HEAD_DIM)
    local_qkv = lax.all_to_all(stacked, "uly", split_axis=1, concat_axis=0, tiled=True)
    local_qkv = local_qkv.reshape(local_qkv.shape[0], -1, 3, HEAD_DIM)
    local_q, local_k, local_v = (
        local_qkv[:, :, i].reshape(local_qkv.shape[0], -1) for i in range(3)
    )
    block_rows, channels = local_q.shape
    heads_here = channels // HEAD_DIM
    maxlen = block_rows // 2
    rows_q = min(512, block_rows)
    window = rows_q + 2 * maxlen
    conv_half = KERNEL // 2
    block_count = block_rows // rows_q
    score_scale = HEAD_DIM ** (-0.5)
    frame_total = lax.axis_size("blk") * block_rows
    first_frame = lax.axis_index("blk") * block_rows
    seg_ext = segment_ids(
        lengths,
        first_frame - maxlen + jnp.arange(block_rows + 2 * maxlen, dtype=jnp.int32),
        frame_total,
    )
    seg_own = seg_ext[maxlen : maxlen + block_rows]
    seg_conv = seg_ext[maxlen - conv_half : maxlen + block_rows + conv_half]
    near_pairs = extended(jnp.concatenate([local_k, local_v], axis=1), (("blk", 0),), maxlen)
    k_ext = near_pairs[:, :channels].reshape(-1, heads_here, HEAD_DIM)
    v_ext = near_pairs[:, channels:].reshape(-1, heads_here, HEAD_DIM)
    q_heads = local_q.reshape(block_rows, heads_here, HEAD_DIM)
    starts = jnp.arange(block_count, dtype=jnp.int32) * rows_q

    assert heads_here == 1
    lo_t, hi_t = tile_ranges(lengths, first_frame - maxlen, block_rows + 2 * maxlen, block_rows)
    qseg_col = seg_own[:, None].astype(jnp.int32)
    kseg_row = seg_ext[None, :].astype(jnp.int32)
    lane_gap = jnp.zeros((block_rows, HEAD_DIM), jnp.bfloat16)
    q_wide = jnp.concatenate([local_q, lane_gap], axis=1)
    att_t, lse_col = vmem_call(
        forward_kernel,
        2,
        4,
        (
            jax.ShapeDtypeStruct((HEAD_DIM, block_rows), jnp.bfloat16),
            jax.ShapeDtypeStruct((block_rows, 1), jnp.float32),
        ),
    )(lo_t, hi_t, q_wide, near_pairs, qseg_col, kseg_row)
    frame_at = first_frame + jnp.arange(block_rows, dtype=jnp.int32)
    seg_start, seg_end = segment_bounds(lengths, frame_at)
    lo_off = (seg_start - frame_at)[None, :].astype(jnp.int32)
    hi_off = (seg_end - frame_at)[None, :].astype(jnp.int32)
    weight_t = conv_weight.T
    conv_out_t, grad_conv_t = vmem_call(
        conv_forward_kernel,
        0,
        6,
        (
            jax.ShapeDtypeStruct((HEAD_DIM, block_rows), jnp.bfloat16),
            jax.ShapeDtypeStruct((HEAD_DIM, block_rows), jnp.float32),
        ),
    )(padded_rims(att_t, conv_half), weight_t, norm_gain[:, None], cotangent, lo_off, hi_off)
    grad_att_t, grad_wide, row_delta = vmem_call(
        conv_backward_kernel,
        0,
        5,
        (
            jax.ShapeDtypeStruct((HEAD_DIM, block_rows), jnp.bfloat16),
            jax.ShapeDtypeStruct((block_rows, 2 * HEAD_DIM), jnp.bfloat16),
            jax.ShapeDtypeStruct((block_rows, 1), jnp.float32),
        ),
    )(padded_rims(grad_conv_t, conv_half), weight_t, att_t, lo_off, hi_off)

    ext_rows = block_rows + 2 * maxlen
    grad_q, dk_t, dv_t = vmem_call(
        backward_kernel,
        2,
        9,
        (
            jax.ShapeDtypeStruct((block_rows, HEAD_DIM), jnp.bfloat16),
            jax.ShapeDtypeStruct((HEAD_DIM, ext_rows), jnp.float32),
            jax.ShapeDtypeStruct((HEAD_DIM, ext_rows), jnp.float32),
        ),
    )(
        lo_t,
        hi_t,
        q_wide,
        near_pairs,
        grad_wide,
        local_q.T,
        grad_att_t,
        qseg_col,
        kseg_row,
        lse_col,
        row_delta,
    )
    ext_terms = jnp.concatenate([dk_t, dv_t], axis=0)
    received = []
    for rim_part, direction in ((ext_terms[:, :maxlen], -1), (ext_terms[:, maxlen + block_rows :], 1)):
        received.append(
            passed_along(rim_part.astype(jnp.bfloat16), "blk", direction).astype(rim_part.dtype)
        )
    key_grads = ext_terms[:, maxlen : maxlen + block_rows] + jnp.concatenate(
        [received[1], received[0]], axis=1
    )
    grad_queries = grad_q.reshape(block_rows, channels)
    grad_keys = key_grads[:HEAD_DIM].astype(jnp.bfloat16)
    grad_values = key_grads[HEAD_DIM:].astype(jnp.bfloat16)
    return (conv_out_t, grad_queries.T, grad_keys, grad_values)


def solution(mesh):
    in_specs = (
        P(("blk", "uly"), None),
        P(("blk", "uly"), None),
        P(("blk", "uly"), None),
        P(),
        P(None, "uly"),
        P("uly"),
        P("uly", "blk"),
    )
    out_specs = (P("uly", "blk"), P("uly", "blk"), P("uly", "blk"), P("uly", "blk"))
    return jax.shard_map(
        on_device, mesh=mesh, in_specs=in_specs, out_specs=out_specs, check_vma=False
    )
```

```python
import jax
import jax.numpy as jnp
import functools
from jax import lax
from jax.experimental import pallas as pl
from jax.experimental.pallas import tpu as pltpu
from jax.sharding import PartitionSpec as P

KERNEL = 31
HEAD_DIM = 64


def extended(block, sides, width):
    for axis, dim in sides:
        count = lax.axis_size(axis)
        forward = [(i, i + 1) for i in range(count - 1)]
        backward = [(target, source) for source, target in forward]
        low = lax.ppermute(
            lax.slice_in_dim(block, block.shape[dim] - width, None, axis=dim), axis, forward
        )
        high = lax.ppermute(lax.slice_in_dim(block, 0, width, axis=dim), axis, backward)
        block = jnp.concatenate([low, block, high], axis=dim)
    return block


def passed_along(block, axis, distance):
    devices = range(lax.axis_size(axis))
    route = [(i - distance, i) for i in devices if i - distance in devices]
    return lax.ppermute(block, axis, route)


def segment_ids(lengths, frames, frame_total):
    starts = jnp.cumsum(lengths) - lengths
    seg_ids = jnp.sum((starts[None, :] <= frames[:, None]).astype(jnp.int32), axis=1) - 1
    inside = (frames >= 0) & (frames < frame_total)
    return jnp.where(inside, seg_ids, -1)


def rows_at(values_in, row_start, row_count):
    return lax.dynamic_slice_in_dim(values_in, row_start, row_count, 0)


def masked_scores(query_rows, key_rows, query_seg, key_seg):
    scores = HEAD_DIM ** (-0.5) * jnp.einsum(
        "rhe,she->hrs", query_rows, key_rows, preferred_element_type=jnp.float32
    )
    same_seg = (query_seg[:, None] == key_seg[None, :])[None]
    return (scores, same_seg)


def weights_of(scores, same_seg, row_top, row_total):
    return jnp.where(same_seg, jnp.exp(scores - row_top), 0.0) / row_total


TILE_Q = 512
TILE_K = 512
NT = (((1,), (1,)), ((), ()))
TN = (((0,), (0,)), ((), ()))


def forward_kernel(lo_ref, hi_ref, q_ref, kv_ref, qseg_ref, kseg_ref, o_ref, lse_ref):
    scale = HEAD_DIM ** (-0.5)

    def q_body(i, carry):
        r0 = pl.multiple_of(i * TILE_Q, TILE_Q)
        q = q_ref[pl.ds(r0, TILE_Q), :] * jnp.asarray(scale, q_ref.dtype)
        qs = qseg_ref[pl.ds(r0, TILE_Q), :]

        def k_body(j, c):
            m, l, acc = c
            c0 = pl.multiple_of(j * TILE_K, TILE_K)
            kv = kv_ref[pl.ds(c0, TILE_K), :]
            ks = kseg_ref[:, pl.ds(c0, TILE_K)]
            s = lax.dot_general(q, kv, NT, preferred_element_type=jnp.float32)
            s = jnp.where(qs == ks, s, -1e30)
            m_new = jnp.maximum(m, jnp.max(s, axis=1, keepdims=True))
            alpha = jnp.exp(m - m_new)
            p = jnp.exp(s - m_new)
            l = alpha * l + jnp.sum(p, axis=1, keepdims=True)
            acc = alpha * acc + jnp.dot(
                p.astype(jnp.bfloat16), kv, preferred_element_type=jnp.float32
            )
            return (m_new, l, acc)

        init = (
            jnp.full((TILE_Q, 1), -1e30, jnp.float32),
            jnp.zeros((TILE_Q, 1), jnp.float32),
            jnp.zeros((TILE_Q, kv_ref.shape[1]), jnp.float32),
        )
        m, l, acc = lax.fori_loop(lo_ref[i], hi_ref[i], k_body, init)
        o_ref[:, pl.ds(r0, TILE_Q)] = (acc / l).T[HEAD_DIM:].astype(o_ref.dtype)
        lse_ref[pl.ds(r0, TILE_Q), :] = m + jnp.log(l)
        return carry

    lax.fori_loop(0, q_ref.shape[0] // TILE_Q, q_body, 0)


def backward_kernel(
    lo_ref, hi_ref, q_ref, kv_ref, do_ref, qt_ref, dot_ref, qseg_ref, kseg_ref, lse_ref,
    d_ref, dq_ref, dk_ref, dv_ref,
):
    scale = HEAD_DIM ** (-0.5)
    dk_ref[...] = jnp.zeros_like(dk_ref)
    dv_ref[...] = jnp.zeros_like(dv_ref)

    def q_body(i, carry):
        r0 = pl.multiple_of(i * TILE_Q, TILE_Q)
        q = q_ref[pl.ds(r0, TILE_Q), :] * jnp.asarray(scale, q_ref.dtype)
        do = do_ref[pl.ds(r0, TILE_Q), :]
        qs = qseg_ref[pl.ds(r0, TILE_Q), :]
        lse = lse_ref[pl.ds(r0, TILE_Q), :]
        dlt = d_ref[pl.ds(r0, TILE_Q), :]
        q_t = qt_ref[:, pl.ds(r0, TILE_Q)]
        do_t = dot_ref[:, pl.ds(r0, TILE_Q)]

        def k_body(j, dq):
            c0 = pl.multiple_of(j * TILE_K, TILE_K)
            kv = kv_ref[pl.ds(c0, TILE_K), :]
            ks = kseg_ref[:, pl.ds(c0, TILE_K)]
            s = lax.dot_general(q, kv, NT, preferred_element_type=jnp.float32)
            p = jnp.exp(jnp.where(qs == ks, s, -1e30) - lse)
            dp = lax.dot_general(do, kv, NT, preferred_element_type=jnp.float32)
            ds = (p * (dp - dlt)).astype(jnp.bfloat16)
            dk_ref[:, pl.ds(c0, TILE_K)] += jnp.dot(q_t, ds, preferred_element_type=jnp.float32)
            dv_ref[:, pl.ds(c0, TILE_K)] += jnp.dot(
                do_t, p.astype(jnp.bfloat16), preferred_element_type=jnp.float32
            )
            return dq + jnp.dot(ds, kv, preferred_element_type=jnp.float32)

        dq = lax.fori_loop(
            lo_ref[i], hi_ref[i], k_body, jnp.zeros((TILE_Q, kv_ref.shape[1]), jnp.float32)
        )
        dq_ref[pl.ds(r0, TILE_Q), :] = (scale * dq[:, :HEAD_DIM]).astype(dq_ref.dtype)
        return carry

    lax.fori_loop(0, q_ref.shape[0] // TILE_Q, q_body, 0)
    dk_ref[...] = scale * dk_ref[...]


def vmem_call(kernel, n_smem, n_vmem, out_shape):
    return pl.pallas_call(
        kernel,
        out_shape=out_shape,
        in_specs=[pl.BlockSpec(memory_space=pltpu.SMEM)] * n_smem
        + [pl.BlockSpec(memory_space=pltpu.VMEM)] * n_vmem,
        out_specs=[pl.BlockSpec(memory_space=pltpu.VMEM)] * len(out_shape),
    )


def segment_bounds(lengths, frames):
    ends = jnp.cumsum(lengths)
    starts = ends - lengths
    seg_start = jnp.max(jnp.where(starts[None, :] <= frames[:, None], starts[None, :], 0), axis=1)
    big = jnp.iinfo(jnp.int32).max
    seg_end = jnp.min(jnp.where(ends[None, :] > frames[:, None], ends[None, :], big), axis=1)
    return (seg_start, jnp.minimum(seg_end, ends[-1]))


def tile_ranges(lengths, base, ext_rows, block_rows):
    frames = base + (ext_rows - block_rows) // 2 + jnp.arange(block_rows, dtype=jnp.int32)
    seg_start, seg_end = segment_bounds(lengths, frames)
    lo = (seg_start[::TILE_Q] - base) // TILE_K
    hi = (seg_end[TILE_Q - 1 :: TILE_Q] - base + TILE_K - 1) // TILE_K
    lo = jnp.clip(lo, 0, ext_rows // TILE_K).astype(jnp.int32)
    hi = jnp.clip(hi, lo, ext_rows // TILE_K).astype(jnp.int32)
    return (lo, hi)


CONV_PAD = 128
CONV_CHUNK = 2048


def conv_chunk(x_ref, wt_ref, lo, hi, c0, sign):
    window = x_ref[:, pl.ds(c0, CONV_CHUNK + 2 * CONV_PAD)]
    width = window.shape[1]
    total = jnp.zeros((window.shape[0], CONV_CHUNK), jnp.float32)
    for tap in range(KERNEL):
        d = sign * (tap - KERNEL // 2)
        shifted = pltpu.roll(window, (width - d) % width, 1) if d else window
        keep = (lo <= d) & (d < hi)
        total = total + wt_ref[:, tap : tap + 1] * jnp.where(
            keep, shifted[:, CONV_PAD : CONV_PAD + CONV_CHUNK], 0.0
        )
    return total


def conv_forward_kernel(x_ref, wt_ref, gain_ref, cot_ref, lo_ref, hi_ref, out_ref, gc_ref):
    gain = gain_ref[...]

    def body(c, carry):
        c0 = pl.multiple_of(c * CONV_CHUNK, CONV_CHUNK)
        cols = pl.ds(c0, CONV_CHUNK)
        conv_sum = conv_chunk(x_ref, wt_ref, lo_ref[:, cols], hi_ref[:, cols], c0, 1)
        spread = jnp.sqrt(jnp.mean(conv_sum * conv_sum, axis=0, keepdims=True) + 1e-05)
        normed = conv_sum / spread
        pre_act = normed * gain
        gate = 1.0 / (1.0 + jnp.exp(-pre_act))
        out_ref[:, cols] = (pre_act * gate).astype(out_ref.dtype)
        grad_pre = cot_ref[:, cols].astype(jnp.float32) * gate * (1.0 + pre_act * (1.0 - gate))
        weighted = grad_pre * gain
        gc_ref[:, cols] = (
            weighted - normed * jnp.mean(weighted * normed, axis=0, keepdims=True)
        ) / spread
        return carry

    lax.fori_loop(0, out_ref.shape[1] // CONV_CHUNK, body, 0)


def conv_backward_kernel(y_ref, wt_ref, att_ref, lo_ref, hi_ref, ga_ref, dop_ref, delta_ref):
    def body(c, carry):
        c0 = pl.multiple_of(c * CONV_CHUNK, CONV_CHUNK)
        cols = pl.ds(c0, CONV_CHUNK)
        grad_sum = conv_chunk(y_ref, wt_ref, lo_ref[:, cols], hi_ref[:, cols], c0, -1)
        grad_att = grad_sum.astype(ga_ref.dtype)
        ga_ref[:, cols] = grad_att
        grad_f32 = grad_att.astype(jnp.float32)
        delta = jnp.sum(grad_f32 * att_ref[:, cols].astype(jnp.float32), axis=0, keepdims=True)
        rows = pl.ds(c0, CONV_CHUNK)
        delta_ref[rows, :] = jnp.broadcast_to(delta, (8, CONV_CHUNK)).T[:, :1]
        wide = jnp.concatenate([jnp.zeros_like(grad_f32), grad_f32], axis=0)
        dop_ref[rows, :] = wide.T.astype(dop_ref.dtype)
        return carry

    lax.fori_loop(0, ga_ref.shape[1] // CONV_CHUNK, body, 0)


def padded_rims(block, half):
    count = lax.axis_size("blk")
    forward = [(i, i + 1) for i in range(count - 1)]
    backward = [(target, source) for source, target in forward]
    low = lax.ppermute(block[:, block.shape[1] - half :], "blk", forward)
    high = lax.ppermute(block[:, :half], "blk", backward)
    gap = jnp.zeros((block.shape[0], CONV_PAD - half), jnp.float32)
    return jnp.concatenate(
        [gap, low.astype(jnp.float32), block.astype(jnp.float32), high.astype(jnp.float32), gap],
        axis=1,
    )


def on_device(queries, keys, values, lengths, conv_weight, norm_gain, cotangent):
    rows_in, width = queries.shape
    heads_total = width // HEAD_DIM
    stacked = jnp.stack(
        [a.reshape(rows_in, heads_total, HEAD_DIM) for a in (queries, keys, values)], axis=2
    ).reshape(rows_in, heads_total * 3 * HEAD_DIM)
    local_qkv = lax.all_to_all(stacked, "uly", split_axis=1, concat_axis=0, tiled=True)
    local_qkv = local_qkv.reshape(local_qkv.shape[0], -1, 3, HEAD_DIM)
    local_q, local_k, local_v = (
        local_qkv[:, :, i].reshape(local_qkv.shape[0], -1) for i in range(3)
    )
    block_rows, channels = local_q.shape
    heads_here = channels // HEAD_DIM
    maxlen = block_rows // 2
    rows_q = min(512, block_rows)
    window = rows_q + 2 * maxlen
    conv_half = KERNEL // 2
    block_count = block_rows // rows_q
    score_scale = HEAD_DIM ** (-0.5)
    frame_total = lax.axis_size("blk") * block_rows
    first_frame = lax.axis_index("blk") * block_rows
    seg_ext = segment_ids(
        lengths,
        first_frame - maxlen + jnp.arange(block_rows + 2 * maxlen, dtype=jnp.int32),
        frame_total,
    )
    seg_own = seg_ext[maxlen : maxlen + block_rows]
    seg_conv = seg_ext[maxlen - conv_half : maxlen + block_rows + conv_half]
    near_pairs = extended(jnp.concatenate([local_k, local_v], axis=1), (("blk", 0),), maxlen)
    k_ext = near_pairs[:, :channels].reshape(-1, heads_here, HEAD_DIM)
    v_ext = near_pairs[:, channels:].reshape(-1, heads_here, HEAD_DIM)
    q_heads = local_q.reshape(block_rows, heads_here, HEAD_DIM)
    starts = jnp.arange(block_count, dtype=jnp.int32) * rows_q

    assert heads_here == 1
    lo_t, hi_t = tile_ranges(lengths, first_frame - maxlen, block_rows + 2 * maxlen, block_rows)
    qseg_col = seg_own[:, None].astype(jnp.int32)
    kseg_row = seg_ext[None, :].astype(jnp.int32)
    lane_gap = jnp.zeros((block_rows, HEAD_DIM), jnp.bfloat16)
    q_wide = jnp.concatenate([local_q, lane_gap], axis=1)
    att_t, lse_col = vmem_call(
        forward_kernel,
        2,
        4,
        (
            jax.ShapeDtypeStruct((HEAD_DIM, block_rows), jnp.bfloat16),
            jax.ShapeDtypeStruct((block_rows, 1), jnp.float32),
        ),
    )(lo_t, hi_t, q_wide, near_pairs, qseg_col, kseg_row)
    frame_at = first_frame + jnp.arange(block_rows, dtype=jnp.int32)
    seg_start, seg_end = segment_bounds(lengths, frame_at)
    lo_off = (seg_start - frame_at)[None, :].astype(jnp.int32)
    hi_off = (seg_end - frame_at)[None, :].astype(jnp.int32)
    weight_t = conv_weight.T
    conv_out_t, grad_conv_t = vmem_call(
        conv_forward_kernel,
        0,
        6,
        (
            jax.ShapeDtypeStruct((HEAD_DIM, block_rows), jnp.bfloat16),
            jax.ShapeDtypeStruct((HEAD_DIM, block_rows), jnp.float32),
        ),
    )(padded_rims(att_t, conv_half), weight_t, norm_gain[:, None], cotangent, lo_off, hi_off)
    grad_att_t, grad_wide, row_delta = vmem_call(
        conv_backward_kernel,
        0,
        5,
        (
            jax.ShapeDtypeStruct((HEAD_DIM, block_rows), jnp.bfloat16),
            jax.ShapeDtypeStruct((block_rows, 2 * HEAD_DIM), jnp.bfloat16),
            jax.ShapeDtypeStruct((block_rows, 1), jnp.float32),
        ),
    )(padded_rims(grad_conv_t, conv_half), weight_t, att_t, lo_off, hi_off)

    ext_rows = block_rows + 2 * maxlen
    grad_q, dk_t, dv_t = vmem_call(
        backward_kernel,
        2,
        9,
        (
            jax.ShapeDtypeStruct((block_rows, HEAD_DIM), jnp.bfloat16),
            jax.ShapeDtypeStruct((HEAD_DIM, ext_rows), jnp.float32),
            jax.ShapeDtypeStruct((HEAD_DIM, ext_rows), jnp.float32),
        ),
    )(
        lo_t,
        hi_t,
        q_wide,
        near_pairs,
        grad_wide,
        local_q.T,
        grad_att_t,
        qseg_col,
        kseg_row,
        lse_col,
        row_delta,
    )
    ext_terms = jnp.concatenate([dk_t, dv_t], axis=0)
    received = []
    for rim_part, direction in ((ext_terms[:, :maxlen], -1), (ext_terms[:, maxlen + block_rows :], 1)):
        received.append(
            passed_along(rim_part.astype(jnp.bfloat16), "blk", direction).astype(rim_part.dtype)
        )
    key_grads = ext_terms[:, maxlen : maxlen + block_rows] + jnp.concatenate(
        [received[1], received[0]], axis=1
    )
    grad_queries = grad_q.reshape(block_rows, channels)
    grad_keys = key_grads[:HEAD_DIM].astype(jnp.bfloat16)
    grad_values = key_grads[HEAD_DIM:].astype(jnp.bfloat16)
    return (conv_out_t, grad_queries.T, grad_keys, grad_values)


def solution(mesh):
    in_specs = (
        P(("blk", "uly"), None),
        P(("blk", "uly"), None),
        P(("blk", "uly"), None),
        P(),
        P(None, "uly"),
        P("uly"),
        P("uly", "blk"),
    )
    out_specs = (P("uly", "blk"), P("uly", "blk"), P("uly", "blk"), P("uly", "blk"))
    return jax.shard_map(
        on_device, mesh=mesh, in_specs=in_specs, out_specs=out_specs, check_vma=False
    )
```

```python
import jax
import jax.numpy as jnp
import functools
from jax import lax
from jax.experimental import pallas as pl
from jax.experimental.pallas import tpu as pltpu
from jax.sharding import PartitionSpec as P

KERNEL = 31
HEAD_DIM = 64


def extended(block, sides, width):
    for axis, dim in sides:
        count = lax.axis_size(axis)
        forward = [(i, i + 1) for i in range(count - 1)]
        backward = [(target, source) for source, target in forward]
        low = lax.ppermute(
            lax.slice_in_dim(block, block.shape[dim] - width, None, axis=dim), axis, forward
        )
        high = lax.ppermute(lax.slice_in_dim(block, 0, width, axis=dim), axis, backward)
        block = jnp.concatenate([low, block, high], axis=dim)
    return block


def passed_along(block, axis, distance):
    devices = range(lax.axis_size(axis))
    route = [(i - distance, i) for i in devices if i - distance in devices]
    return lax.ppermute(block, axis, route)


def segment_ids(lengths, frames, frame_total):
    starts = jnp.cumsum(lengths) - lengths
    seg_ids = jnp.sum((starts[None, :] <= frames[:, None]).astype(jnp.int32), axis=1) - 1
    inside = (frames >= 0) & (frames < frame_total)
    return jnp.where(inside, seg_ids, -1)


def rows_at(values_in, row_start, row_count):
    return lax.dynamic_slice_in_dim(values_in, row_start, row_count, 0)


def masked_scores(query_rows, key_rows, query_seg, key_seg):
    scores = HEAD_DIM ** (-0.5) * jnp.einsum(
        "rhe,she->hrs", query_rows, key_rows, preferred_element_type=jnp.float32
    )
    same_seg = (query_seg[:, None] == key_seg[None, :])[None]
    return (scores, same_seg)


def weights_of(scores, same_seg, row_top, row_total):
    return jnp.where(same_seg, jnp.exp(scores - row_top), 0.0) / row_total


TILE_Q = 512
TILE_K = 512
NT = (((1,), (1,)), ((), ()))
TN = (((0,), (0,)), ((), ()))


def forward_kernel(lo_ref, hi_ref, q_ref, kv_ref, qseg_ref, kseg_ref, o_ref, lse_ref):
    scale = HEAD_DIM ** (-0.5)

    def q_body(i, carry):
        r0 = pl.multiple_of(i * TILE_Q, TILE_Q)
        q = q_ref[pl.ds(r0, TILE_Q), :] * jnp.asarray(scale, q_ref.dtype)
        qs = qseg_ref[pl.ds(r0, TILE_Q), :]

        def k_body(j, c):
            m, l, acc = c
            c0 = pl.multiple_of(j * TILE_K, TILE_K)
            kv = kv_ref[pl.ds(c0, TILE_K), :]
            ks = kseg_ref[:, pl.ds(c0, TILE_K)]
            s = lax.dot_general(q, kv, NT, preferred_element_type=jnp.float32)
            s = jnp.where(qs == ks, s, -1e30)
            m_new = jnp.maximum(m, jnp.max(s, axis=1, keepdims=True))
            alpha = jnp.exp(m - m_new)
            p = jnp.exp(s - m_new)
            l = alpha * l + jnp.sum(p, axis=1, keepdims=True)
            acc = alpha * acc + jnp.dot(
                p.astype(jnp.bfloat16), kv, preferred_element_type=jnp.float32
            )
            return (m_new, l, acc)

        init = (
            jnp.full((TILE_Q, 1), -1e30, jnp.float32),
            jnp.zeros((TILE_Q, 1), jnp.float32),
            jnp.zeros((TILE_Q, kv_ref.shape[1]), jnp.float32),
        )
        m, l, acc = lax.fori_loop(lo_ref[i], hi_ref[i], k_body, init)
        o_ref[:, pl.ds(r0, TILE_Q)] = (acc / l).T[HEAD_DIM:].astype(o_ref.dtype)
        lse_ref[pl.ds(r0, TILE_Q), :] = m + jnp.log(l)
        return carry

    lax.fori_loop(0, q_ref.shape[0] // TILE_Q, q_body, 0)


def backward_kernel(
    lo_ref, hi_ref, q_ref, kv_ref, do_ref, qt_ref, dot_ref, qseg_ref, kseg_ref, lse_ref,
    d_ref, dq_ref, dk_ref, dv_ref,
):
    scale = HEAD_DIM ** (-0.5)
    dk_ref[...] = jnp.zeros_like(dk_ref)
    dv_ref[...] = jnp.zeros_like(dv_ref)

    def q_body(i, carry):
        r0 = pl.multiple_of(i * TILE_Q, TILE_Q)
        q = q_ref[pl.ds(r0, TILE_Q), :] * jnp.asarray(scale, q_ref.dtype)
        do = do_ref[pl.ds(r0, TILE_Q), :]
        qs = qseg_ref[pl.ds(r0, TILE_Q), :]
        lse = lse_ref[pl.ds(r0, TILE_Q), :]
        dlt = d_ref[pl.ds(r0, TILE_Q), :]
        q_t = qt_ref[:, pl.ds(r0, TILE_Q)]
        do_t = dot_ref[:, pl.ds(r0, TILE_Q)]

        def k_body(j, dq):
            c0 = pl.multiple_of(j * TILE_K, TILE_K)
            kv = kv_ref[pl.ds(c0, TILE_K), :]
            ks = kseg_ref[:, pl.ds(c0, TILE_K)]
            s = lax.dot_general(q, kv, NT, preferred_element_type=jnp.float32)
            p = jnp.exp(jnp.where(qs == ks, s, -1e30) - lse)
            dp = lax.dot_general(do, kv, NT, preferred_element_type=jnp.float32)
            ds = (p * (dp - dlt)).astype(jnp.bfloat16)
            dk_ref[:, pl.ds(c0, TILE_K)] += jnp.dot(q_t, ds, preferred_element_type=jnp.float32)
            dv_ref[:, pl.ds(c0, TILE_K)] += jnp.dot(
                do_t, p.astype(jnp.bfloat16), preferred_element_type=jnp.float32
            )
            return dq + jnp.dot(ds, kv, preferred_element_type=jnp.float32)

        dq = lax.fori_loop(
            lo_ref[i], hi_ref[i], k_body, jnp.zeros((TILE_Q, kv_ref.shape[1]), jnp.float32)
        )
        dq_ref[pl.ds(r0, TILE_Q), :] = (scale * dq[:, :HEAD_DIM]).astype(dq_ref.dtype)
        return carry

    lax.fori_loop(0, q_ref.shape[0] // TILE_Q, q_body, 0)
    dk_ref[...] = scale * dk_ref[...]


def vmem_call(kernel, n_smem, n_vmem, out_shape):
    return pl.pallas_call(
        kernel,
        out_shape=out_shape,
        in_specs=[pl.BlockSpec(memory_space=pltpu.SMEM)] * n_smem
        + [pl.BlockSpec(memory_space=pltpu.VMEM)] * n_vmem,
        out_specs=[pl.BlockSpec(memory_space=pltpu.VMEM)] * len(out_shape),
    )


def segment_bounds(lengths, frames):
    ends = jnp.cumsum(lengths)
    starts = ends - lengths
    seg_start = jnp.max(jnp.where(starts[None, :] <= frames[:, None], starts[None, :], 0), axis=1)
    big = jnp.iinfo(jnp.int32).max
    seg_end = jnp.min(jnp.where(ends[None, :] > frames[:, None], ends[None, :], big), axis=1)
    return (seg_start, jnp.minimum(seg_end, ends[-1]))


def tile_ranges(lengths, base, ext_rows, block_rows):
    frames = base + (ext_rows - block_rows) // 2 + jnp.arange(block_rows, dtype=jnp.int32)
    seg_start, seg_end = segment_bounds(lengths, frames)
    lo = (seg_start[::TILE_Q] - base) // TILE_K
    hi = (seg_end[TILE_Q - 1 :: TILE_Q] - base + TILE_K - 1) // TILE_K
    lo = jnp.clip(lo, 0, ext_rows // TILE_K).astype(jnp.int32)
    hi = jnp.clip(hi, lo, ext_rows // TILE_K).astype(jnp.int32)
    return (lo, hi)


CONV_PAD = 128
CONV_CHUNK = 2048


def conv_chunk(x_ref, wt_ref, lo, hi, c0, sign):
    window = x_ref[:, pl.ds(c0, CONV_CHUNK + 2 * CONV_PAD)]
    width = window.shape[1]
    total = jnp.zeros((window.shape[0], CONV_CHUNK), jnp.float32)
    for tap in range(KERNEL):
        d = sign * (tap - KERNEL // 2)
        shifted = pltpu.roll(window, (width - d) % width, 1) if d else window
        keep = (lo <= d) & (d < hi)
        total = total + wt_ref[:, tap : tap + 1] * jnp.where(
            keep, shifted[:, CONV_PAD : CONV_PAD + CONV_CHUNK], 0.0
        )
    return total


def conv_forward_kernel(x_ref, wt_ref, gain_ref, cot_ref, lo_ref, hi_ref, out_ref, gc_ref):
    gain = gain_ref[...]

    def body(c, carry):
        c0 = pl.multiple_of(c * CONV_CHUNK, CONV_CHUNK)
        cols = pl.ds(c0, CONV_CHUNK)
        conv_sum = conv_chunk(x_ref, wt_ref, lo_ref[:, cols], hi_ref[:, cols], c0, 1)
        spread = jnp.sqrt(jnp.mean(conv_sum * conv_sum, axis=0, keepdims=True) + 1e-05)
        inv_spread = 1.0 / spread
        normed = conv_sum * inv_spread
        pre_act = normed * gain
        gate = 1.0 / (1.0 + jnp.exp(-pre_act))
        out_ref[:, cols] = (pre_act * gate).astype(out_ref.dtype)
        grad_pre = cot_ref[:, cols].astype(jnp.float32) * gate * (1.0 + pre_act * (1.0 - gate))
        weighted = grad_pre * gain
        gc_ref[:, cols] = (
            weighted - normed * jnp.mean(weighted * normed, axis=0, keepdims=True)
        ) * inv_spread
        return carry

    lax.fori_loop(0, out_ref.shape[1] // CONV_CHUNK, body, 0)


def conv_backward_kernel(y_ref, wt_ref, att_ref, lo_ref, hi_ref, ga_ref, dop_ref, delta_ref):
    def body(c, carry):
        c0 = pl.multiple_of(c * CONV_CHUNK, CONV_CHUNK)
        cols = pl.ds(c0, CONV_CHUNK)
        grad_sum = conv_chunk(y_ref, wt_ref, lo_ref[:, cols], hi_ref[:, cols], c0, -1)
        grad_att = grad_sum.astype(ga_ref.dtype)
        ga_ref[:, cols] = grad_att
        grad_f32 = grad_att.astype(jnp.float32)
        delta = jnp.sum(grad_f32 * att_ref[:, cols].astype(jnp.float32), axis=0, keepdims=True)
        rows = pl.ds(c0, CONV_CHUNK)
        delta_ref[rows, :] = jnp.broadcast_to(delta, (8, CONV_CHUNK)).T[:, :1]
        wide = jnp.concatenate([jnp.zeros_like(grad_f32), grad_f32], axis=0)
        dop_ref[rows, :] = wide.T.astype(dop_ref.dtype)
        return carry

    lax.fori_loop(0, ga_ref.shape[1] // CONV_CHUNK, body, 0)


def padded_rims(block, half):
    count = lax.axis_size("blk")
    forward = [(i, i + 1) for i in range(count - 1)]
    backward = [(target, source) for source, target in forward]
    low = lax.ppermute(block[:, block.shape[1] - half :], "blk", forward)
    high = lax.ppermute(block[:, :half], "blk", backward)
    gap = jnp.zeros((block.shape[0], CONV_PAD - half), jnp.float32)
    return jnp.concatenate(
        [gap, low.astype(jnp.float32), block.astype(jnp.float32), high.astype(jnp.float32), gap],
        axis=1,
    )


def on_device(queries, keys, values, lengths, conv_weight, norm_gain, cotangent):
    rows_in, width = queries.shape
    heads_total = width // HEAD_DIM
    stacked = jnp.stack(
        [a.reshape(rows_in, heads_total, HEAD_DIM) for a in (queries, keys, values)], axis=2
    ).reshape(rows_in, heads_total * 3 * HEAD_DIM)
    local_qkv = lax.all_to_all(stacked, "uly", split_axis=1, concat_axis=0, tiled=True)
    local_qkv = local_qkv.reshape(local_qkv.shape[0], -1, 3, HEAD_DIM)
    local_q, local_k, local_v = (
        local_qkv[:, :, i].reshape(local_qkv.shape[0], -1) for i in range(3)
    )
    block_rows, channels = local_q.shape
    heads_here = channels // HEAD_DIM
    maxlen = block_rows // 2
    rows_q = min(512, block_rows)
    window = rows_q + 2 * maxlen
    conv_half = KERNEL // 2
    block_count = block_rows // rows_q
    score_scale = HEAD_DIM ** (-0.5)
    frame_total = lax.axis_size("blk") * block_rows
    first_frame = lax.axis_index("blk") * block_rows
    seg_ext = segment_ids(
        lengths,
        first_frame - maxlen + jnp.arange(block_rows + 2 * maxlen, dtype=jnp.int32),
        frame_total,
    )
    seg_own = seg_ext[maxlen : maxlen + block_rows]
    seg_conv = seg_ext[maxlen - conv_half : maxlen + block_rows + conv_half]
    near_pairs = extended(jnp.concatenate([local_k, local_v], axis=1), (("blk", 0),), maxlen)
    k_ext = near_pairs[:, :channels].reshape(-1, heads_here, HEAD_DIM)
    v_ext = near_pairs[:, channels:].reshape(-1, heads_here, HEAD_DIM)
    q_heads = local_q.reshape(block_rows, heads_here, HEAD_DIM)
    starts = jnp.arange(block_count, dtype=jnp.int32) * rows_q

    assert heads_here == 1
    lo_t, hi_t = tile_ranges(lengths, first_frame - maxlen, block_rows + 2 * maxlen, block_rows)
    qseg_col = seg_own[:, None].astype(jnp.int32)
    kseg_row = seg_ext[None, :].astype(jnp.int32)
    lane_gap = jnp.zeros((block_rows, HEAD_DIM), jnp.bfloat16)
    q_wide = jnp.concatenate([local_q, lane_gap], axis=1)
    att_t, lse_col = vmem_call(
        forward_kernel,
        2,
        4,
        (
            jax.ShapeDtypeStruct((HEAD_DIM, block_rows), jnp.bfloat16),
            jax.ShapeDtypeStruct((block_rows, 1), jnp.float32),
        ),
    )(lo_t, hi_t, q_wide, near_pairs, qseg_col, kseg_row)
    frame_at = first_frame + jnp.arange(block_rows, dtype=jnp.int32)
    seg_start, seg_end = segment_bounds(lengths, frame_at)
    lo_off = (seg_start - frame_at)[None, :].astype(jnp.int32)
    hi_off = (seg_end - frame_at)[None, :].astype(jnp.int32)
    weight_t = conv_weight.T
    conv_out_t, grad_conv_t = vmem_call(
        conv_forward_kernel,
        0,
        6,
        (
            jax.ShapeDtypeStruct((HEAD_DIM, block_rows), jnp.bfloat16),
            jax.ShapeDtypeStruct((HEAD_DIM, block_rows), jnp.float32),
        ),
    )(padded_rims(att_t, conv_half), weight_t, norm_gain[:, None], cotangent, lo_off, hi_off)
    grad_att_t, grad_wide, row_delta = vmem_call(
        conv_backward_kernel,
        0,
        5,
        (
            jax.ShapeDtypeStruct((HEAD_DIM, block_rows), jnp.bfloat16),
            jax.ShapeDtypeStruct((block_rows, 2 * HEAD_DIM), jnp.bfloat16),
            jax.ShapeDtypeStruct((block_rows, 1), jnp.float32),
        ),
    )(padded_rims(grad_conv_t, conv_half), weight_t, att_t, lo_off, hi_off)

    ext_rows = block_rows + 2 * maxlen
    grad_q, dk_t, dv_t = vmem_call(
        backward_kernel,
        2,
        9,
        (
            jax.ShapeDtypeStruct((block_rows, HEAD_DIM), jnp.bfloat16),
            jax.ShapeDtypeStruct((HEAD_DIM, ext_rows), jnp.float32),
            jax.ShapeDtypeStruct((HEAD_DIM, ext_rows), jnp.float32),
        ),
    )(
        lo_t,
        hi_t,
        q_wide,
        near_pairs,
        grad_wide,
        local_q.T,
        grad_att_t,
        qseg_col,
        kseg_row,
        lse_col,
        row_delta,
    )
    ext_terms = jnp.concatenate([dk_t, dv_t], axis=0)
    received = []
    for rim_part, direction in ((ext_terms[:, :maxlen], -1), (ext_terms[:, maxlen + block_rows :], 1)):
        received.append(
            passed_along(rim_part.astype(jnp.bfloat16), "blk", direction).astype(rim_part.dtype)
        )
    key_grads = ext_terms[:, maxlen : maxlen + block_rows] + jnp.concatenate(
        [received[1], received[0]], axis=1
    )
    grad_queries = grad_q.reshape(block_rows, channels)
    grad_keys = key_grads[:HEAD_DIM].astype(jnp.bfloat16)
    grad_values = key_grads[HEAD_DIM:].astype(jnp.bfloat16)
    return (conv_out_t, grad_queries.T, grad_keys, grad_values)


def solution(mesh):
    in_specs = (
        P(("blk", "uly"), None),
        P(("blk", "uly"), None),
        P(("blk", "uly"), None),
        P(),
        P(None, "uly"),
        P("uly"),
        P("uly", "blk"),
    )
    out_specs = (P("uly", "blk"), P("uly", "blk"), P("uly", "blk"), P("uly", "blk"))
    return jax.shard_map(
        on_device, mesh=mesh, in_specs=in_specs, out_specs=out_specs, check_vma=False
    )
```

```python
import jax
import jax.numpy as jnp
import functools
from jax import lax
from jax.experimental import pallas as pl
from jax.experimental.pallas import tpu as pltpu
from jax.sharding import PartitionSpec as P

KERNEL = 31
HEAD_DIM = 64


def extended(block, sides, width):
    for axis, dim in sides:
        count = lax.axis_size(axis)
        forward = [(i, i + 1) for i in range(count - 1)]
        backward = [(target, source) for source, target in forward]
        low = lax.ppermute(
            lax.slice_in_dim(block, block.shape[dim] - width, None, axis=dim), axis, forward
        )
        high = lax.ppermute(lax.slice_in_dim(block, 0, width, axis=dim), axis, backward)
        block = jnp.concatenate([low, block, high], axis=dim)
    return block


def passed_along(block, axis, distance):
    devices = range(lax.axis_size(axis))
    route = [(i - distance, i) for i in devices if i - distance in devices]
    return lax.ppermute(block, axis, route)


def segment_ids(lengths, frames, frame_total):
    starts = jnp.cumsum(lengths) - lengths
    seg_ids = jnp.sum((starts[None, :] <= frames[:, None]).astype(jnp.int32), axis=1) - 1
    inside = (frames >= 0) & (frames < frame_total)
    return jnp.where(inside, seg_ids, -1)


def rows_at(values_in, row_start, row_count):
    return lax.dynamic_slice_in_dim(values_in, row_start, row_count, 0)


def masked_scores(query_rows, key_rows, query_seg, key_seg):
    scores = HEAD_DIM ** (-0.5) * jnp.einsum(
        "rhe,she->hrs", query_rows, key_rows, preferred_element_type=jnp.float32
    )
    same_seg = (query_seg[:, None] == key_seg[None, :])[None]
    return (scores, same_seg)


def weights_of(scores, same_seg, row_top, row_total):
    return jnp.where(same_seg, jnp.exp(scores - row_top), 0.0) / row_total


TILE_Q = 256
TILE_K = 1024
NT = (((1,), (1,)), ((), ()))
TN = (((0,), (0,)), ((), ()))


def forward_kernel(lo_ref, hi_ref, q_ref, kv_ref, qseg_ref, kseg_ref, o_ref, lse_ref):
    scale = HEAD_DIM ** (-0.5)

    def q_body(i, carry):
        r0 = pl.multiple_of(i * TILE_Q, TILE_Q)
        q = q_ref[pl.ds(r0, TILE_Q), :] * jnp.asarray(scale, q_ref.dtype)
        qs = qseg_ref[pl.ds(r0, TILE_Q), :]

        def k_body(j, c):
            m, l, acc = c
            c0 = pl.multiple_of(j * TILE_K, TILE_K)
            kv = kv_ref[pl.ds(c0, TILE_K), :]
            ks = kseg_ref[:, pl.ds(c0, TILE_K)]
            s = lax.dot_general(q, kv, NT, preferred_element_type=jnp.float32)
            s = jnp.where(qs == ks, s, -1e30)
            m_new = jnp.maximum(m, jnp.max(s, axis=1, keepdims=True))
            alpha = jnp.exp(m - m_new)
            p = jnp.exp(s - m_new)
            l = alpha * l + jnp.sum(p, axis=1, keepdims=True)
            acc = alpha * acc + jnp.dot(
                p.astype(jnp.bfloat16), kv, preferred_element_type=jnp.float32
            )
            return (m_new, l, acc)

        init = (
            jnp.full((TILE_Q, 1), -1e30, jnp.float32),
            jnp.zeros((TILE_Q, 1), jnp.float32),
            jnp.zeros((TILE_Q, kv_ref.shape[1]), jnp.float32),
        )
        m, l, acc = lax.fori_loop(lo_ref[i], hi_ref[i], k_body, init)
        o_ref[:, pl.ds(r0, TILE_Q)] = (acc / l).T[HEAD_DIM:].astype(o_ref.dtype)
        lse_ref[pl.ds(r0, TILE_Q), :] = m + jnp.log(l)
        return carry

    lax.fori_loop(0, q_ref.shape[0] // TILE_Q, q_body, 0)


def backward_kernel(
    lo_ref, hi_ref, q_ref, kv_ref, do_ref, qt_ref, dot_ref, qseg_ref, kseg_ref, lse_ref,
    d_ref, dq_ref, dk_ref, dv_ref,
):
    scale = HEAD_DIM ** (-0.5)
    dk_ref[...] = jnp.zeros_like(dk_ref)
    dv_ref[...] = jnp.zeros_like(dv_ref)

    def q_body(i, carry):
        r0 = pl.multiple_of(i * TILE_Q, TILE_Q)
        q = q_ref[pl.ds(r0, TILE_Q), :] * jnp.asarray(scale, q_ref.dtype)
        do = do_ref[pl.ds(r0, TILE_Q), :]
        qs = qseg_ref[pl.ds(r0, TILE_Q), :]
        lse = lse_ref[pl.ds(r0, TILE_Q), :]
        dlt = d_ref[pl.ds(r0, TILE_Q), :]
        q_t = qt_ref[:, pl.ds(r0, TILE_Q)]
        do_t = dot_ref[:, pl.ds(r0, TILE_Q)]

        def k_body(j, dq):
            c0 = pl.multiple_of(j * TILE_K, TILE_K)
            kv = kv_ref[pl.ds(c0, TILE_K), :]
            ks = kseg_ref[:, pl.ds(c0, TILE_K)]
            s = lax.dot_general(q, kv, NT, preferred_element_type=jnp.float32)
            p = jnp.exp(jnp.where(qs == ks, s, -1e30) - lse)
            dp = lax.dot_general(do, kv, NT, preferred_element_type=jnp.float32)
            ds = (p * (dp - dlt)).astype(jnp.bfloat16)
            dk_ref[:, pl.ds(c0, TILE_K)] += jnp.dot(q_t, ds, preferred_element_type=jnp.float32)
            dv_ref[:, pl.ds(c0, TILE_K)] += jnp.dot(
                do_t, p.astype(jnp.bfloat16), preferred_element_type=jnp.float32
            )
            return dq + jnp.dot(ds, kv, preferred_element_type=jnp.float32)

        dq = lax.fori_loop(
            lo_ref[i], hi_ref[i], k_body, jnp.zeros((TILE_Q, kv_ref.shape[1]), jnp.float32)
        )
        dq_ref[pl.ds(r0, TILE_Q), :] = (scale * dq[:, :HEAD_DIM]).astype(dq_ref.dtype)
        return carry

    lax.fori_loop(0, q_ref.shape[0] // TILE_Q, q_body, 0)
    dk_ref[...] = scale * dk_ref[...]


def vmem_call(kernel, n_smem, n_vmem, out_shape):
    return pl.pallas_call(
        kernel,
        out_shape=out_shape,
        in_specs=[pl.BlockSpec(memory_space=pltpu.SMEM)] * n_smem
        + [pl.BlockSpec(memory_space=pltpu.VMEM)] * n_vmem,
        out_specs=[pl.BlockSpec(memory_space=pltpu.VMEM)] * len(out_shape),
    )


def segment_bounds(lengths, frames):
    ends = jnp.cumsum(lengths)
    starts = ends - lengths
    seg_start = jnp.max(jnp.where(starts[None, :] <= frames[:, None], starts[None, :], 0), axis=1)
    big = jnp.iinfo(jnp.int32).max
    seg_end = jnp.min(jnp.where(ends[None, :] > frames[:, None], ends[None, :], big), axis=1)
    return (seg_start, jnp.minimum(seg_end, ends[-1]))


def tile_ranges(lengths, base, ext_rows, block_rows):
    frames = base + (ext_rows - block_rows) // 2 + jnp.arange(block_rows, dtype=jnp.int32)
    seg_start, seg_end = segment_bounds(lengths, frames)
    lo = (seg_start[::TILE_Q] - base) // TILE_K
    hi = (seg_end[TILE_Q - 1 :: TILE_Q] - base + TILE_K - 1) // TILE_K
    lo = jnp.clip(lo, 0, ext_rows // TILE_K).astype(jnp.int32)
    hi = jnp.clip(hi, lo, ext_rows // TILE_K).astype(jnp.int32)
    return (lo, hi)


CONV_PAD = 128
CONV_CHUNK = 2048


def conv_chunk(x_ref, wt_ref, lo, hi, c0, sign):
    window = x_ref[:, pl.ds(c0, CONV_CHUNK + 2 * CONV_PAD)]
    width = window.shape[1]
    total = jnp.zeros((window.shape[0], CONV_CHUNK), jnp.float32)
    for tap in range(KERNEL):
        d = sign * (tap - KERNEL // 2)
        shifted = pltpu.roll(window, (width - d) % width, 1) if d else window
        keep = (lo <= d) & (d < hi)
        total = total + wt_ref[:, tap : tap + 1] * jnp.where(
            keep, shifted[:, CONV_PAD : CONV_PAD + CONV_CHUNK], 0.0
        )
    return total


def conv_forward_kernel(x_ref, wt_ref, gain_ref, cot_ref, lo_ref, hi_ref, out_ref, gc_ref):
    gain = gain_ref[...]

    def body(c, carry):
        c0 = pl.multiple_of(c * CONV_CHUNK, CONV_CHUNK)
        cols = pl.ds(c0, CONV_CHUNK)
        conv_sum = conv_chunk(x_ref, wt_ref, lo_ref[:, cols], hi_ref[:, cols], c0, 1)
        spread = jnp.sqrt(jnp.mean(conv_sum * conv_sum, axis=0, keepdims=True) + 1e-05)
        normed = conv_sum / spread
        pre_act = normed * gain
        gate = 1.0 / (1.0 + jnp.exp(-pre_act))
        out_ref[:, cols] = (pre_act * gate).astype(out_ref.dtype)
        grad_pre = cot_ref[:, cols].astype(jnp.float32) * gate * (1.0 + pre_act * (1.0 - gate))
        weighted = grad_pre * gain
        gc_ref[:, cols] = (
            weighted - normed * jnp.mean(weighted * normed, axis=0, keepdims=True)
        ) / spread
        return carry

    lax.fori_loop(0, out_ref.shape[1] // CONV_CHUNK, body, 0)


def conv_backward_kernel(y_ref, wt_ref, att_ref, lo_ref, hi_ref, ga_ref, dop_ref, delta_ref):
    def body(c, carry):
        c0 = pl.multiple_of(c * CONV_CHUNK, CONV_CHUNK)
        cols = pl.ds(c0, CONV_CHUNK)
        grad_sum = conv_chunk(y_ref, wt_ref, lo_ref[:, cols], hi_ref[:, cols], c0, -1)
        grad_att = grad_sum.astype(ga_ref.dtype)
        ga_ref[:, cols] = grad_att
        grad_f32 = grad_att.astype(jnp.float32)
        delta = jnp.sum(grad_f32 * att_ref[:, cols].astype(jnp.float32), axis=0, keepdims=True)
        rows = pl.ds(c0, CONV_CHUNK)
        delta_ref[rows, :] = jnp.broadcast_to(delta, (8, CONV_CHUNK)).T[:, :1]
        wide = jnp.concatenate([jnp.zeros_like(grad_f32), grad_f32], axis=0)
        dop_ref[rows, :] = wide.T.astype(dop_ref.dtype)
        return carry

    lax.fori_loop(0, ga_ref.shape[1] // CONV_CHUNK, body, 0)


def padded_rims(block, half):
    count = lax.axis_size("blk")
    forward = [(i, i + 1) for i in range(count - 1)]
    backward = [(target, source) for source, target in forward]
    low = lax.ppermute(block[:, block.shape[1] - half :], "blk", forward)
    high = lax.ppermute(block[:, :half], "blk", backward)
    gap = jnp.zeros((block.shape[0], CONV_PAD - half), jnp.float32)
    return jnp.concatenate(
        [gap, low.astype(jnp.float32), block.astype(jnp.float32), high.astype(jnp.float32), gap],
        axis=1,
    )


def on_device(queries, keys, values, lengths, conv_weight, norm_gain, cotangent):
    rows_in, width = queries.shape
    heads_total = width // HEAD_DIM
    stacked = jnp.stack(
        [a.reshape(rows_in, heads_total, HEAD_DIM) for a in (queries, keys, values)], axis=2
    ).reshape(rows_in, heads_total * 3 * HEAD_DIM)
    local_qkv = lax.all_to_all(stacked, "uly", split_axis=1, concat_axis=0, tiled=True)
    local_qkv = local_qkv.reshape(local_qkv.shape[0], -1, 3, HEAD_DIM)
    local_q, local_k, local_v = (
        local_qkv[:, :, i].reshape(local_qkv.shape[0], -1) for i in range(3)
    )
    block_rows, channels = local_q.shape
    heads_here = channels // HEAD_DIM
    maxlen = block_rows // 2
    rows_q = min(512, block_rows)
    window = rows_q + 2 * maxlen
    conv_half = KERNEL // 2
    block_count = block_rows // rows_q
    score_scale = HEAD_DIM ** (-0.5)
    frame_total = lax.axis_size("blk") * block_rows
    first_frame = lax.axis_index("blk") * block_rows
    seg_ext = segment_ids(
        lengths,
        first_frame - maxlen + jnp.arange(block_rows + 2 * maxlen, dtype=jnp.int32),
        frame_total,
    )
    seg_own = seg_ext[maxlen : maxlen + block_rows]
    seg_conv = seg_ext[maxlen - conv_half : maxlen + block_rows + conv_half]
    near_pairs = extended(jnp.concatenate([local_k, local_v], axis=1), (("blk", 0),), maxlen)
    k_ext = near_pairs[:, :channels].reshape(-1, heads_here, HEAD_DIM)
    v_ext = near_pairs[:, channels:].reshape(-1, heads_here, HEAD_DIM)
    q_heads = local_q.reshape(block_rows, heads_here, HEAD_DIM)
    starts = jnp.arange(block_count, dtype=jnp.int32) * rows_q

    assert heads_here == 1
    lo_t, hi_t = tile_ranges(lengths, first_frame - maxlen, block_rows + 2 * maxlen, block_rows)
    qseg_col = seg_own[:, None].astype(jnp.int32)
    kseg_row = seg_ext[None, :].astype(jnp.int32)
    lane_gap = jnp.zeros((block_rows, HEAD_DIM), jnp.bfloat16)
    q_wide = jnp.concatenate([local_q, lane_gap], axis=1)
    att_t, lse_col = vmem_call(
        forward_kernel,
        2,
        4,
        (
            jax.ShapeDtypeStruct((HEAD_DIM, block_rows), jnp.bfloat16),
            jax.ShapeDtypeStruct((block_rows, 1), jnp.float32),
        ),
    )(lo_t, hi_t, q_wide, near_pairs, qseg_col, kseg_row)
    frame_at = first_frame + jnp.arange(block_rows, dtype=jnp.int32)
    seg_start, seg_end = segment_bounds(lengths, frame_at)
    lo_off = (seg_start - frame_at)[None, :].astype(jnp.int32)
    hi_off = (seg_end - frame_at)[None, :].astype(jnp.int32)
    weight_t = conv_weight.T
    conv_out_t, grad_conv_t = vmem_call(
        conv_forward_kernel,
        0,
        6,
        (
            jax.ShapeDtypeStruct((HEAD_DIM, block_rows), jnp.bfloat16),
            jax.ShapeDtypeStruct((HEAD_DIM, block_rows), jnp.float32),
        ),
    )(padded_rims(att_t, conv_half), weight_t, norm_gain[:, None], cotangent, lo_off, hi_off)
    grad_att_t, grad_wide, row_delta = vmem_call(
        conv_backward_kernel,
        0,
        5,
        (
            jax.ShapeDtypeStruct((HEAD_DIM, block_rows), jnp.bfloat16),
            jax.ShapeDtypeStruct((block_rows, 2 * HEAD_DIM), jnp.bfloat16),
            jax.ShapeDtypeStruct((block_rows, 1), jnp.float32),
        ),
    )(padded_rims(grad_conv_t, conv_half), weight_t, att_t, lo_off, hi_off)

    ext_rows = block_rows + 2 * maxlen
    grad_q, dk_t, dv_t = vmem_call(
        backward_kernel,
        2,
        9,
        (
            jax.ShapeDtypeStruct((block_rows, HEAD_DIM), jnp.bfloat16),
            jax.ShapeDtypeStruct((HEAD_DIM, ext_rows), jnp.float32),
            jax.ShapeDtypeStruct((HEAD_DIM, ext_rows), jnp.float32),
        ),
    )(
        lo_t,
        hi_t,
        q_wide,
        near_pairs,
        grad_wide,
        local_q.T,
        grad_att_t,
        qseg_col,
        kseg_row,
        lse_col,
        row_delta,
    )
    ext_terms = jnp.concatenate([dk_t, dv_t], axis=0)
    received = []
    for rim_part, direction in ((ext_terms[:, :maxlen], -1), (ext_terms[:, maxlen + block_rows :], 1)):
        received.append(
            passed_along(rim_part.astype(jnp.bfloat16), "blk", direction).astype(rim_part.dtype)
        )
    key_grads = ext_terms[:, maxlen : maxlen + block_rows] + jnp.concatenate(
        [received[1], received[0]], axis=1
    )
    grad_queries = grad_q.reshape(block_rows, channels)
    grad_keys = key_grads[:HEAD_DIM].astype(jnp.bfloat16)
    grad_values = key_grads[HEAD_DIM:].astype(jnp.bfloat16)
    return (conv_out_t, grad_queries.T, grad_keys, grad_values)


def solution(mesh):
    in_specs = (
        P(("blk", "uly"), None),
        P(("blk", "uly"), None),
        P(("blk", "uly"), None),
        P(),
        P(None, "uly"),
        P("uly"),
        P("uly", "blk"),
    )
    out_specs = (P("uly", "blk"), P("uly", "blk"), P("uly", "blk"), P("uly", "blk"))
    return jax.shard_map(
        on_device, mesh=mesh, in_specs=in_specs, out_specs=out_specs, check_vma=False
    )
```

```python
import jax
import jax.numpy as jnp
import functools
from jax import lax
from jax.experimental import pallas as pl
from jax.experimental.pallas import tpu as pltpu
from jax.sharding import PartitionSpec as P

KERNEL = 31
HEAD_DIM = 64


def extended(block, sides, width):
    for axis, dim in sides:
        count = lax.axis_size(axis)
        forward = [(i, i + 1) for i in range(count - 1)]
        backward = [(target, source) for source, target in forward]
        low = lax.ppermute(
            lax.slice_in_dim(block, block.shape[dim] - width, None, axis=dim), axis, forward
        )
        high = lax.ppermute(lax.slice_in_dim(block, 0, width, axis=dim), axis, backward)
        block = jnp.concatenate([low, block, high], axis=dim)
    return block


def passed_along(block, axis, distance):
    devices = range(lax.axis_size(axis))
    route = [(i - distance, i) for i in devices if i - distance in devices]
    return lax.ppermute(block, axis, route)


def segment_ids(lengths, frames, frame_total):
    starts = jnp.cumsum(lengths) - lengths
    seg_ids = jnp.sum((starts[None, :] <= frames[:, None]).astype(jnp.int32), axis=1) - 1
    inside = (frames >= 0) & (frames < frame_total)
    return jnp.where(inside, seg_ids, -1)


def rows_at(values_in, row_start, row_count):
    return lax.dynamic_slice_in_dim(values_in, row_start, row_count, 0)


def masked_scores(query_rows, key_rows, query_seg, key_seg):
    scores = HEAD_DIM ** (-0.5) * jnp.einsum(
        "rhe,she->hrs", query_rows, key_rows, preferred_element_type=jnp.float32
    )
    same_seg = (query_seg[:, None] == key_seg[None, :])[None]
    return (scores, same_seg)


def weights_of(scores, same_seg, row_top, row_total):
    return jnp.where(same_seg, jnp.exp(scores - row_top), 0.0) / row_total


TILE_Q = 512
TILE_K = 512
NT = (((1,), (1,)), ((), ()))
TN = (((0,), (0,)), ((), ()))


def forward_kernel(lo_ref, hi_ref, q_ref, kv_ref, qseg_ref, kseg_ref, o_ref, lse_ref):
    scale = HEAD_DIM ** (-0.5)

    def q_body(i, carry):
        r0 = pl.multiple_of(i * TILE_Q, TILE_Q)
        q = q_ref[pl.ds(r0, TILE_Q), :] * jnp.asarray(scale, q_ref.dtype)
        qs = qseg_ref[pl.ds(r0, TILE_Q), :]

        def k_body(j, c):
            m, l, acc = c
            c0 = pl.multiple_of(j * TILE_K, TILE_K)
            kv = kv_ref[pl.ds(c0, TILE_K), :]
            ks = kseg_ref[:, pl.ds(c0, TILE_K)]
            s = lax.dot_general(q, kv, NT, preferred_element_type=jnp.float32)
            s = jnp.where(qs == ks, s, -1e30)
            m_new = jnp.maximum(m, jnp.max(s, axis=1, keepdims=True))
            alpha = jnp.exp(m - m_new)
            p = jnp.exp(s - m_new)
            l = alpha * l + jnp.sum(p, axis=1, keepdims=True)
            acc = alpha * acc + jnp.dot(
                p.astype(jnp.bfloat16), kv, preferred_element_type=jnp.float32
            )
            return (m_new, l, acc)

        init = (
            jnp.full((TILE_Q, 1), -1e30, jnp.float32),
            jnp.zeros((TILE_Q, 1), jnp.float32),
            jnp.zeros((TILE_Q, kv_ref.shape[1]), jnp.float32),
        )
        m, l, acc = lax.fori_loop(lo_ref[i], hi_ref[i], k_body, init)
        o_ref[:, pl.ds(r0, TILE_Q)] = (acc / l).T[HEAD_DIM:].astype(o_ref.dtype)
        lse_ref[pl.ds(r0, TILE_Q), :] = m + jnp.log(l)
        return carry

    lax.fori_loop(0, q_ref.shape[0] // TILE_Q, q_body, 0)


def backward_kernel(
    lo_ref, hi_ref, q_ref, kv_ref, do_ref, qt_ref, dot_ref, qseg_ref, kseg_ref, lse_ref,
    d_ref, dq_ref, dkv_ref,
):
    scale = HEAD_DIM ** (-0.5)
    dkv_ref[...] = jnp.zeros_like(dkv_ref)

    def q_body(i, carry):
        r0 = pl.multiple_of(i * TILE_Q, TILE_Q)
        q = q_ref[pl.ds(r0, TILE_Q), :] * jnp.asarray(scale, q_ref.dtype)
        do = do_ref[pl.ds(r0, TILE_Q), :]
        qs = qseg_ref[pl.ds(r0, TILE_Q), :]
        lse = lse_ref[pl.ds(r0, TILE_Q), :]
        dlt = d_ref[pl.ds(r0, TILE_Q), :]
        q_t = qt_ref[:, pl.ds(r0, TILE_Q)]
        do_t = dot_ref[:, pl.ds(r0, TILE_Q)]

        def k_body(j, dq):
            c0 = pl.multiple_of(j * TILE_K, TILE_K)
            kv = kv_ref[pl.ds(c0, TILE_K), :]
            ks = kseg_ref[:, pl.ds(c0, TILE_K)]
            s = lax.dot_general(q, kv, NT, preferred_element_type=jnp.float32)
            p = jnp.exp(jnp.where(qs == ks, s, -1e30) - lse)
            dp = lax.dot_general(do, kv, NT, preferred_element_type=jnp.float32)
            ds = (p * (dp - dlt)).astype(jnp.bfloat16)
            dkv_ref[:HEAD_DIM, pl.ds(c0, TILE_K)] += jnp.dot(
                q_t, ds, preferred_element_type=jnp.float32
            )
            dkv_ref[HEAD_DIM:, pl.ds(c0, TILE_K)] += jnp.dot(
                do_t, p.astype(jnp.bfloat16), preferred_element_type=jnp.float32
            )
            return dq + jnp.dot(ds, kv, preferred_element_type=jnp.float32)

        dq = lax.fori_loop(
            lo_ref[i], hi_ref[i], k_body, jnp.zeros((TILE_Q, kv_ref.shape[1]), jnp.float32)
        )
        dq_ref[pl.ds(r0, TILE_Q), :] = (scale * dq[:, :HEAD_DIM]).astype(dq_ref.dtype)
        return carry

    lax.fori_loop(0, q_ref.shape[0] // TILE_Q, q_body, 0)
    dkv_ref[:HEAD_DIM, :] = scale * dkv_ref[:HEAD_DIM, :]


def vmem_call(kernel, n_smem, n_vmem, out_shape):
    return pl.pallas_call(
        kernel,
        out_shape=out_shape,
        in_specs=[pl.BlockSpec(memory_space=pltpu.SMEM)] * n_smem
        + [pl.BlockSpec(memory_space=pltpu.VMEM)] * n_vmem,
        out_specs=[pl.BlockSpec(memory_space=pltpu.VMEM)] * len(out_shape),
    )


def segment_bounds(lengths, frames):
    ends = jnp.cumsum(lengths)
    starts = ends - lengths
    seg_start = jnp.max(jnp.where(starts[None, :] <= frames[:, None], starts[None, :], 0), axis=1)
    big = jnp.iinfo(jnp.int32).max
    seg_end = jnp.min(jnp.where(ends[None, :] > frames[:, None], ends[None, :], big), axis=1)
    return (seg_start, jnp.minimum(seg_end, ends[-1]))


def tile_ranges(lengths, base, ext_rows, block_rows):
    frames = base + (ext_rows - block_rows) // 2 + jnp.arange(block_rows, dtype=jnp.int32)
    seg_start, seg_end = segment_bounds(lengths, frames)
    lo = (seg_start[::TILE_Q] - base) // TILE_K
    hi = (seg_end[TILE_Q - 1 :: TILE_Q] - base + TILE_K - 1) // TILE_K
    lo = jnp.clip(lo, 0, ext_rows // TILE_K).astype(jnp.int32)
    hi = jnp.clip(hi, lo, ext_rows // TILE_K).astype(jnp.int32)
    return (lo, hi)


CONV_PAD = 128
CONV_CHUNK = 2048


def conv_chunk(x_ref, wt_ref, lo, hi, c0, sign):
    window = x_ref[:, pl.ds(c0, CONV_CHUNK + 2 * CONV_PAD)]
    width = window.shape[1]
    total = jnp.zeros((window.shape[0], CONV_CHUNK), jnp.float32)
    for tap in range(KERNEL):
        d = sign * (tap - KERNEL // 2)
        shifted = pltpu.roll(window, (width - d) % width, 1) if d else window
        keep = (lo <= d) & (d < hi)
        total = total + wt_ref[:, tap : tap + 1] * jnp.where(
            keep, shifted[:, CONV_PAD : CONV_PAD + CONV_CHUNK], 0.0
        )
    return total


def conv_forward_kernel(x_ref, wt_ref, gain_ref, cot_ref, lo_ref, hi_ref, out_ref, gc_ref):
    gain = gain_ref[...]

    def body(c, carry):
        c0 = pl.multiple_of(c * CONV_CHUNK, CONV_CHUNK)
        cols = pl.ds(c0, CONV_CHUNK)
        conv_sum = conv_chunk(x_ref, wt_ref, lo_ref[:, cols], hi_ref[:, cols], c0, 1)
        spread = jnp.sqrt(jnp.mean(conv_sum * conv_sum, axis=0, keepdims=True) + 1e-05)
        normed = conv_sum / spread
        pre_act = normed * gain
        gate = 1.0 / (1.0 + jnp.exp(-pre_act))
        out_ref[:, cols] = (pre_act * gate).astype(out_ref.dtype)
        grad_pre = cot_ref[:, cols].astype(jnp.float32) * gate * (1.0 + pre_act * (1.0 - gate))
        weighted = grad_pre * gain
        gc_ref[:, cols] = (
            weighted - normed * jnp.mean(weighted * normed, axis=0, keepdims=True)
        ) / spread
        return carry

    lax.fori_loop(0, out_ref.shape[1] // CONV_CHUNK, body, 0)


def conv_backward_kernel(y_ref, wt_ref, att_ref, lo_ref, hi_ref, ga_ref, dop_ref, delta_ref):
    def body(c, carry):
        c0 = pl.multiple_of(c * CONV_CHUNK, CONV_CHUNK)
        cols = pl.ds(c0, CONV_CHUNK)
        grad_sum = conv_chunk(y_ref, wt_ref, lo_ref[:, cols], hi_ref[:, cols], c0, -1)
        grad_att = grad_sum.astype(ga_ref.dtype)
        ga_ref[:, cols] = grad_att
        grad_f32 = grad_att.astype(jnp.float32)
        delta = jnp.sum(grad_f32 * att_ref[:, cols].astype(jnp.float32), axis=0, keepdims=True)
        rows = pl.ds(c0, CONV_CHUNK)
        delta_ref[rows, :] = jnp.broadcast_to(delta, (8, CONV_CHUNK)).T[:, :1]
        wide = jnp.concatenate([jnp.zeros_like(grad_f32), grad_f32], axis=0)
        dop_ref[rows, :] = wide.T.astype(dop_ref.dtype)
        return carry

    lax.fori_loop(0, ga_ref.shape[1] // CONV_CHUNK, body, 0)


def padded_rims(block, half):
    count = lax.axis_size("blk")
    forward = [(i, i + 1) for i in range(count - 1)]
    backward = [(target, source) for source, target in forward]
    low = lax.ppermute(block[:, block.shape[1] - half :], "blk", forward)
    high = lax.ppermute(block[:, :half], "blk", backward)
    gap = jnp.zeros((block.shape[0], CONV_PAD - half), jnp.float32)
    return jnp.concatenate(
        [gap, low.astype(jnp.float32), block.astype(jnp.float32), high.astype(jnp.float32), gap],
        axis=1,
    )


def on_device(queries, keys, values, lengths, conv_weight, norm_gain, cotangent):
    rows_in, width = queries.shape
    heads_total = width // HEAD_DIM
    stacked = jnp.stack(
        [a.reshape(rows_in, heads_total, HEAD_DIM) for a in (queries, keys, values)], axis=2
    ).reshape(rows_in, heads_total * 3 * HEAD_DIM)
    local_qkv = lax.all_to_all(stacked, "uly", split_axis=1, concat_axis=0, tiled=True)
    local_qkv = local_qkv.reshape(local_qkv.shape[0], -1, 3, HEAD_DIM)
    local_q, local_k, local_v = (
        local_qkv[:, :, i].reshape(local_qkv.shape[0], -1) for i in range(3)
    )
    block_rows, channels = local_q.shape
    heads_here = channels // HEAD_DIM
    maxlen = block_rows // 2
    rows_q = min(512, block_rows)
    window = rows_q + 2 * maxlen
    conv_half = KERNEL // 2
    block_count = block_rows // rows_q
    score_scale = HEAD_DIM ** (-0.5)
    frame_total = lax.axis_size("blk") * block_rows
    first_frame = lax.axis_index("blk") * block_rows
    seg_ext = segment_ids(
        lengths,
        first_frame - maxlen + jnp.arange(block_rows + 2 * maxlen, dtype=jnp.int32),
        frame_total,
    )
    seg_own = seg_ext[maxlen : maxlen + block_rows]
    seg_conv = seg_ext[maxlen - conv_half : maxlen + block_rows + conv_half]
    near_pairs = extended(jnp.concatenate([local_k, local_v], axis=1), (("blk", 0),), maxlen)
    k_ext = near_pairs[:, :channels].reshape(-1, heads_here, HEAD_DIM)
    v_ext = near_pairs[:, channels:].reshape(-1, heads_here, HEAD_DIM)
    q_heads = local_q.reshape(block_rows, heads_here, HEAD_DIM)
    starts = jnp.arange(block_count, dtype=jnp.int32) * rows_q

    assert heads_here == 1
    lo_t, hi_t = tile_ranges(lengths, first_frame - maxlen, block_rows + 2 * maxlen, block_rows)
    qseg_col = seg_own[:, None].astype(jnp.int32)
    kseg_row = seg_ext[None, :].astype(jnp.int32)
    lane_gap = jnp.zeros((block_rows, HEAD_DIM), jnp.bfloat16)
    q_wide = jnp.concatenate([local_q, lane_gap], axis=1)
    att_t, lse_col = vmem_call(
        forward_kernel,
        2,
        4,
        (
            jax.ShapeDtypeStruct((HEAD_DIM, block_rows), jnp.bfloat16),
            jax.ShapeDtypeStruct((block_rows, 1), jnp.float32),
        ),
    )(lo_t, hi_t, q_wide, near_pairs, qseg_col, kseg_row)
    frame_at = first_frame + jnp.arange(block_rows, dtype=jnp.int32)
    seg_start, seg_end = segment_bounds(lengths, frame_at)
    lo_off = (seg_start - frame_at)[None, :].astype(jnp.int32)
    hi_off = (seg_end - frame_at)[None, :].astype(jnp.int32)
    weight_t = conv_weight.T
    conv_out_t, grad_conv_t = vmem_call(
        conv_forward_kernel,
        0,
        6,
        (
            jax.ShapeDtypeStruct((HEAD_DIM, block_rows), jnp.bfloat16),
            jax.ShapeDtypeStruct((HEAD_DIM, block_rows), jnp.float32),
        ),
    )(padded_rims(att_t, conv_half), weight_t, norm_gain[:, None], cotangent, lo_off, hi_off)
    grad_att_t, grad_wide, row_delta = vmem_call(
        conv_backward_kernel,
        0,
        5,
        (
            jax.ShapeDtypeStruct((HEAD_DIM, block_rows), jnp.bfloat16),
            jax.ShapeDtypeStruct((block_rows, 2 * HEAD_DIM), jnp.bfloat16),
            jax.ShapeDtypeStruct((block_rows, 1), jnp.float32),
        ),
    )(padded_rims(grad_conv_t, conv_half), weight_t, att_t, lo_off, hi_off)

    ext_rows = block_rows + 2 * maxlen
    grad_q, ext_terms = vmem_call(
        backward_kernel,
        2,
        9,
        (
            jax.ShapeDtypeStruct((block_rows, HEAD_DIM), jnp.bfloat16),
            jax.ShapeDtypeStruct((2 * HEAD_DIM, ext_rows), jnp.float32),
        ),
    )(
        lo_t,
        hi_t,
        q_wide,
        near_pairs,
        grad_wide,
        local_q.T,
        grad_att_t,
        qseg_col,
        kseg_row,
        lse_col,
        row_delta,
    )
    received = []
    for rim_part, direction in ((ext_terms[:, :maxlen], -1), (ext_terms[:, maxlen + block_rows :], 1)):
        received.append(
            passed_along(rim_part.astype(jnp.bfloat16), "blk", direction).astype(rim_part.dtype)
        )
    key_grads = ext_terms[:, maxlen : maxlen + block_rows] + jnp.concatenate(
        [received[1], received[0]], axis=1
    )
    grad_queries = grad_q.reshape(block_rows, channels)
    grad_keys = key_grads[:HEAD_DIM].astype(jnp.bfloat16)
    grad_values = key_grads[HEAD_DIM:].astype(jnp.bfloat16)
    return (conv_out_t, grad_queries.T, grad_keys, grad_values)


def solution(mesh):
    in_specs = (
        P(("blk", "uly"), None),
        P(("blk", "uly"), None),
        P(("blk", "uly"), None),
        P(),
        P(None, "uly"),
        P("uly"),
        P("uly", "blk"),
    )
    out_specs = (P("uly", "blk"), P("uly", "blk"), P("uly", "blk"), P("uly", "blk"))
    return jax.shard_map(
        on_device, mesh=mesh, in_specs=in_specs, out_specs=out_specs, check_vma=False
    )
```

```python
import jax
import jax.numpy as jnp
import functools
from jax import lax
from jax.experimental import pallas as pl
from jax.experimental.pallas import tpu as pltpu
from jax.sharding import PartitionSpec as P

KERNEL = 31
HEAD_DIM = 64


def extended(block, sides, width):
    for axis, dim in sides:
        count = lax.axis_size(axis)
        forward = [(i, i + 1) for i in range(count - 1)]
        backward = [(target, source) for source, target in forward]
        low = lax.ppermute(
            lax.slice_in_dim(block, block.shape[dim] - width, None, axis=dim), axis, forward
        )
        high = lax.ppermute(lax.slice_in_dim(block, 0, width, axis=dim), axis, backward)
        block = jnp.concatenate([low, block, high], axis=dim)
    return block


def passed_along(block, axis, distance):
    devices = range(lax.axis_size(axis))
    route = [(i - distance, i) for i in devices if i - distance in devices]
    return lax.ppermute(block, axis, route)


def segment_ids(lengths, frames, frame_total):
    starts = jnp.cumsum(lengths) - lengths
    seg_ids = jnp.sum((starts[None, :] <= frames[:, None]).astype(jnp.int32), axis=1) - 1
    inside = (frames >= 0) & (frames < frame_total)
    return jnp.where(inside, seg_ids, -1)


def rows_at(values_in, row_start, row_count):
    return lax.dynamic_slice_in_dim(values_in, row_start, row_count, 0)


def masked_scores(query_rows, key_rows, query_seg, key_seg):
    scores = HEAD_DIM ** (-0.5) * jnp.einsum(
        "rhe,she->hrs", query_rows, key_rows, preferred_element_type=jnp.float32
    )
    same_seg = (query_seg[:, None] == key_seg[None, :])[None]
    return (scores, same_seg)


def weights_of(scores, same_seg, row_top, row_total):
    return jnp.where(same_seg, jnp.exp(scores - row_top), 0.0) / row_total


TILE_Q = 512
TILE_K = 512
NT = (((1,), (1,)), ((), ()))
TN = (((0,), (0,)), ((), ()))


def forward_kernel(lo_ref, hi_ref, q_ref, kv_ref, qseg_ref, kseg_ref, o_ref, lse_ref):
    scale = HEAD_DIM ** (-0.5)

    def q_body(i, carry):
        r0 = i * TILE_Q
        q = q_ref[pl.ds(r0, TILE_Q), :] * jnp.asarray(scale, q_ref.dtype)
        qs = qseg_ref[pl.ds(r0, TILE_Q), :]

        def k_body(j, c):
            m, l, acc = c
            c0 = pl.multiple_of(j * TILE_K, TILE_K)
            kv = kv_ref[pl.ds(c0, TILE_K), :]
            ks = kseg_ref[:, pl.ds(c0, TILE_K)]
            s = lax.dot_general(q, kv, NT, preferred_element_type=jnp.float32)
            s = jnp.where(qs == ks, s, -1e30)
            m_new = jnp.maximum(m, jnp.max(s, axis=1, keepdims=True))
            alpha = jnp.exp(m - m_new)
            p = jnp.exp(s - m_new)
            l = alpha * l + jnp.sum(p, axis=1, keepdims=True)
            acc = alpha * acc + jnp.dot(
                p.astype(jnp.bfloat16), kv, preferred_element_type=jnp.float32
            )
            return (m_new, l, acc)

        init = (
            jnp.full((TILE_Q, 1), -1e30, jnp.float32),
            jnp.zeros((TILE_Q, 1), jnp.float32),
            jnp.zeros((TILE_Q, kv_ref.shape[1]), jnp.float32),
        )
        m, l, acc = lax.fori_loop(lo_ref[i], hi_ref[i], k_body, init)
        o_ref[:, pl.ds(r0, TILE_Q)] = (acc / l).T[HEAD_DIM:].astype(o_ref.dtype)
        lse_ref[pl.ds(r0, TILE_Q), :] = m + jnp.log(l)
        return carry

    for tile in range(q_ref.shape[0] // TILE_Q):
        q_body(tile, 0)


def backward_kernel(
    lo_ref, hi_ref, q_ref, kv_ref, do_ref, qt_ref, dot_ref, qseg_ref, kseg_ref, lse_ref,
    d_ref, dq_ref, dk_ref, dv_ref,
):
    scale = HEAD_DIM ** (-0.5)
    dk_ref[...] = jnp.zeros_like(dk_ref)
    dv_ref[...] = jnp.zeros_like(dv_ref)

    def q_body(i, carry):
        r0 = i * TILE_Q
        q = q_ref[pl.ds(r0, TILE_Q), :] * jnp.asarray(scale, q_ref.dtype)
        do = do_ref[pl.ds(r0, TILE_Q), :]
        qs = qseg_ref[pl.ds(r0, TILE_Q), :]
        lse = lse_ref[pl.ds(r0, TILE_Q), :]
        dlt = d_ref[pl.ds(r0, TILE_Q), :]
        q_t = qt_ref[:, pl.ds(r0, TILE_Q)]
        do_t = dot_ref[:, pl.ds(r0, TILE_Q)]

        def k_body(j, dq):
            c0 = pl.multiple_of(j * TILE_K, TILE_K)
            kv = kv_ref[pl.ds(c0, TILE_K), :]
            ks = kseg_ref[:, pl.ds(c0, TILE_K)]
            s = lax.dot_general(q, kv, NT, preferred_element_type=jnp.float32)
            p = jnp.exp(jnp.where(qs == ks, s, -1e30) - lse)
            dp = lax.dot_general(do, kv, NT, preferred_element_type=jnp.float32)
            ds = (p * (dp - dlt)).astype(jnp.bfloat16)
            dk_ref[:, pl.ds(c0, TILE_K)] += jnp.dot(q_t, ds, preferred_element_type=jnp.float32)
            dv_ref[:, pl.ds(c0, TILE_K)] += jnp.dot(
                do_t, p.astype(jnp.bfloat16), preferred_element_type=jnp.float32
            )
            return dq + jnp.dot(ds, kv, preferred_element_type=jnp.float32)

        dq = lax.fori_loop(
            lo_ref[i], hi_ref[i], k_body, jnp.zeros((TILE_Q, kv_ref.shape[1]), jnp.float32)
        )
        dq_ref[pl.ds(r0, TILE_Q), :] = (scale * dq[:, :HEAD_DIM]).astype(dq_ref.dtype)
        return carry

    for tile in range(q_ref.shape[0] // TILE_Q):
        q_body(tile, 0)
    dk_ref[...] = scale * dk_ref[...]


def vmem_call(kernel, n_smem, n_vmem, out_shape):
    return pl.pallas_call(
        kernel,
        out_shape=out_shape,
        in_specs=[pl.BlockSpec(memory_space=pltpu.SMEM)] * n_smem
        + [pl.BlockSpec(memory_space=pltpu.VMEM)] * n_vmem,
        out_specs=[pl.BlockSpec(memory_space=pltpu.VMEM)] * len(out_shape),
    )


def segment_bounds(lengths, frames):
    ends = jnp.cumsum(lengths)
    starts = ends - lengths
    seg_start = jnp.max(jnp.where(starts[None, :] <= frames[:, None], starts[None, :], 0), axis=1)
    big = jnp.iinfo(jnp.int32).max
    seg_end = jnp.min(jnp.where(ends[None, :] > frames[:, None], ends[None, :], big), axis=1)
    return (seg_start, jnp.minimum(seg_end, ends[-1]))


def tile_ranges(lengths, base, ext_rows, block_rows):
    frames = base + (ext_rows - block_rows) // 2 + jnp.arange(block_rows, dtype=jnp.int32)
    seg_start, seg_end = segment_bounds(lengths, frames)
    lo = (seg_start[::TILE_Q] - base) // TILE_K
    hi = (seg_end[TILE_Q - 1 :: TILE_Q] - base + TILE_K - 1) // TILE_K
    lo = jnp.clip(lo, 0, ext_rows // TILE_K).astype(jnp.int32)
    hi = jnp.clip(hi, lo, ext_rows // TILE_K).astype(jnp.int32)
    return (lo, hi)


CONV_PAD = 128
CONV_CHUNK = 2048


def conv_chunk(x_ref, wt_ref, lo, hi, c0, sign):
    window = x_ref[:, pl.ds(c0, CONV_CHUNK + 2 * CONV_PAD)]
    width = window.shape[1]
    total = jnp.zeros((window.shape[0], CONV_CHUNK), jnp.float32)
    for tap in range(KERNEL):
        d = sign * (tap - KERNEL // 2)
        shifted = pltpu.roll(window, (width - d) % width, 1) if d else window
        keep = (lo <= d) & (d < hi)
        total = total + wt_ref[:, tap : tap + 1] * jnp.where(
            keep, shifted[:, CONV_PAD : CONV_PAD + CONV_CHUNK], 0.0
        )
    return total


def conv_forward_kernel(x_ref, wt_ref, gain_ref, cot_ref, lo_ref, hi_ref, out_ref, gc_ref):
    gain = gain_ref[...]

    def body(c, carry):
        c0 = pl.multiple_of(c * CONV_CHUNK, CONV_CHUNK)
        cols = pl.ds(c0, CONV_CHUNK)
        conv_sum = conv_chunk(x_ref, wt_ref, lo_ref[:, cols], hi_ref[:, cols], c0, 1)
        spread = jnp.sqrt(jnp.mean(conv_sum * conv_sum, axis=0, keepdims=True) + 1e-05)
        normed = conv_sum / spread
        pre_act = normed * gain
        gate = 1.0 / (1.0 + jnp.exp(-pre_act))
        out_ref[:, cols] = (pre_act * gate).astype(out_ref.dtype)
        grad_pre = cot_ref[:, cols].astype(jnp.float32) * gate * (1.0 + pre_act * (1.0 - gate))
        weighted = grad_pre * gain
        gc_ref[:, cols] = (
            weighted - normed * jnp.mean(weighted * normed, axis=0, keepdims=True)
        ) / spread
        return carry

    lax.fori_loop(0, out_ref.shape[1] // CONV_CHUNK, body, 0)


def conv_backward_kernel(y_ref, wt_ref, att_ref, lo_ref, hi_ref, ga_ref, dop_ref, delta_ref):
    def body(c, carry):
        c0 = pl.multiple_of(c * CONV_CHUNK, CONV_CHUNK)
        cols = pl.ds(c0, CONV_CHUNK)
        grad_sum = conv_chunk(y_ref, wt_ref, lo_ref[:, cols], hi_ref[:, cols], c0, -1)
        grad_att = grad_sum.astype(ga_ref.dtype)
        ga_ref[:, cols] = grad_att
        grad_f32 = grad_att.astype(jnp.float32)
        delta = jnp.sum(grad_f32 * att_ref[:, cols].astype(jnp.float32), axis=0, keepdims=True)
        rows = pl.ds(c0, CONV_CHUNK)
        delta_ref[rows, :] = jnp.broadcast_to(delta, (8, CONV_CHUNK)).T[:, :1]
        wide = jnp.concatenate([jnp.zeros_like(grad_f32), grad_f32], axis=0)
        dop_ref[rows, :] = wide.T.astype(dop_ref.dtype)
        return carry

    lax.fori_loop(0, ga_ref.shape[1] // CONV_CHUNK, body, 0)


def padded_rims(block, half):
    count = lax.axis_size("blk")
    forward = [(i, i + 1) for i in range(count - 1)]
    backward = [(target, source) for source, target in forward]
    low = lax.ppermute(block[:, block.shape[1] - half :], "blk", forward)
    high = lax.ppermute(block[:, :half], "blk", backward)
    gap = jnp.zeros((block.shape[0], CONV_PAD - half), jnp.float32)
    return jnp.concatenate(
        [gap, low.astype(jnp.float32), block.astype(jnp.float32), high.astype(jnp.float32), gap],
        axis=1,
    )


def on_device(queries, keys, values, lengths, conv_weight, norm_gain, cotangent):
    rows_in, width = queries.shape
    heads_total = width // HEAD_DIM
    stacked = jnp.stack(
        [a.reshape(rows_in, heads_total, HEAD_DIM) for a in (queries, keys, values)], axis=2
    ).reshape(rows_in, heads_total * 3 * HEAD_DIM)
    local_qkv = lax.all_to_all(stacked, "uly", split_axis=1, concat_axis=0, tiled=True)
    local_qkv = local_qkv.reshape(local_qkv.shape[0], -1, 3, HEAD_DIM)
    local_q, local_k, local_v = (
        local_qkv[:, :, i].reshape(local_qkv.shape[0], -1) for i in range(3)
    )
    block_rows, channels = local_q.shape
    heads_here = channels // HEAD_DIM
    maxlen = block_rows // 2
    rows_q = min(512, block_rows)
    window = rows_q + 2 * maxlen
    conv_half = KERNEL // 2
    block_count = block_rows // rows_q
    score_scale = HEAD_DIM ** (-0.5)
    frame_total = lax.axis_size("blk") * block_rows
    first_frame = lax.axis_index("blk") * block_rows
    seg_ext = segment_ids(
        lengths,
        first_frame - maxlen + jnp.arange(block_rows + 2 * maxlen, dtype=jnp.int32),
        frame_total,
    )
    seg_own = seg_ext[maxlen : maxlen + block_rows]
    seg_conv = seg_ext[maxlen - conv_half : maxlen + block_rows + conv_half]
    near_pairs = extended(jnp.concatenate([local_k, local_v], axis=1), (("blk", 0),), maxlen)
    k_ext = near_pairs[:, :channels].reshape(-1, heads_here, HEAD_DIM)
    v_ext = near_pairs[:, channels:].reshape(-1, heads_here, HEAD_DIM)
    q_heads = local_q.reshape(block_rows, heads_here, HEAD_DIM)
    starts = jnp.arange(block_count, dtype=jnp.int32) * rows_q

    assert heads_here == 1
    lo_t, hi_t = tile_ranges(lengths, first_frame - maxlen, block_rows + 2 * maxlen, block_rows)
    qseg_col = seg_own[:, None].astype(jnp.int32)
    kseg_row = seg_ext[None, :].astype(jnp.int32)
    lane_gap = jnp.zeros((block_rows, HEAD_DIM), jnp.bfloat16)
    q_wide = jnp.concatenate([local_q, lane_gap], axis=1)
    att_t, lse_col = vmem_call(
        forward_kernel,
        2,
        4,
        (
            jax.ShapeDtypeStruct((HEAD_DIM, block_rows), jnp.bfloat16),
            jax.ShapeDtypeStruct((block_rows, 1), jnp.float32),
        ),
    )(lo_t, hi_t, q_wide, near_pairs, qseg_col, kseg_row)
    frame_at = first_frame + jnp.arange(block_rows, dtype=jnp.int32)
    seg_start, seg_end = segment_bounds(lengths, frame_at)
    lo_off = (seg_start - frame_at)[None, :].astype(jnp.int32)
    hi_off = (seg_end - frame_at)[None, :].astype(jnp.int32)
    weight_t = conv_weight.T
    conv_out_t, grad_conv_t = vmem_call(
        conv_forward_kernel,
        0,
        6,
        (
            jax.ShapeDtypeStruct((HEAD_DIM, block_rows), jnp.bfloat16),
            jax.ShapeDtypeStruct((HEAD_DIM, block_rows), jnp.float32),
        ),
    )(padded_rims(att_t, conv_half), weight_t, norm_gain[:, None], cotangent, lo_off, hi_off)
    grad_att_t, grad_wide, row_delta = vmem_call(
        conv_backward_kernel,
        0,
        5,
        (
            jax.ShapeDtypeStruct((HEAD_DIM, block_rows), jnp.bfloat16),
            jax.ShapeDtypeStruct((block_rows, 2 * HEAD_DIM), jnp.bfloat16),
            jax.ShapeDtypeStruct((block_rows, 1), jnp.float32),
        ),
    )(padded_rims(grad_conv_t, conv_half), weight_t, att_t, lo_off, hi_off)

    ext_rows = block_rows + 2 * maxlen
    grad_q, dk_t, dv_t = vmem_call(
        backward_kernel,
        2,
        9,
        (
            jax.ShapeDtypeStruct((block_rows, HEAD_DIM), jnp.bfloat16),
            jax.ShapeDtypeStruct((HEAD_DIM, ext_rows), jnp.float32),
            jax.ShapeDtypeStruct((HEAD_DIM, ext_rows), jnp.float32),
        ),
    )(
        lo_t,
        hi_t,
        q_wide,
        near_pairs,
        grad_wide,
        local_q.T,
        grad_att_t,
        qseg_col,
        kseg_row,
        lse_col,
        row_delta,
    )
    ext_terms = jnp.concatenate([dk_t, dv_t], axis=0)
    received = []
    for rim_part, direction in ((ext_terms[:, :maxlen], -1), (ext_terms[:, maxlen + block_rows :], 1)):
        received.append(
            passed_along(rim_part.astype(jnp.bfloat16), "blk", direction).astype(rim_part.dtype)
        )
    key_grads = ext_terms[:, maxlen : maxlen + block_rows] + jnp.concatenate(
        [received[1], received[0]], axis=1
    )
    grad_queries = grad_q.reshape(block_rows, channels)
    grad_keys = key_grads[:HEAD_DIM].astype(jnp.bfloat16)
    grad_values = key_grads[HEAD_DIM:].astype(jnp.bfloat16)
    return (conv_out_t, grad_queries.T, grad_keys, grad_values)


def solution(mesh):
    in_specs = (
        P(("blk", "uly"), None),
        P(("blk", "uly"), None),
        P(("blk", "uly"), None),
        P(),
        P(None, "uly"),
        P("uly"),
        P("uly", "blk"),
    )
    out_specs = (P("uly", "blk"), P("uly", "blk"), P("uly", "blk"), P("uly", "blk"))
    return jax.shard_map(
        on_device, mesh=mesh, in_specs=in_specs, out_specs=out_specs, check_vma=False
    )
```

```python
import jax
import jax.numpy as jnp
import functools
from jax import lax
from jax.experimental import pallas as pl
from jax.experimental.pallas import tpu as pltpu
from jax.sharding import PartitionSpec as P

KERNEL = 31
HEAD_DIM = 64


def extended(block, sides, width):
    for axis, dim in sides:
        count = lax.axis_size(axis)
        forward = [(i, i + 1) for i in range(count - 1)]
        backward = [(target, source) for source, target in forward]
        low = lax.ppermute(
            lax.slice_in_dim(block, block.shape[dim] - width, None, axis=dim), axis, forward
        )
        high = lax.ppermute(lax.slice_in_dim(block, 0, width, axis=dim), axis, backward)
        block = jnp.concatenate([low, block, high], axis=dim)
    return block


def passed_along(block, axis, distance):
    devices = range(lax.axis_size(axis))
    route = [(i - distance, i) for i in devices if i - distance in devices]
    return lax.ppermute(block, axis, route)


def segment_ids(lengths, frames, frame_total):
    starts = jnp.cumsum(lengths) - lengths
    seg_ids = jnp.sum((starts[None, :] <= frames[:, None]).astype(jnp.int32), axis=1) - 1
    inside = (frames >= 0) & (frames < frame_total)
    return jnp.where(inside, seg_ids, -1)


def rows_at(values_in, row_start, row_count):
    return lax.dynamic_slice_in_dim(values_in, row_start, row_count, 0)


def masked_scores(query_rows, key_rows, query_seg, key_seg):
    scores = HEAD_DIM ** (-0.5) * jnp.einsum(
        "rhe,she->hrs", query_rows, key_rows, preferred_element_type=jnp.float32
    )
    same_seg = (query_seg[:, None] == key_seg[None, :])[None]
    return (scores, same_seg)


def weights_of(scores, same_seg, row_top, row_total):
    return jnp.where(same_seg, jnp.exp(scores - row_top), 0.0) / row_total


TILE_Q = 512
TILE_K = 512
NT = (((1,), (1,)), ((), ()))
TN = (((0,), (0,)), ((), ()))


def forward_kernel(lo_ref, hi_ref, q_ref, kv_ref, kseg_ref, o_ref, lse_ref):
    scale = HEAD_DIM ** (-0.5)

    def q_body(i, carry):
        r0 = pl.multiple_of(i * TILE_Q, TILE_Q)
        q = q_ref[pl.ds(r0, TILE_Q), :] * jnp.asarray(scale, q_ref.dtype)
        q_off = (kseg_ref.shape[1] - q_ref.shape[0]) // 2
        qs = jnp.broadcast_to(kseg_ref[:, pl.ds(q_off + r0, TILE_Q)], (8, TILE_Q)).T[:, :1]

        def k_body(j, c):
            m, l, acc = c
            c0 = pl.multiple_of(j * TILE_K, TILE_K)
            kv = kv_ref[pl.ds(c0, TILE_K), :]
            ks = kseg_ref[:, pl.ds(c0, TILE_K)]
            s = lax.dot_general(q, kv, NT, preferred_element_type=jnp.float32)
            s = jnp.where(qs == ks, s, -1e30)
            m_new = jnp.maximum(m, jnp.max(s, axis=1, keepdims=True))
            alpha = jnp.exp(m - m_new)
            p = jnp.exp(s - m_new)
            l = alpha * l + jnp.sum(p, axis=1, keepdims=True)
            acc = alpha * acc + jnp.dot(
                p.astype(jnp.bfloat16), kv, preferred_element_type=jnp.float32
            )
            return (m_new, l, acc)

        init = (
            jnp.full((TILE_Q, 1), -1e30, jnp.float32),
            jnp.zeros((TILE_Q, 1), jnp.float32),
            jnp.zeros((TILE_Q, kv_ref.shape[1]), jnp.float32),
        )
        m, l, acc = lax.fori_loop(lo_ref[i], hi_ref[i], k_body, init)
        o_ref[:, pl.ds(r0, TILE_Q)] = (acc / l).T[HEAD_DIM:].astype(o_ref.dtype)
        lse_ref[pl.ds(r0, TILE_Q), :] = m + jnp.log(l)
        return carry

    lax.fori_loop(0, q_ref.shape[0] // TILE_Q, q_body, 0)


def backward_kernel(
    lo_ref, hi_ref, q_ref, kv_ref, do_ref, qt_ref, dot_ref, kseg_ref, lse_ref,
    d_ref, dq_ref, dk_ref, dv_ref,
):
    scale = HEAD_DIM ** (-0.5)
    dk_ref[...] = jnp.zeros_like(dk_ref)
    dv_ref[...] = jnp.zeros_like(dv_ref)

    def q_body(i, carry):
        r0 = pl.multiple_of(i * TILE_Q, TILE_Q)
        q = q_ref[pl.ds(r0, TILE_Q), :] * jnp.asarray(scale, q_ref.dtype)
        do = do_ref[pl.ds(r0, TILE_Q), :]
        q_off = (kseg_ref.shape[1] - q_ref.shape[0]) // 2
        qs = jnp.broadcast_to(kseg_ref[:, pl.ds(q_off + r0, TILE_Q)], (8, TILE_Q)).T[:, :1]
        lse = lse_ref[pl.ds(r0, TILE_Q), :]
        dlt = d_ref[pl.ds(r0, TILE_Q), :]
        q_t = qt_ref[:, pl.ds(r0, TILE_Q)]
        do_t = dot_ref[:, pl.ds(r0, TILE_Q)]

        def k_body(j, dq):
            c0 = pl.multiple_of(j * TILE_K, TILE_K)
            kv = kv_ref[pl.ds(c0, TILE_K), :]
            ks = kseg_ref[:, pl.ds(c0, TILE_K)]
            s = lax.dot_general(q, kv, NT, preferred_element_type=jnp.float32)
            p = jnp.exp(jnp.where(qs == ks, s, -1e30) - lse)
            dp = lax.dot_general(do, kv, NT, preferred_element_type=jnp.float32)
            ds = (p * (dp - dlt)).astype(jnp.bfloat16)
            dk_ref[:, pl.ds(c0, TILE_K)] += jnp.dot(q_t, ds, preferred_element_type=jnp.float32)
            dv_ref[:, pl.ds(c0, TILE_K)] += jnp.dot(
                do_t, p.astype(jnp.bfloat16), preferred_element_type=jnp.float32
            )
            return dq + jnp.dot(ds, kv, preferred_element_type=jnp.float32)

        dq = lax.fori_loop(
            lo_ref[i], hi_ref[i], k_body, jnp.zeros((TILE_Q, kv_ref.shape[1]), jnp.float32)
        )
        dq_ref[pl.ds(r0, TILE_Q), :] = (scale * dq[:, :HEAD_DIM]).astype(dq_ref.dtype)
        return carry

    lax.fori_loop(0, q_ref.shape[0] // TILE_Q, q_body, 0)
    dk_ref[...] = scale * dk_ref[...]


def vmem_call(kernel, n_smem, n_vmem, out_shape):
    return pl.pallas_call(
        kernel,
        out_shape=out_shape,
        in_specs=[pl.BlockSpec(memory_space=pltpu.SMEM)] * n_smem
        + [pl.BlockSpec(memory_space=pltpu.VMEM)] * n_vmem,
        out_specs=[pl.BlockSpec(memory_space=pltpu.VMEM)] * len(out_shape),
    )


def segment_bounds(lengths, frames):
    ends = jnp.cumsum(lengths)
    starts = ends - lengths
    seg_start = jnp.max(jnp.where(starts[None, :] <= frames[:, None], starts[None, :], 0), axis=1)
    big = jnp.iinfo(jnp.int32).max
    seg_end = jnp.min(jnp.where(ends[None, :] > frames[:, None], ends[None, :], big), axis=1)
    return (seg_start, jnp.minimum(seg_end, ends[-1]))


def tile_ranges(lengths, base, ext_rows, block_rows):
    frames = base + (ext_rows - block_rows) // 2 + jnp.arange(block_rows, dtype=jnp.int32)
    seg_start, seg_end = segment_bounds(lengths, frames)
    lo = (seg_start[::TILE_Q] - base) // TILE_K
    hi = (seg_end[TILE_Q - 1 :: TILE_Q] - base + TILE_K - 1) // TILE_K
    lo = jnp.clip(lo, 0, ext_rows // TILE_K).astype(jnp.int32)
    hi = jnp.clip(hi, lo, ext_rows // TILE_K).astype(jnp.int32)
    return (lo, hi)


CONV_PAD = 128
CONV_CHUNK = 2048


def conv_chunk(x_ref, wt_ref, lo, hi, c0, sign):
    window = x_ref[:, pl.ds(c0, CONV_CHUNK + 2 * CONV_PAD)]
    width = window.shape[1]
    total = jnp.zeros((window.shape[0], CONV_CHUNK), jnp.float32)
    for tap in range(KERNEL):
        d = sign * (tap - KERNEL // 2)
        shifted = pltpu.roll(window, (width - d) % width, 1) if d else window
        keep = (lo <= d) & (d < hi)
        total = total + wt_ref[:, tap : tap + 1] * jnp.where(
            keep, shifted[:, CONV_PAD : CONV_PAD + CONV_CHUNK], 0.0
        )
    return total


def conv_forward_kernel(x_ref, wt_ref, gain_ref, cot_ref, lo_ref, hi_ref, out_ref, gc_ref):
    gain = gain_ref[...]

    def body(c, carry):
        c0 = pl.multiple_of(c * CONV_CHUNK, CONV_CHUNK)
        cols = pl.ds(c0, CONV_CHUNK)
        conv_sum = conv_chunk(x_ref, wt_ref, lo_ref[:, cols], hi_ref[:, cols], c0, 1)
        spread = jnp.sqrt(jnp.mean(conv_sum * conv_sum, axis=0, keepdims=True) + 1e-05)
        normed = conv_sum / spread
        pre_act = normed * gain
        gate = 1.0 / (1.0 + jnp.exp(-pre_act))
        out_ref[:, cols] = (pre_act * gate).astype(out_ref.dtype)
        grad_pre = cot_ref[:, cols].astype(jnp.float32) * gate * (1.0 + pre_act * (1.0 - gate))
        weighted = grad_pre * gain
        gc_ref[:, cols] = (
            weighted - normed * jnp.mean(weighted * normed, axis=0, keepdims=True)
        ) / spread
        return carry

    lax.fori_loop(0, out_ref.shape[1] // CONV_CHUNK, body, 0)


def conv_backward_kernel(y_ref, wt_ref, att_ref, lo_ref, hi_ref, ga_ref, dop_ref, delta_ref):
    def body(c, carry):
        c0 = pl.multiple_of(c * CONV_CHUNK, CONV_CHUNK)
        cols = pl.ds(c0, CONV_CHUNK)
        grad_sum = conv_chunk(y_ref, wt_ref, lo_ref[:, cols], hi_ref[:, cols], c0, -1)
        grad_att = grad_sum.astype(ga_ref.dtype)
        ga_ref[:, cols] = grad_att
        grad_f32 = grad_att.astype(jnp.float32)
        delta = jnp.sum(grad_f32 * att_ref[:, cols].astype(jnp.float32), axis=0, keepdims=True)
        rows = pl.ds(c0, CONV_CHUNK)
        delta_ref[rows, :] = jnp.broadcast_to(delta, (8, CONV_CHUNK)).T[:, :1]
        wide = jnp.concatenate([jnp.zeros_like(grad_f32), grad_f32], axis=0)
        dop_ref[rows, :] = wide.T.astype(dop_ref.dtype)
        return carry

    lax.fori_loop(0, ga_ref.shape[1] // CONV_CHUNK, body, 0)


def padded_rims(block, half):
    count = lax.axis_size("blk")
    forward = [(i, i + 1) for i in range(count - 1)]
    backward = [(target, source) for source, target in forward]
    low = lax.ppermute(block[:, block.shape[1] - half :], "blk", forward)
    high = lax.ppermute(block[:, :half], "blk", backward)
    gap = jnp.zeros((block.shape[0], CONV_PAD - half), jnp.float32)
    return jnp.concatenate(
        [gap, low.astype(jnp.float32), block.astype(jnp.float32), high.astype(jnp.float32), gap],
        axis=1,
    )


def on_device(queries, keys, values, lengths, conv_weight, norm_gain, cotangent):
    rows_in, width = queries.shape
    heads_total = width // HEAD_DIM
    stacked = jnp.stack(
        [a.reshape(rows_in, heads_total, HEAD_DIM) for a in (queries, keys, values)], axis=2
    ).reshape(rows_in, heads_total * 3 * HEAD_DIM)
    local_qkv = lax.all_to_all(stacked, "uly", split_axis=1, concat_axis=0, tiled=True)
    local_qkv = local_qkv.reshape(local_qkv.shape[0], -1, 3, HEAD_DIM)
    local_q, local_k, local_v = (
        local_qkv[:, :, i].reshape(local_qkv.shape[0], -1) for i in range(3)
    )
    block_rows, channels = local_q.shape
    heads_here = channels // HEAD_DIM
    maxlen = block_rows // 2
    rows_q = min(512, block_rows)
    window = rows_q + 2 * maxlen
    conv_half = KERNEL // 2
    block_count = block_rows // rows_q
    score_scale = HEAD_DIM ** (-0.5)
    frame_total = lax.axis_size("blk") * block_rows
    first_frame = lax.axis_index("blk") * block_rows
    seg_ext = segment_ids(
        lengths,
        first_frame - maxlen + jnp.arange(block_rows + 2 * maxlen, dtype=jnp.int32),
        frame_total,
    )
    seg_own = seg_ext[maxlen : maxlen + block_rows]
    seg_conv = seg_ext[maxlen - conv_half : maxlen + block_rows + conv_half]
    near_pairs = extended(jnp.concatenate([local_k, local_v], axis=1), (("blk", 0),), maxlen)
    k_ext = near_pairs[:, :channels].reshape(-1, heads_here, HEAD_DIM)
    v_ext = near_pairs[:, channels:].reshape(-1, heads_here, HEAD_DIM)
    q_heads = local_q.reshape(block_rows, heads_here, HEAD_DIM)
    starts = jnp.arange(block_count, dtype=jnp.int32) * rows_q

    assert heads_here == 1
    lo_t, hi_t = tile_ranges(lengths, first_frame - maxlen, block_rows + 2 * maxlen, block_rows)
    qseg_col = seg_own[:, None].astype(jnp.int32)
    kseg_row = seg_ext[None, :].astype(jnp.int32)
    lane_gap = jnp.zeros((block_rows, HEAD_DIM), jnp.bfloat16)
    q_wide = jnp.concatenate([local_q, lane_gap], axis=1)
    att_t, lse_col = vmem_call(
        forward_kernel,
        2,
        3,
        (
            jax.ShapeDtypeStruct((HEAD_DIM, block_rows), jnp.bfloat16),
            jax.ShapeDtypeStruct((block_rows, 1), jnp.float32),
        ),
    )(lo_t, hi_t, q_wide, near_pairs, kseg_row)
    frame_at = first_frame + jnp.arange(block_rows, dtype=jnp.int32)
    seg_start, seg_end = segment_bounds(lengths, frame_at)
    lo_off = (seg_start - frame_at)[None, :].astype(jnp.int32)
    hi_off = (seg_end - frame_at)[None, :].astype(jnp.int32)
    weight_t = conv_weight.T
    conv_out_t, grad_conv_t = vmem_call(
        conv_forward_kernel,
        0,
        6,
        (
            jax.ShapeDtypeStruct((HEAD_DIM, block_rows), jnp.bfloat16),
            jax.ShapeDtypeStruct((HEAD_DIM, block_rows), jnp.float32),
        ),
    )(padded_rims(att_t, conv_half), weight_t, norm_gain[:, None], cotangent, lo_off, hi_off)
    grad_att_t, grad_wide, row_delta = vmem_call(
        conv_backward_kernel,
        0,
        5,
        (
            jax.ShapeDtypeStruct((HEAD_DIM, block_rows), jnp.bfloat16),
            jax.ShapeDtypeStruct((block_rows, 2 * HEAD_DIM), jnp.bfloat16),
            jax.ShapeDtypeStruct((block_rows, 1), jnp.float32),
        ),
    )(padded_rims(grad_conv_t, conv_half), weight_t, att_t, lo_off, hi_off)

    ext_rows = block_rows + 2 * maxlen
    grad_q, dk_t, dv_t = vmem_call(
        backward_kernel,
        2,
        8,
        (
            jax.ShapeDtypeStruct((block_rows, HEAD_DIM), jnp.bfloat16),
            jax.ShapeDtypeStruct((HEAD_DIM, ext_rows), jnp.float32),
            jax.ShapeDtypeStruct((HEAD_DIM, ext_rows), jnp.float32),
        ),
    )(
        lo_t,
        hi_t,
        q_wide,
        near_pairs,
        grad_wide,
        local_q.T,
        grad_att_t,
        kseg_row,
        lse_col,
        row_delta,
    )
    ext_terms = jnp.concatenate([dk_t, dv_t], axis=0)
    received = []
    for rim_part, direction in ((ext_terms[:, :maxlen], -1), (ext_terms[:, maxlen + block_rows :], 1)):
        received.append(
            passed_along(rim_part.astype(jnp.bfloat16), "blk", direction).astype(rim_part.dtype)
        )
    key_grads = ext_terms[:, maxlen : maxlen + block_rows] + jnp.concatenate(
        [received[1], received[0]], axis=1
    )
    grad_queries = grad_q.reshape(block_rows, channels)
    grad_keys = key_grads[:HEAD_DIM].astype(jnp.bfloat16)
    grad_values = key_grads[HEAD_DIM:].astype(jnp.bfloat16)
    return (conv_out_t, grad_queries.T, grad_keys, grad_values)


def solution(mesh):
    in_specs = (
        P(("blk", "uly"), None),
        P(("blk", "uly"), None),
        P(("blk", "uly"), None),
        P(),
        P(None, "uly"),
        P("uly"),
        P("uly", "blk"),
    )
    out_specs = (P("uly", "blk"), P("uly", "blk"), P("uly", "blk"), P("uly", "blk"))
    return jax.shard_map(
        on_device, mesh=mesh, in_specs=in_specs, out_specs=out_specs, check_vma=False
    )
```
